256 devices in a mesh: gx: 32 (over x, z_hi, core), gy: 8 (over z_lo, y).
Axes of the slice: x: 4, y: 4, z: 8 (z_hi: 4, z_lo: 2; z = z_hi * 2 + z_lo), core: 2. Of those that a mesh axis runs over, the one named last changes fastest.
Arguments:
- populations: float32 [19, 128, 256, 128], P(None, 'gx', 'gy'), may hold values from 0 to 1, as said below
- labels: int32 [128, 256, 128], P('gx', 'gy'), may hold values from 0 to 3
- solid_mask: int32 [128, 256, 128], P('gx', 'gy'), may hold values 0 or 1
Outputs:
- new_populations: float32 [19, 128, 256, 128], P(None, 'gx', 'gy')
- phase: float32 [128, 256, 128], P('gx', 'gy')
The draws below stay inside these ranges and needn't reach their ends.
Inputs may be any that keep to these rules, and one draw needn't show every extreme that they name: `populations`: every entry is positive.
All inputs are finite; a program needn't handle non-finite values. No bound on the sum of `solid_mask` on one device may be relied on, other than what follows from the above.
Results may differ from the reference program's by a relative error of at most 0.00011.
Values sent between devices are 32-bit elements; how exact they have to be, the bound alone decides.
No kernel may reach another device: no remote copies, remote signals or barrier semaphores. Data moves between devices by JAX's collectives and lax.ppermute only.
A program may use at most 64 MiB of HBM per device.

```python
import jax
import jax.numpy as jnp
import numpy as np
from jax import lax

NZ = 128
STEPS = 2
NX = 128
NY = 256


WEIGHTS_TABLE = [1.0 / 3.0] + [1.0 / 18.0] * 6 + [1.0 / 36.0] * 12


def draw_populations(key, part):
    lattice_weights = jnp.asarray(WEIGHTS_TABLE, jnp.float32).reshape(19, 1, 1, 1)
    noise = jax.random.uniform(key, (19, NX, NY, NZ), jnp.float32, -1.0, 1.0)
    result = lattice_weights * (1.0 + 0.5 * noise)
    return result


def place_ends(drawn, own_key, smallest, top_value):
    extent = drawn.shape
    spot = [jax.random.randint(jax.random.fold_in(own_key, axis), (), 0, extent[axis]) for axis in range(len(extent))]
    drawn = drawn.at[tuple(spot)].set(smallest)
    longest = extent.index(max(extent))
    spot[longest] = (spot[longest] + 1) % extent[longest]
    return drawn.at[tuple(spot)].set(top_value)


def setup_inputs(seed: int = 0) -> dict:
    seeds = jax.random.split(jax.random.key(seed), 4)
    return {
        "populations": draw_populations(jax.random.fold_in(seeds[3], 71), 0),
        "labels": place_ends(jax.random.randint(seeds[1], (NX, NY, NZ), 0, 4), jax.random.fold_in(seeds[1], 1), 0, 3).astype(jnp.int32),
        "solid_mask": place_ends((jax.random.randint(seeds[2], (NX, NY, NZ), 0, 8) < 1).astype(jnp.int32), jax.random.fold_in(seeds[2], 1), 0, 1),
    }


VELOCITY_SET = [(0, 0, 0), (1, 0, 0), (-1, 0, 0), (0, 1, 0), (0, -1, 0), (0, 0, 1), (0, 0, -1), (1, 1, 0), (-1, -1, 0), (1, -1, 0), (-1, 1, 0), (1, 0, 1), (-1, 0, -1), (1, 0, -1), (-1, 0, 1), (0, 1, 1), (0, -1, -1), (0, 1, -1), (0, -1, 1)]
OPPOSITE = [0, 2, 1, 4, 3, 6, 5, 8, 7, 10, 9, 12, 11, 14, 13, 16, 15, 18, 17]
WEIGHTS = [1.0 / 3.0] + [1.0 / 18.0] * 6 + [1.0 / 36.0] * 12
BALANCE = [-1.0 / 3.0] + [1.0 / 18.0] * 6 + [1.0 / 36.0] * 12
RELAX_RATES = [0.0, 0.0, 0.0, 0.0, 1.0, 1.25, 1.25, 1.25, 1.25, 1.25, 1.2, 1.2, 1.2, 1.2, 1.2, 1.2, 1.4, 1.4, 1.4]
SURFACE_COEF = 0.2
SEGREGATION_RATE = 0.7
GRAD_FLOOR = 0.1

def moment_values(ex, ey, ez):
    return [1.0, ex, ey, ez, ex * ex + ey * ey + ez * ez, ex * ex - ey * ey, ey * ey - ez * ez, ex * ey, ex * ez, ey * ez, ex * ex * ey, ex * ex * ez, ey * ey * ex, ey * ey * ez, ez * ez * ex, ez * ez * ey, ex * ex * ey * ey, ex * ex * ez * ez, ey * ey * ez * ez]

def build_collision():
    count = 19
    columns = [moment_values(float(v[0]), float(v[1]), float(v[2])) for v in VELOCITY_SET]
    moments = [[columns[col_index][row_index] for col_index in range(count)] for row_index in range(count)]
    augmented = [moments[row_index][:] + [1.0 if row_index == col_index else 0.0 for col_index in range(count)] for row_index in range(count)]
    for column in range(count):
        pivot_row = column
        for row_index in range(column + 1, count):
            if abs(augmented[row_index][column]) > abs(augmented[pivot_row][column]):
                pivot_row = row_index
        augmented[column], augmented[pivot_row] = (augmented[pivot_row], augmented[column])
        leading = augmented[column][column]
        augmented[column] = [entry / leading for entry in augmented[column]]
        for row_index in range(count):
            if row_index != column:
                factor = augmented[row_index][column]
                if factor != 0.0:
                    augmented[row_index] = [entry - factor * pivot_entry for entry, pivot_entry in zip(augmented[row_index], augmented[column])]
    inverse = [augmented[row_index][count:] for row_index in range(count)]
    result = [[sum((inverse[row_index][inner] * RELAX_RATES[inner] * moments[inner][col_index] for inner in range(count))) for col_index in range(count)] for row_index in range(count)]
    return np.array(result, dtype=np.float32)

def velocity_table():
    return np.array(VELOCITY_SET, dtype=np.float32).T.copy()

def gradient_of(padded, size_x, size_y):
    shape = (size_x, size_y, padded.shape[2])
    grad_x = jnp.zeros(shape, jnp.float32)
    grad_y = jnp.zeros(shape, jnp.float32)
    grad_z = jnp.zeros(shape, jnp.float32)
    for direction in range(1, 19):
        ex, ey, ez = VELOCITY_SET[direction]
        part = padded[1 + ex:1 + ex + size_x, 1 + ey:1 + ey + size_y]
        value = jnp.roll(part, -ez, axis=2)
        factor = 3.0 * WEIGHTS[direction]
        if ex != 0:
            grad_x = grad_x + factor * ex * value
        if ey != 0:
            grad_y = grad_y + factor * ey * value
        if ez != 0:
            grad_z = grad_z + factor * ez * value
    return jnp.stack([grad_x, grad_y, grad_z])

def collide(pops, phase, grad, wall_nodes):
    tail = (1,) * (pops.ndim - 1)
    lattice_weights = jnp.asarray(WEIGHTS, jnp.float32).reshape((19,) + tail)
    balance = jnp.asarray(BALANCE, jnp.float32).reshape((19,) + tail)
    table = jnp.asarray(velocity_table(), jnp.float32)
    collision_k = jnp.asarray(build_collision(), jnp.float32)
    highest = lax.Precision.HIGHEST
    fluid_density = lax.optimization_barrier(jnp.sum(pops, axis=0))
    momentum = jnp.einsum('ci,i...->c...', table, pops, precision=highest)
    velocity = momentum / fluid_density
    projected = jnp.einsum('ci,c...->i...', table, velocity, precision=highest)
    speed_sq = lax.optimization_barrier(jnp.sum(velocity * velocity, axis=0))
    equilibrium = lattice_weights * fluid_density * (1.0 + 3.0 * projected + 4.5 * projected * projected - 1.5 * speed_sq)
    relaxed = pops - jnp.einsum('ij,j...->i...', collision_k, pops - equilibrium, precision=highest)
    grad_sq = lax.optimization_barrier(jnp.sum(grad * grad, axis=0))
    clipped_values = jnp.maximum(jnp.sqrt(grad_sq), GRAD_FLOOR)
    aligned_component = jnp.einsum('ci,c...->i...', table, grad, precision=highest)
    surface_perturbation = relaxed + 0.5 * SURFACE_COEF * (lattice_weights * aligned_component * aligned_component - balance * grad_sq) / clipped_values
    red_fraction = 0.5 * (1.0 + phase)
    separated_colours = red_fraction * surface_perturbation + SEGREGATION_RATE * 0.25 * fluid_density * (1.0 - phase * phase) * lattice_weights * aligned_component / clipped_values
    reflected_populations = pops[np.array(OPPOSITE)]
    total_post = jnp.where(wall_nodes, reflected_populations, surface_perturbation)
    red_after_collide = jnp.where(wall_nodes, red_fraction * reflected_populations, separated_colours)
    return (total_post, red_after_collide)

def move(field, ex, ey, ez):
    field = jnp.roll(field, ex, axis=0)
    zeros_row = jnp.zeros((field.shape[0], 1, field.shape[2]), jnp.float32)
    if ey == 1:
        field = jnp.concatenate([zeros_row, field[:, :-1]], axis=1)
    if ey == -1:
        field = jnp.concatenate([field[:, 1:], zeros_row], axis=1)
    return jnp.roll(field, ez, axis=2)

def reference(populations, labels, solid_mask):
    phase = jnp.where(labels > 0, 1.0, -1.0).astype(jnp.float32)
    ypos = jnp.arange(NY)
    wall = (ypos == 0) | (ypos == NY - 1)
    wall_nodes = (solid_mask > 0) | wall[None, :, None]
    pops = populations
    for step in range(STEPS):
        padded = jnp.concatenate([phase[-1:], phase, phase[:1]], axis=0)
        padded = jnp.pad(padded, ((0, 0), (1, 1), (0, 0)))
        grad = gradient_of(padded, NX, NY)

        def plane(position):
            plane_pops = lax.dynamic_index_in_dim(pops, position, 1, keepdims=False)
            plane_grad = lax.dynamic_index_in_dim(grad, position, 1, keepdims=False)
            plane_phase = lax.dynamic_index_in_dim(phase, position, 0, keepdims=False)
            plane_solid = lax.dynamic_index_in_dim(wall_nodes, position, 0, keepdims=False)
            return collide(plane_pops, plane_phase, plane_grad, plane_solid)
        total_post, red_after_collide = lax.map(plane, jnp.arange(NX))
        new_total = jnp.stack([move(total_post[:, d], *VELOCITY_SET[d]) for d in range(19)])
        new_red = jnp.stack([move(red_after_collide[:, d], *VELOCITY_SET[d]) for d in range(19)])
        pops = new_total
        phase = 2.0 * lax.optimization_barrier(jnp.sum(new_red, axis=0)) / lax.optimization_barrier(jnp.sum(new_total, axis=0)) - 1.0
    return (pops, phase)
```

```python
import jax
import jax.numpy as jnp
import numpy as np
from jax import lax
from jax.experimental import pallas as pl
from jax.experimental.pallas import tpu as pltpu
from jax.sharding import PartitionSpec as P

VELOCITY_SET = [
    (0, 0, 0), (1, 0, 0), (-1, 0, 0), (0, 1, 0), (0, -1, 0), (0, 0, 1), (0, 0, -1),
    (1, 1, 0), (-1, -1, 0), (1, -1, 0), (-1, 1, 0), (1, 0, 1), (-1, 0, -1), (1, 0, -1),
    (-1, 0, 1), (0, 1, 1), (0, -1, -1), (0, 1, -1), (0, -1, 1),
]
DIRS = [
    (-1, 0, 0), (-1, 1, 0), (-1, -1, 0), (-1, 0, 1), (-1, 0, -1),
    (1, 0, 0), (1, 1, 0), (1, -1, 0), (1, 0, 1), (1, 0, -1),
    (0, 0, 0), (0, 1, 0), (0, -1, 0), (0, 0, 1), (0, 0, -1),
    (0, 1, 1), (0, -1, -1), (0, 1, -1), (0, -1, 1),
]
REF_OF = [VELOCITY_SET.index(d) for d in DIRS]
POS = {d: k for k, d in enumerate(DIRS)}
GROUPS = [(-1, 0), (-1, 1), (-1, -1), (1, 0), (1, 1), (1, -1), (0, 0), (0, 1), (0, -1)]
GPOS = {g: k for k, g in enumerate(GROUPS)}
NXL = 4
NYL = 32
EXT = 40
NT = 5
ROW0 = 8
SROWS = 56
YROWS = 256
W1 = 1.0 / 18.0
W2 = 1.0 / 36.0


def neg(d):
    return (-d[0], -d[1], -d[2])


def zroll(v, shift):
    if shift == 0:
        return v
    return pltpu.roll(v, shift % 128, 1)


def collide(f):
    def pair(a, b):
        pa, pb = f[a], f[b]
        return pa + pb, pa - pb

    s1, d1 = pair((1, 1, 0), (-1, -1, 0))
    s2, d2 = pair((1, -1, 0), (-1, 1, 0))
    xxyy, xy, xyy, xxy = s1 + s2, s1 - s2, d1 + d2, d1 - d2
    s1, d1 = pair((1, 0, 1), (-1, 0, -1))
    s2, d2 = pair((1, 0, -1), (-1, 0, 1))
    xxzz, xz, xzz, xxz = s1 + s2, s1 - s2, d1 + d2, d1 - d2
    s1, d1 = pair((0, 1, 1), (0, -1, -1))
    s2, d2 = pair((0, 1, -1), (0, -1, 1))
    yyzz, yz, yzz, yyz = s1 + s2, s1 - s2, d1 + d2, d1 - d2
    ax, dx = pair((1, 0, 0), (-1, 0, 0))
    ay, dy = pair((0, 1, 0), (0, -1, 0))
    az, dz = pair((0, 0, 1), (0, 0, -1))
    jx = dx + (xyy + xzz)
    jy = dy + (xxy + yzz)
    jz = dz + (xxz + yyz)
    mxx = ax + (xxyy + xxzz)
    myy = ay + (xxyy + yyzz)
    mzz = az + (xxzz + yyzz)
    rho = (f[(0, 0, 0)] + (ax + ay)) + (az + (xxyy + (xxzz + yyzz)))
    inv = 1.0 / rho
    ux, uy, uz = jx * inv, jy * inv, jz * inv
    qx, qy, qz = jx * ux, jy * uy, jz * uz
    third = rho * (1.0 / 3.0)
    nxx = mxx - third - qx
    nyy = myy - third - qy
    nzz = mzz - third - qz
    trace = nxx + nyy + nzz
    iso = trace * (-1.0 / 24.0)
    hxx = 0.625 * nxx + iso
    hyy = 0.625 * nyy + iso
    hzz = 0.625 * nzz + iso
    dxy = 0.3125 * (xy - jx * uy)
    dxz = 0.3125 * (xz - jx * uz)
    dyz = 0.3125 * (yz - jy * uz)
    kx, ky, kz = jx * 0.1, jy * 0.1, jz * 0.1
    dxyy = 0.3 * xyy - kx
    dxzz = 0.3 * xzz - kx
    dxxy = 0.3 * xxy - ky
    dyzz = 0.3 * yzz - ky
    dxxz = 0.3 * xxz - kz
    dyyz = 0.3 * yyz - kz
    base = (0.35 / 9.0) * rho + (0.35 / 3.0) * (qx + qy + qz)
    dxxyy = 0.35 * xxyy - (base - 0.175 * qz)
    dxxzz = 0.35 * xxzz - (base - 0.175 * qy)
    dyyzz = 0.35 * yyzz - (base - 0.175 * qx)
    out = {}

    def diagonal(quad, cross, la, lb, da, db):
        t1, t2 = quad + cross, quad - cross
        v1, v2 = la + lb, la - lb
        out_dirs = []
        for sa, sb in ((1, 1), (-1, -1), (1, -1), (-1, 1)):
            e = tuple(sa * p + sb * q for p, q in zip(da, db))
            out_dirs.append(e)
        out[out_dirs[0]] = f[out_dirs[0]] - (t1 + v1)
        out[out_dirs[1]] = f[out_dirs[1]] - (t1 - v1)
        out[out_dirs[2]] = f[out_dirs[2]] - (t2 + v2)
        out[out_dirs[3]] = f[out_dirs[3]] - (t2 - v2)

    X, Y, Z = (1, 0, 0), (0, 1, 0), (0, 0, 1)
    diagonal(dxxyy, dxy, dxyy, dxxy, X, Y)
    diagonal(dxxzz, dxz, dxzz, dxxz, X, Z)
    diagonal(dyyzz, dyz, dyzz, dyyz, Y, Z)

    def axis(half, q1, q2, l1, l2, d):
        even = half - 2.0 * (q1 + q2)
        odd = 2.0 * (l1 + l2)
        out[d] = f[d] - (even - odd)
        out[neg(d)] = f[neg(d)] - (even + odd)

    axis(hxx, dxxyy, dxxzz, dxyy, dxzz, X)
    axis(hyy, dxxyy, dyyzz, dxxy, dyzz, Y)
    axis(hzz, dxxzz, dyyzz, dxxz, dyyz, Z)
    out[(0, 0, 0)] = f[(0, 0, 0)] + trace - 4.0 * (dxxyy + dxxzz + dyyzz)
    return out, rho


def gradient(ph, plane, row):
    def at(dx, dy):
        return ph[plane + dx, pl.ds(row + dy, 8), :]

    c = at(0, 0)
    xp, xm, yp, ym = at(1, 0), at(-1, 0), at(0, 1), at(0, -1)
    d1 = at(1, 1) - at(-1, -1)
    d2 = at(1, -1) - at(-1, 1)
    ex = xp - xm
    ey = yp - ym
    h = 2.0 * c + ((xp + xm) + (yp + ym))
    k = 1.0 / 12.0
    gx = k * ((2.0 * ex + (d1 + d2)) + (zroll(ex, 1) + zroll(ex, -1)))
    gy = k * ((2.0 * ey + (d1 - d2)) + (zroll(ey, 1) + zroll(ey, -1)))
    gz = k * (zroll(h, -1) - zroll(h, 1))
    return c, gx, gy, gz


def finish(dirs, s_of, ph, rho, fluid, plane, row, fp, red):
    p, gx, gy, gz = gradient(ph, plane + 1, row)
    g2 = gx * gx + gy * gy + gz * gz
    inv = lax.rsqrt(jnp.maximum(g2, 0.01)) * fluid
    h1 = (0.1 * W1) * inv
    h2 = (0.1 * W2) * inv
    cc = (0.175 * rho) * ((1.0 - p * p) * inv)
    c1 = W1 * cc
    c2 = W2 * cc
    frac = 0.5 + 0.5 * p
    comp = (gx, gy, gz)
    sums = {}
    cache = {}
    for d in dirs:
        moving = [k for k in range(3) if d[k] != 0]
        if not moving:
            q, c = h1 * (6.0 * g2), None
        else:
            sign = d[moving[0]]
            key = d if sign > 0 else neg(d)
            if key not in cache:
                if len(moving) == 1:
                    a = comp[moving[0]]
                    cache[key] = (h1 * (a * a - g2), c1 * a)
                else:
                    u, v = moving
                    a = comp[u] + comp[v] if key[v] > 0 else comp[u] - comp[v]
                    cache[key] = (h2 * (a * a - g2), c2 * a)
            q, c = cache[key]
        val = s_of(d) + q
        fp[POS[d], plane, pl.ds(row, 8), :] = zroll(val, d[2])
        r = frac * val
        if c is not None:
            r = r + c if sign > 0 else r - c
        r = zroll(r, d[2])
        g = d[:2]
        sums[g] = r if g not in sums else sums[g] + r
    for g, r in sums.items():
        red[GPOS[g], plane, pl.ds(row, 8), :] = r


def arrived(d, fp, plane, row):
    return fp[POS[d], plane - d[0], pl.ds(row - d[1], 8), :]


def red_arrived(red, plane, row):
    total = None
    for g in GROUPS:
        v = red[GPOS[g], plane - g[0], pl.ds(row - g[1], 8), :]
        total = v if total is None else total + v
    return total


def tile_rows(t):
    return lax.broadcasted_iota(jnp.int32, (8, 128), 0) + (8 * t - 4)


def pack_y_kernel(pops, labels, solid, out_a, out_b):
    odd = lax.axis_index("gy") % 2

    def pack(out, high):
        for i in range(19):
            for x in range(NXL):
                r = NYL - 3 if high else 0
                out[pl.ds(i * 12 + x * 3, 3), :] = pops[i, x, pl.ds(r, 3), :]
        for x in range(NXL):
            r = NYL - 4 if high else 0
            out[pl.ds(228 + x * 4, 4), :] = labels[x, pl.ds(r, 4), :].astype(jnp.float32)
            r = NYL - 3 if high else 0
            out[pl.ds(244 + x * 3, 3), :] = solid[x, pl.ds(r, 3), :].astype(jnp.float32)

    @pl.when(odd == 0)
    def _():
        pack(out_a, True)
        pack(out_b, False)

    @pl.when(odd == 1)
    def _():
        pack(out_a, False)
        pack(out_b, True)


def first_kernel(pops, labels, solid, ya, yb, s_out, rho_out, fl_out, ph_out, xa, xb, raw, aux):
    gy = lax.axis_index("gy")
    odd = gy % 2
    low_edge = gy == 0
    high_edge = gy == lax.axis_size("gy") - 1

    def unpack(src, top):
        r = 1 if top else 4
        for i in range(19):
            for x in range(NXL):
                raw[i, x, pl.ds(r, 3), :] = src[pl.ds(i * 12 + x * 3, 3), :]
        for x in range(NXL):
            aux[0, x, pl.ds(0 if top else 4, 4), :] = src[pl.ds(228 + x * 4, 4), :]
            aux[1, x, pl.ds(r, 3), :] = src[pl.ds(244 + x * 3, 3), :]

    @pl.when(odd == 0)
    def _():
        unpack(ya, False)
        unpack(yb, True)

    @pl.when(odd == 1)
    def _():
        unpack(ya, True)
        unpack(yb, False)

    def plane(x, carry):
        for t in range(NT):
            def pick(own, halo):
                if 1 <= t <= 3:
                    return own(8 * t - 4, 8)
                if t == 0:
                    return jnp.concatenate([halo()[0:4], own(0, 4)], axis=0)
                return jnp.concatenate([own(NYL - 4, 4), halo()[4:8]], axis=0)

            f = {}
            for k, d in enumerate(DIRS):
                ref = REF_OF[k]
                f[d] = pick(
                    lambda r, n: pops[ref, x, pl.ds(r, n), :], lambda: raw[ref, x]
                )
            lab = pick(
                lambda r, n: labels[x, pl.ds(r, n), :].astype(jnp.float32),
                lambda: aux[0, x],
            )
            sol = pick(
                lambda r, n: solid[x, pl.ds(r, n), :].astype(jnp.float32),
                lambda: aux[1, x],
            )
            y = tile_rows(t)
            is_solid = sol > 0.5
            p = jnp.where(lab > 0.5, 1.0, -1.0)
            inside = None
            if t == 0:
                is_solid = is_solid | ((y == 0) & low_edge)
                inside = (y >= 0) | jnp.logical_not(low_edge)
            if t == NT - 1:
                is_solid = is_solid | ((y == NYL - 1) & high_edge)
                inside = (y < NYL) | jnp.logical_not(high_edge)
            relaxed, rho = collide(f)
            fl = jnp.where(is_solid, 0.0, 1.0)
            if inside is not None:
                fl = jnp.where(inside, fl, 0.0)
                p = jnp.where(inside, p, 0.0)
            rows = pl.ds(8 * t, 8)
            for d in DIRS:
                v = jnp.where(is_solid, f[neg(d)], relaxed[d])
                if inside is not None:
                    v = jnp.where(inside, v, 0.0)
                s_out[POS[d], x, rows, :] = v
            rho_out[x, rows, :] = rho
            fl_out[x, rows, :] = fl
            ph_out[x, rows, :] = p
        return carry

    lax.fori_loop(0, NXL, plane, 0)
    pack_x(s_out, ph_out, rho_out, fl_out, xa, xb)


def pack_x(s, ph, rho, fl, xa, xb):
    odd = lax.axis_index("gx") % 2

    def pack(out, high):
        base = jnp.where(high, 5, 0)
        face = jnp.where(high, NXL - 1, 0)
        second = jnp.where(high, NXL - 2, 1)
        for j in range(5):
            out[j] = s[base + j, face]
        out[5] = rho[face]
        out[6] = ph[face]
        out[7] = ph[second]
        if fl is not None:
            out[8] = fl[face]

    pack(xa, odd == 0)
    pack(xb, odd == 1)


def unpack_x(xa, xb, hx, ph, n):
    odd = lax.axis_index("gx") % 2

    def put(src, side):
        for j in range(n):
            if j not in (6, 7):
                hx[side, j] = src[j]
        near = jnp.where(side == 1, NXL + 2, 1)
        far = jnp.where(side == 1, NXL + 3, 0)
        ph[near, pl.ds(ROW0, EXT), :] = src[6]
        ph[far, pl.ds(ROW0, EXT), :] = src[7]

    put(xa, jnp.where(odd == 0, 1, 0))
    put(xb, jnp.where(odd == 0, 0, 1))


def interface(s, rho, fl, hx, hfl, ph, fp, red):
    def plane(x, carry):
        for t in range(NT):
            rows = pl.ds(8 * t, 8)
            finish(
                DIRS, lambda d: s[POS[d], x, rows, :], ph, rho[x, rows, :],
                fl[x, rows, :], x + 1, ROW0 + 8 * t, fp, red,
            )
        return carry

    lax.fori_loop(0, NXL, plane, 0)
    for side, plane_index, dirs in ((0, 0, DIRS[5:10]), (1, NXL + 1, DIRS[0:5])):
        for t in range(NT):
            rows = pl.ds(8 * t, 8)
            finish(
                dirs, lambda d: hx[side, dirs.index(d), rows, :], ph, hx[side, 5, rows, :],
                hfl[side, rows, :], plane_index, ROW0 + 8 * t, fp, red,
            )


def middle_kernel(s, rho, fl, p_in, xa, xb, s_out, rho_out, ph_out, hfl_out, xa_out, xb_out,
                  hx, ph, fp, red):
    gy = lax.axis_index("gy")
    low_edge = gy == 0
    high_edge = gy == lax.axis_size("gy") - 1
    unpack_x(xa, xb, hx, ph, 9)
    for x in range(NXL):
        ph[x + 2, pl.ds(ROW0, EXT), :] = p_in[x]
    for side in range(2):
        hfl_out[side] = hx[side, 8]
    interface(s, rho, fl, hx, hfl_out, ph, fp, red)

    def plane(x, carry):
        for t in range(NT):
            row = ROW0 + 8 * t
            rows = pl.ds(8 * t, 8)
            f = {d: arrived(d, fp, x + 1, row) for d in DIRS}
            relaxed, total = collide(f)
            p = 2.0 * red_arrived(red, x + 1, row) / total - 1.0
            y = tile_rows(t)
            inside = None
            if t == 0:
                inside = (y >= 0) | jnp.logical_not(low_edge)
            if t == NT - 1:
                inside = (y < NYL) | jnp.logical_not(high_edge)
            if inside is not None:
                p = jnp.where(inside, p, 0.0)
            is_fluid = fl[x, rows, :] > 0.5
            for d in DIRS:
                v = jnp.where(is_fluid, relaxed[d], f[neg(d)])
                if inside is not None:
                    v = jnp.where(inside, v, 0.0)
                s_out[POS[d], x, rows, :] = v
            rho_out[x, rows, :] = total
            ph_out[x, rows, :] = p
        return carry

    lax.fori_loop(0, NXL, plane, 0)
    pack_x(s_out, ph_out, rho_out, None, xa_out, xb_out)


def last_kernel(s, rho, fl, p_in, hfl, xa, xb, pops_out, phase_out, hx, ph, fp, red):
    unpack_x(xa, xb, hx, ph, 8)
    for x in range(NXL):
        ph[x + 2, pl.ds(ROW0, EXT), :] = p_in[x]
    interface(s, rho, fl, hx, hfl, ph, fp, red)

    def plane(x, carry):
        for t in range(NYL // 8):
            row = ROW0 + 4 + 8 * t
            rows = pl.ds(8 * t, 8)
            total = None
            for d in DIRS:
                v = arrived(d, fp, x + 1, row)
                pops_out[REF_OF[POS[d]], x, rows, :] = v
                total = v if total is None else total + v
            phase_out[x, rows, :] = 2.0 * red_arrived(red, x + 1, row) / total - 1.0
        return carry

    lax.fori_loop(0, NXL, plane, 0)


F32 = jnp.float32
VM = pl.BlockSpec(memory_space=pltpu.VMEM)
PARAMS = pltpu.CompilerParams(vmem_limit_bytes=40 * 1024 * 1024)


def shaped(*dims):
    return jax.ShapeDtypeStruct(dims, F32)


def call(kernel, n_in, outs, scratch, name):
    return pl.pallas_call(
        kernel,
        in_specs=[VM] * n_in,
        out_specs=[VM] * len(outs),
        out_shape=outs,
        scratch_shapes=[pltpu.VMEM(d, F32) for d in scratch],
        compiler_params=PARAMS,
        name=name,
    )


def pairs(count, first):
    out = []
    for i in range(first, count + first, 2):
        a, b = i % count, (i + 1) % count
        out += [(a, b), (b, a)]
    return out


def swap(a, b, axis):
    count = lax.axis_size(axis)
    got_b = lax.ppermute(b, axis, pairs(count, 1))
    got_a = lax.ppermute(a, axis, pairs(count, 0))
    return got_a, got_b


def on_device(populations, labels, solid_mask):
    ya, yb = call(pack_y_kernel, 3, [shaped(YROWS, 128)] * 2, [], "pack_y")(
        populations, labels, solid_mask
    )
    ya, yb = swap(ya, yb, "gy")
    s, rho, fl, ph, xa, xb = call(
        first_kernel, 5,
        [shaped(19, NXL, EXT, 128)] + [shaped(NXL, EXT, 128)] * 3 + [shaped(9, EXT, 128)] * 2,
        [(19, NXL, 8, 128), (2, NXL, 8, 128)], "first",
    )(populations, labels, solid_mask, ya, yb)
    xa, xb = swap(xa, xb, "gx")
    work = [
        (2, 9, EXT, 128), (NXL + 4, SROWS, 128), (19, NXL + 2, SROWS, 128),
        (9, NXL + 2, SROWS, 128),
    ]
    s, rho, ph, hfl, xa, xb = call(
        middle_kernel, 6,
        [shaped(19, NXL, EXT, 128)] + [shaped(NXL, EXT, 128)] * 2
        + [shaped(2, EXT, 128)] + [shaped(8, EXT, 128)] * 2,
        work, "middle",
    )(s, rho, fl, ph, xa, xb)
    xa, xb = swap(xa, xb, "gx")
    return call(
        last_kernel, 7, [shaped(19, NXL, NYL, 128), shaped(NXL, NYL, 128)], work, "last",
    )(s, rho, fl, ph, hfl, xa, xb)


def solution(mesh):
    in_specs = (P(None, "gx", "gy", None), P("gx", "gy", None), P("gx", "gy", None))
    out_specs = (P(None, "gx", "gy", None), P("gx", "gy", None))

    def run(populations, labels, solid_mask):
        new, phase = on_device(populations, labels, solid_mask)
        return new, phase

    return jax.shard_map(
        run, mesh=mesh, in_specs=in_specs, out_specs=out_specs, check_vma=False
    )
```

```python
import jax
import jax.numpy as jnp
import numpy as np
from jax import lax
from jax.experimental import pallas as pl
from jax.experimental.pallas import tpu as pltpu
from jax.sharding import PartitionSpec as P

VELOCITY_SET = [
    (0, 0, 0), (1, 0, 0), (-1, 0, 0), (0, 1, 0), (0, -1, 0), (0, 0, 1), (0, 0, -1),
    (1, 1, 0), (-1, -1, 0), (1, -1, 0), (-1, 1, 0), (1, 0, 1), (-1, 0, -1), (1, 0, -1),
    (-1, 0, 1), (0, 1, 1), (0, -1, -1), (0, 1, -1), (0, -1, 1),
]
DIRS = [
    (-1, 0, 0), (-1, 1, 0), (-1, -1, 0), (-1, 0, 1), (-1, 0, -1),
    (1, 0, 0), (1, 1, 0), (1, -1, 0), (1, 0, 1), (1, 0, -1),
    (0, 0, 0), (0, 1, 0), (0, -1, 0), (0, 0, 1), (0, 0, -1),
    (0, 1, 1), (0, -1, -1), (0, 1, -1), (0, -1, 1),
]
REF_OF = [VELOCITY_SET.index(d) for d in DIRS]
POS = {d: k for k, d in enumerate(DIRS)}
GROUPS = [(-1, 0), (-1, 1), (-1, -1), (1, 0), (1, 1), (1, -1), (0, 0), (0, 1), (0, -1)]
GPOS = {g: k for k, g in enumerate(GROUPS)}
NXL = 4
NYL = 32
EXT = 40
NT = 5
ROW0 = 8
SROWS = 56
YROWS = 256
W1 = 1.0 / 18.0
W2 = 1.0 / 36.0


def neg(d):
    return (-d[0], -d[1], -d[2])


def zroll(v, shift):
    if shift == 0:
        return v
    return pltpu.roll(v, shift % 128, 1)


def collide(f):
    def pair(a, b):
        pa, pb = f[a], f[b]
        return pa + pb, pa - pb

    s1, d1 = pair((1, 1, 0), (-1, -1, 0))
    s2, d2 = pair((1, -1, 0), (-1, 1, 0))
    xxyy, xy, xyy, xxy = s1 + s2, s1 - s2, d1 + d2, d1 - d2
    s1, d1 = pair((1, 0, 1), (-1, 0, -1))
    s2, d2 = pair((1, 0, -1), (-1, 0, 1))
    xxzz, xz, xzz, xxz = s1 + s2, s1 - s2, d1 + d2, d1 - d2
    s1, d1 = pair((0, 1, 1), (0, -1, -1))
    s2, d2 = pair((0, 1, -1), (0, -1, 1))
    yyzz, yz, yzz, yyz = s1 + s2, s1 - s2, d1 + d2, d1 - d2
    ax, dx = pair((1, 0, 0), (-1, 0, 0))
    ay, dy = pair((0, 1, 0), (0, -1, 0))
    az, dz = pair((0, 0, 1), (0, 0, -1))
    jx = dx + (xyy + xzz)
    jy = dy + (xxy + yzz)
    jz = dz + (xxz + yyz)
    mxx = ax + (xxyy + xxzz)
    myy = ay + (xxyy + yyzz)
    mzz = az + (xxzz + yyzz)
    rho = (f[(0, 0, 0)] + (ax + ay)) + (az + (xxyy + (xxzz + yyzz)))
    inv = 1.0 / rho
    ux, uy, uz = jx * inv, jy * inv, jz * inv
    qx, qy, qz = jx * ux, jy * uy, jz * uz
    third = rho * (1.0 / 3.0)
    nxx = mxx - third - qx
    nyy = myy - third - qy
    nzz = mzz - third - qz
    trace = nxx + nyy + nzz
    iso = trace * (-1.0 / 24.0)
    hxx = 0.625 * nxx + iso
    hyy = 0.625 * nyy + iso
    hzz = 0.625 * nzz + iso
    dxy = 0.3125 * (xy - jx * uy)
    dxz = 0.3125 * (xz - jx * uz)
    dyz = 0.3125 * (yz - jy * uz)
    kx, ky, kz = jx * 0.1, jy * 0.1, jz * 0.1
    dxyy = 0.3 * xyy - kx
    dxzz = 0.3 * xzz - kx
    dxxy = 0.3 * xxy - ky
    dyzz = 0.3 * yzz - ky
    dxxz = 0.3 * xxz - kz
    dyyz = 0.3 * yyz - kz
    base = (0.35 / 9.0) * rho + (0.35 / 3.0) * (qx + qy + qz)
    dxxyy = 0.35 * xxyy - (base - 0.175 * qz)
    dxxzz = 0.35 * xxzz - (base - 0.175 * qy)
    dyyzz = 0.35 * yyzz - (base - 0.175 * qx)
    out = {}

    def diagonal(quad, cross, la, lb, da, db):
        t1, t2 = quad + cross, quad - cross
        v1, v2 = la + lb, la - lb
        out_dirs = []
        for sa, sb in ((1, 1), (-1, -1), (1, -1), (-1, 1)):
            e = tuple(sa * p + sb * q for p, q in zip(da, db))
            out_dirs.append(e)
        out[out_dirs[0]] = f[out_dirs[0]] - (t1 + v1)
        out[out_dirs[1]] = f[out_dirs[1]] - (t1 - v1)
        out[out_dirs[2]] = f[out_dirs[2]] - (t2 + v2)
        out[out_dirs[3]] = f[out_dirs[3]] - (t2 - v2)

    X, Y, Z = (1, 0, 0), (0, 1, 0), (0, 0, 1)
    diagonal(dxxyy, dxy, dxyy, dxxy, X, Y)
    diagonal(dxxzz, dxz, dxzz, dxxz, X, Z)
    diagonal(dyyzz, dyz, dyzz, dyyz, Y, Z)

    def axis(half, q1, q2, l1, l2, d):
        even = half - 2.0 * (q1 + q2)
        odd = 2.0 * (l1 + l2)
        out[d] = f[d] - (even - odd)
        out[neg(d)] = f[neg(d)] - (even + odd)

    axis(hxx, dxxyy, dxxzz, dxyy, dxzz, X)
    axis(hyy, dxxyy, dyyzz, dxxy, dyzz, Y)
    axis(hzz, dxxzz, dyyzz, dxxz, dyyz, Z)
    out[(0, 0, 0)] = f[(0, 0, 0)] + trace - 4.0 * (dxxyy + dxxzz + dyyzz)
    return out, rho


def gradient(ph, plane, row):
    def at(dx, dy):
        return ph[plane + dx, pl.ds(row + dy, 8), :]

    c = at(0, 0)
    xp, xm, yp, ym = at(1, 0), at(-1, 0), at(0, 1), at(0, -1)
    d1 = at(1, 1) - at(-1, -1)
    d2 = at(1, -1) - at(-1, 1)
    ex = xp - xm
    ey = yp - ym
    h = 2.0 * c + ((xp + xm) + (yp + ym))
    k = 1.0 / 12.0
    gx = k * ((2.0 * ex + (d1 + d2)) + (zroll(ex, 1) + zroll(ex, -1)))
    gy = k * ((2.0 * ey + (d1 - d2)) + (zroll(ey, 1) + zroll(ey, -1)))
    gz = k * (zroll(h, -1) - zroll(h, 1))
    return c, gx, gy, gz


def finish(dirs, s_of, ph, rho, fluid, plane, row, fp, red):
    p, gx, gy, gz = gradient(ph, plane + 1, row)
    g2 = gx * gx + gy * gy + gz * gz
    inv = lax.rsqrt(jnp.maximum(g2, 0.01)) * fluid
    h1 = (0.1 * W1) * inv
    h2 = (0.1 * W2) * inv
    cc = (0.175 * rho) * ((1.0 - p * p) * inv)
    c1 = W1 * cc
    c2 = W2 * cc
    frac = 0.5 + 0.5 * p
    comp = (gx, gy, gz)
    sums = {}
    cache = {}
    for d in dirs:
        moving = [k for k in range(3) if d[k] != 0]
        if not moving:
            q, c = h1 * (6.0 * g2), None
        else:
            sign = d[moving[0]]
            key = d if sign > 0 else neg(d)
            if key not in cache:
                if len(moving) == 1:
                    a = comp[moving[0]]
                    cache[key] = (h1 * (a * a - g2), c1 * a)
                else:
                    u, v = moving
                    a = comp[u] + comp[v] if key[v] > 0 else comp[u] - comp[v]
                    cache[key] = (h2 * (a * a - g2), c2 * a)
            q, c = cache[key]
        val = s_of(d) + q
        fp[POS[d], plane, pl.ds(row, 8), :] = zroll(val, d[2])
        r = frac * val
        if c is not None:
            r = r + c if sign > 0 else r - c
        r = zroll(r, d[2])
        g = d[:2]
        sums[g] = r if g not in sums else sums[g] + r
    for g, r in sums.items():
        red[GPOS[g], plane, pl.ds(row, 8), :] = r


def arrived(d, fp, plane, row):
    return fp[POS[d], plane - d[0], pl.ds(row - d[1], 8), :]


def red_arrived(red, plane, row):
    total = None
    for g in GROUPS:
        v = red[GPOS[g], plane - g[0], pl.ds(row - g[1], 8), :]
        total = v if total is None else total + v
    return total


def tile_rows(t):
    return lax.broadcasted_iota(jnp.int32, (8, 128), 0) + (8 * t - 4)


def face(high):
    a = jnp.where(high, NXL - 1, 0)
    b = jnp.where(high, NXL - 2, 1)
    c = jnp.where(high, NXL - 3, 2)
    out = jnp.where(high, 5, 0)
    back = jnp.where(high, 0, 5)
    return a, b, c, out, back


def build_message(msg, high, tiles, s, rho, fl, ph, fp, red):
    a, b, c, out, back = face(high)
    gout = jnp.where(high, 3, 0)
    gback = jnp.where(high, 0, 3)
    for n, t in enumerate(tiles):
        rows = pl.ds(8 * t, 8)
        to = pl.ds(8 * n, 8)
        row = ROW0 + 8 * t
        for j in range(5):
            msg[j, to, :] = s[out + j, a, rows, :]
        for j in range(9):
            msg[5 + j, to, :] = s[10 + j, a, rows, :]
        total = None
        for j in range(5):
            ey = DIRS[j][1]
            shifted = pl.ds(row - ey, 8)
            msg[14 + j, to, :] = fp[out + j, b + 1, shifted, :]
            v = fp[out + j, c + 1, shifted, :] + fp[back + j, a + 1, shifted, :]
            total = v if total is None else total + v
        for j in range(9):
            total = total + fp[10 + j, b + 1, pl.ds(row - DIRS[10 + j][1], 8), :]
        moved, rsum = None, None
        for j in range(3):
            shifted = pl.ds(row - GROUPS[j][1], 8)
            v = red[gout + j, b + 1, shifted, :]
            moved = v if moved is None else moved + v
            v = (red[gout + j, c + 1, shifted, :] + red[gback + j, a + 1, shifted, :]) + red[
                6 + j, b + 1, shifted, :
            ]
            rsum = v if rsum is None else rsum + v
        msg[19, to, :] = rho[a, rows, :]
        msg[20, to, :] = ph[a + 2, pl.ds(row, 8), :]
        msg[21, to, :] = ph[b + 2, pl.ds(row, 8), :]
        msg[22, to, :] = fl[a, rows, :]
        msg[23, to, :] = moved
        msg[24, to, :] = total
        msg[25, to, :] = rsum


def inner_step(tiles, s, rho, fl, ph, fp, red):
    def plane(x, carry):
        for t in tiles:
            rows = pl.ds(8 * t, 8)
            finish(
                DIRS, lambda d: s[POS[d], x, rows, :], ph, rho[x, rows, :],
                fl[x, rows, :], x + 1, ROW0 + 8 * t, fp, red,
            )
        return carry

    lax.fori_loop(1, NXL - 1, plane, 0)
    for x, base in ((0, 5), (NXL - 1, 0)):
        for t in tiles:
            row = ROW0 + 8 * t
            frac = 0.5 + 0.5 * ph[x + 2, pl.ds(row, 8), :]
            sums = {}
            for d in DIRS[base:base + 5]:
                v = s[POS[d], x, pl.ds(8 * t, 8), :]
                fp[POS[d], x + 1, pl.ds(row, 8), :] = zroll(v, d[2])
                r = zroll(frac * v, d[2])
                sums[d[:2]] = r if d[:2] not in sums else sums[d[:2]] + r
            for g, r in sums.items():
                red[GPOS[g], x + 1, pl.ds(row, 8), :] = r


def start_kernel(pops_hbm, labels_hbm, solid_hbm, ya, yb, s, rho, fl, ph, fp, red, xa, xb,
                 pops, labels, solid, sems):
    gy = lax.axis_index("gy")
    odd = gy % 2
    copies = [
        pltpu.make_async_copy(labels_hbm, labels, sems.at[0]),
        pltpu.make_async_copy(solid_hbm, solid, sems.at[1]),
    ] + [
        pltpu.make_async_copy(pops_hbm.at[:, x], pops.at[:, x], sems.at[2 + x])
        for x in range(NXL)
    ]
    for c in copies:
        c.start()
    for c in copies:
        c.wait()

    def pack(out, high):
        for i in range(19):
            for x in range(NXL):
                r = NYL - 3 if high else 0
                out[pl.ds(i * 12 + x * 3, 3), :] = pops[i, x, pl.ds(r, 3), :]
        for x in range(NXL):
            r = NYL - 4 if high else 0
            out[pl.ds(228 + x * 4, 4), :] = labels[x, pl.ds(r, 4), :].astype(jnp.float32)
            r = NYL - 3 if high else 0
            out[pl.ds(244 + x * 3, 3), :] = solid[x, pl.ds(r, 3), :].astype(jnp.float32)

    @pl.when(odd == 0)
    def _():
        pack(ya, True)
        pack(yb, False)

    @pl.when(odd == 1)
    def _():
        pack(ya, False)
        pack(yb, True)

    low_edge = gy == 0
    high_edge = gy == lax.axis_size("gy") - 1

    def plane(x, carry):
        for t in range(NYL // 8):
            own = pl.ds(8 * t, 8)
            rows = pl.ds(8 * t + 4, 8)
            f = {d: pops[REF_OF[k], x, own, :] for k, d in enumerate(DIRS)}
            is_solid = solid[x, own, :] > 0
            y = lax.broadcasted_iota(jnp.int32, (8, 128), 0) + 8 * t
            if t == 0:
                is_solid = is_solid | ((y == 0) & low_edge)
            if t == NYL // 8 - 1:
                is_solid = is_solid | ((y == NYL - 1) & high_edge)
            relaxed, total = collide(f)
            for d in DIRS:
                s[POS[d], x, rows, :] = jnp.where(is_solid, f[neg(d)], relaxed[d])
            rho[x, rows, :] = total
            fl[x, rows, :] = jnp.where(is_solid, 0.0, 1.0)
            ph[x + 2, pl.ds(ROW0 + 4 + 8 * t, 8), :] = jnp.where(labels[x, own, :] > 0, 1.0, -1.0)
        return carry

    lax.fori_loop(0, NXL, plane, 0)
    inner_step(range(NT), s, rho, fl, ph, fp, red)
    low_a = lax.axis_index("gx") % 2 == 1
    build_message(xb, low_a, (1, 2, 3), s, rho, fl, ph, fp, red)
    build_message(xa, jnp.logical_not(low_a), (1, 2, 3), s, rho, fl, ph, fp, red)


def edge_kernel(ya, yb, s_in, rho_in, fl_in, ph_in, fp_in, red_in,
                s, rho, fl, ph, fp, red, xd, xc, raw):
    gy = lax.axis_index("gy")
    odd = gy % 2
    low_edge = gy == 0
    high_edge = gy == lax.axis_size("gy") - 1

    def unpack(src, top):
        r = 1 if top else 4
        for x in range(NXL):
            for i in range(19):
                raw[i, x, pl.ds(r, 3), :] = src[pl.ds(i * 12 + x * 3, 3), :]
            raw[19, x, pl.ds(0 if top else 4, 4), :] = src[pl.ds(228 + x * 4, 4), :]
            raw[20, x, pl.ds(r, 3), :] = src[pl.ds(244 + x * 3, 3), :]

    @pl.when(odd == 0)
    def _():
        unpack(ya, False)
        unpack(yb, True)

    @pl.when(odd == 1)
    def _():
        unpack(ya, True)
        unpack(yb, False)

    row = lax.broadcasted_iota(jnp.int32, (8, 128), 0)
    inside = jnp.where(row < 4, jnp.where(low_edge, 0, 1), jnp.where(high_edge, 0, 1)) > 0

    def plane(x, carry):
        def put(ref, base, v):
            ref[pl.ds(base, 4), :] = v[0:4]
            ref[pl.ds(base + NYL + 4, 4), :] = v[4:8]

        f = {d: raw[REF_OF[k], x] for k, d in enumerate(DIRS)}
        is_solid = raw[20, x] > 0.5
        relaxed, total = collide(f)
        for d in DIRS:
            v = jnp.where(is_solid, f[neg(d)], relaxed[d])
            put(s.at[POS[d], x], 0, jnp.where(inside, v, 0.0))
        put(rho.at[x], 0, total)
        put(fl.at[x], 0, jnp.where(inside & jnp.logical_not(is_solid), 1.0, 0.0))
        p = jnp.where(raw[19, x] > 0.5, 1.0, -1.0)
        put(ph.at[x + 2], ROW0, jnp.where(inside, p, 0.0))
        return carry

    lax.fori_loop(0, NXL, plane, 0)
    inner_step((0, NT - 1), s, rho, fl, ph, fp, red)
    low_a = lax.axis_index("gx") % 2 == 1
    build_message(xc, low_a, (0, NT - 1), s, rho, fl, ph, fp, red)
    build_message(xd, jnp.logical_not(low_a), (0, NT - 1), s, rho, fl, ph, fp, red)


def last_kernel(s, rho, fl, ph_in, fp_in, red_in, xa, xb, xc, xd,
                pops_out, phase_out, ph, fp, red, hx, s2, rho2):
    gy = lax.axis_index("gy")
    low_edge = gy == 0
    high_edge = gy == lax.axis_size("gy") - 1
    side_a = 1 - lax.axis_index("gx") % 2

    def put(src, side, tiles):
        near = jnp.where(side == 1, NXL + 2, 1)
        far = jnp.where(side == 1, NXL + 3, 0)
        for n, t in enumerate(tiles):
            part = pl.ds(8 * n, 8)
            for j in range(26):
                if j not in (20, 21):
                    hx[side, j, pl.ds(8 * t, 8), :] = src[j, part, :]
            ph[near, pl.ds(ROW0 + 8 * t, 8), :] = src[20, part, :]
            ph[far, pl.ds(ROW0 + 8 * t, 8), :] = src[21, part, :]

    put(xa, side_a, (1, 2, 3))
    put(xd, side_a, (0, NT - 1))
    put(xb, 1 - side_a, (1, 2, 3))
    put(xc, 1 - side_a, (0, NT - 1))

    def mask(t):
        y = tile_rows(t)
        if t == 0:
            return (y >= 0) | jnp.logical_not(low_edge)
        if t == NT - 1:
            return (y < NYL) | jnp.logical_not(high_edge)
        return None

    sides = ((0, 0, DIRS[5:10], DIRS[0:5]), (1, NXL + 1, DIRS[0:5], DIRS[5:10]))

    for x in (0, NXL - 1):
        for t in range(NT):
            rows = pl.ds(8 * t, 8)
            finish(
                DIRS, lambda d: s[POS[d], x, rows, :], ph, rho[x, rows, :],
                fl[x, rows, :], x + 1, ROW0 + 8 * t, fp, red,
            )
    for side, plane_index, towards, back in sides:
        for t in range(NT):
            rows = pl.ds(8 * t, 8)

            def value(d):
                if d in back:
                    return 0.0
                if d in towards:
                    return hx[side, towards.index(d), rows, :]
                return hx[side, 5 + POS[d] - 10, rows, :]

            finish(
                DIRS, value, ph, hx[side, 19, rows, :], hx[side, 22, rows, :],
                plane_index, ROW0 + 8 * t, fp, red,
            )

    def plane(x, carry):
        for t in range(NT):
            row = ROW0 + 8 * t
            rows = pl.ds(8 * t, 8)
            f = {d: arrived(d, fp, x + 1, row) for d in DIRS}
            relaxed, total = collide(f)
            p = 2.0 * red_arrived(red, x + 1, row) / total - 1.0
            inside = mask(t)
            if inside is not None:
                p = jnp.where(inside, p, 0.0)
            is_fluid = fl[x, rows, :] > 0.5
            for d in DIRS:
                v = jnp.where(is_fluid, relaxed[d], f[neg(d)])
                if inside is not None:
                    v = jnp.where(inside, v, 0.0)
                s2[POS[d], x + 1, rows, :] = v
            rho2[x + 1, rows, :] = total
            ph[x + 2, pl.ds(row, 8), :] = p
        return carry

    lax.fori_loop(0, NXL, plane, 0)
    for side, index, towards, back in sides:
        near, far = (NXL + 2, NXL + 3) if side == 1 else (1, 0)
        for t in range(NT):
            row = ROW0 + 8 * t
            rows = pl.ds(8 * t, 8)
            f = {}
            for d in DIRS:
                if d in towards:
                    f[d] = hx[side, 14 + towards.index(d), rows, :]
                else:
                    f[d] = arrived(d, fp, index, row)
            relaxed, total = collide(f)
            rsum = hx[side, 23, rows, :]
            rfar = hx[side, 25, rows, :]
            for g in GROUPS:
                shifted = pl.ds(row - g[1], 8)
                if g[0] != towards[0][0]:
                    rsum = rsum + red[GPOS[g], index - g[0], shifted, :]
                if g[0] == back[0][0]:
                    rfar = rfar + red[GPOS[g], index, shifted, :]
            ffar = hx[side, 24, rows, :]
            for d in back:
                ffar = ffar + fp[POS[d], index, pl.ds(row - d[1], 8), :]
            p = 2.0 * rsum / total - 1.0
            pfar = 2.0 * rfar / ffar - 1.0
            inside = mask(t)
            if inside is not None:
                p = jnp.where(inside, p, 0.0)
                pfar = jnp.where(inside, pfar, 0.0)
            is_fluid = hx[side, 22, rows, :] > 0.5
            for d in towards:
                v = jnp.where(is_fluid, relaxed[d], f[neg(d)])
                if inside is not None:
                    v = jnp.where(inside, v, 0.0)
                s2[POS[d], index, rows, :] = v
            rho2[index, rows, :] = total
            ph[near, pl.ds(row, 8), :] = p
            ph[far, pl.ds(row, 8), :] = pfar

    def second(x, carry):
        for t in range(NT):
            rows = pl.ds(8 * t, 8)
            finish(
                DIRS, lambda d: s2[POS[d], x + 1, rows, :], ph, rho2[x + 1, rows, :],
                fl[x, rows, :], x + 1, ROW0 + 8 * t, fp, red,
            )
        return carry

    lax.fori_loop(0, NXL, second, 0)
    for side, index, towards, back in sides:
        for t in range(NT):
            rows = pl.ds(8 * t, 8)
            finish(
                towards, lambda d: s2[POS[d], index, rows, :], ph, rho2[index, rows, :],
                hx[side, 22, rows, :], index, ROW0 + 8 * t, fp, red,
            )

    def final(x, carry):
        for t in range(NYL // 8):
            row = ROW0 + 4 + 8 * t
            rows = pl.ds(8 * t, 8)
            total = None
            for d in DIRS:
                v = arrived(d, fp, x + 1, row)
                pops_out[REF_OF[POS[d]], x, rows, :] = v
                total = v if total is None else total + v
            phase_out[x, rows, :] = 2.0 * red_arrived(red, x + 1, row) / total - 1.0
        return carry

    lax.fori_loop(0, NXL, final, 0)


F32 = jnp.float32
VM = pl.BlockSpec(memory_space=pltpu.VMEM)
HB = pl.BlockSpec(memory_space=pltpu.HBM)
MIB = 1024 * 1024


def shaped(*dims):
    return jax.ShapeDtypeStruct(dims, F32)


def call(kernel, in_specs, outs, scratch, name, aliases=None, vmem=40, cost=0):
    return pl.pallas_call(
        kernel,
        in_specs=in_specs,
        out_specs=[VM] * len(outs),
        out_shape=outs,
        scratch_shapes=scratch,
        input_output_aliases=aliases or {},
        compiler_params=pltpu.CompilerParams(vmem_limit_bytes=vmem * MIB),
        cost_estimate=pl.CostEstimate(flops=cost, bytes_accessed=cost, transcendentals=0),
        name=name,
    )


def pairs(count, first):
    out = []
    for i in range(first, count + first, 2):
        a, b = i % count, (i + 1) % count
        out += [(a, b), (b, a)]
    return out


def swap(value, axis, first):
    return lax.ppermute(value, axis, pairs(lax.axis_size(axis), first))


def on_device(populations, labels, solid_mask):
    state = [
        shaped(19, NXL, EXT, 128), shaped(NXL, EXT, 128), shaped(NXL, EXT, 128),
        shaped(NXL + 4, SROWS, 128), shaped(19, NXL + 2, SROWS, 128),
        shaped(9, NXL + 2, SROWS, 128),
    ]
    got = call(
        start_kernel, [HB] * 3, [shaped(YROWS, 128)] * 2 + state + [shaped(26, 24, 128)] * 2,
        [
            pltpu.VMEM((19, NXL, NYL, 128), F32), pltpu.VMEM((NXL, NYL, 128), jnp.int32),
            pltpu.VMEM((NXL, NYL, 128), jnp.int32), pltpu.SemaphoreType.DMA((6,)),
        ],
        "start", vmem=40,
    )(*[pltpu.with_memory_space_constraint(v, pltpu.HBM) for v in (populations, labels, solid_mask)])
    ya, yb, *mid, xa, xb = got
    xb = swap(xb, "gx", 1)
    xa = swap(xa, "gx", 0)
    ya = swap(ya, "gy", 0)
    yb = swap(yb, "gy", 1)
    *mid, xd, xc = call(
        edge_kernel, [VM] * 8, state + [shaped(26, 16, 128)] * 2,
        [pltpu.VMEM((21, NXL, 8, 128), F32)], "edge", {2 + i: i for i in range(6)},
    )(ya, yb, *mid)
    xc = swap(xc, "gx", 1)
    xd = swap(xd, "gx", 0)
    out = call(
        last_kernel, [VM] * 10,
        [shaped(19, NXL, NYL, 128), shaped(NXL, NYL, 128)] + state[3:],
        [
            pltpu.VMEM((2, 26, EXT, 128), F32), pltpu.VMEM((19, NXL + 2, EXT, 128), F32),
            pltpu.VMEM((NXL + 2, EXT, 128), F32),
        ],
        "last", {3: 2, 4: 3, 5: 4},
    )(*mid, xa, xb, xc, xd)
    return out[0], out[1]


def solution(mesh):
    in_specs = (P(None, "gx", "gy", None), P("gx", "gy", None), P("gx", "gy", None))
    out_specs = (P(None, "gx", "gy", None), P("gx", "gy", None))

    def run(populations, labels, solid_mask):
        new, phase = on_device(populations, labels, solid_mask)
        return new, phase

    return jax.shard_map(
        run, mesh=mesh, in_specs=in_specs, out_specs=out_specs, check_vma=False
    )
```

```python
import jax
import jax.numpy as jnp
import numpy as np
from jax import lax
from jax.experimental import pallas as pl
from jax.experimental.pallas import tpu as pltpu
from jax.sharding import PartitionSpec as P

VELOCITY_SET = [
    (0, 0, 0), (1, 0, 0), (-1, 0, 0), (0, 1, 0), (0, -1, 0), (0, 0, 1), (0, 0, -1),
    (1, 1, 0), (-1, -1, 0), (1, -1, 0), (-1, 1, 0), (1, 0, 1), (-1, 0, -1), (1, 0, -1),
    (-1, 0, 1), (0, 1, 1), (0, -1, -1), (0, 1, -1), (0, -1, 1),
]
DIRS = [
    (-1, 0, 0), (-1, 1, 0), (-1, -1, 0), (-1, 0, 1), (-1, 0, -1),
    (1, 0, 0), (1, 1, 0), (1, -1, 0), (1, 0, 1), (1, 0, -1),
    (0, 0, 0), (0, 1, 0), (0, -1, 0), (0, 0, 1), (0, 0, -1),
    (0, 1, 1), (0, -1, -1), (0, 1, -1), (0, -1, 1),
]
REF_OF = [VELOCITY_SET.index(d) for d in DIRS]
POS = {d: k for k, d in enumerate(DIRS)}
GROUPS = [(-1, 0), (-1, 1), (-1, -1), (1, 0), (1, 1), (1, -1), (0, 0), (0, 1), (0, -1)]
GPOS = {g: k for k, g in enumerate(GROUPS)}
NXL = 4
NYL = 32
EXT = 40
NT = 5
ROW0 = 8
SROWS = 56
YROWS = 256
W1 = 1.0 / 18.0
W2 = 1.0 / 36.0


def neg(d):
    return (-d[0], -d[1], -d[2])


def zroll(v, shift):
    if shift == 0:
        return v
    return pltpu.roll(v, shift % 128, 1)


def collide(f, known=None, equilibrium=True):
    def pair(a, b):
        pa, pb = f[a], f[b]
        if pb is None:
            return pa, pa
        if pa is None:
            return pb, -pb
        return pa + pb, pa - pb

    s1, d1 = pair((1, 1, 0), (-1, -1, 0))
    s2, d2 = pair((1, -1, 0), (-1, 1, 0))
    xxyy, xy, xyy, xxy = s1 + s2, s1 - s2, d1 + d2, d1 - d2
    s1, d1 = pair((1, 0, 1), (-1, 0, -1))
    s2, d2 = pair((1, 0, -1), (-1, 0, 1))
    xxzz, xz, xzz, xxz = s1 + s2, s1 - s2, d1 + d2, d1 - d2
    s1, d1 = pair((0, 1, 1), (0, -1, -1))
    s2, d2 = pair((0, 1, -1), (0, -1, 1))
    yyzz, yz, yzz, yyz = s1 + s2, s1 - s2, d1 + d2, d1 - d2
    ax, dx = pair((1, 0, 0), (-1, 0, 0))
    ay, dy = pair((0, 1, 0), (0, -1, 0))
    az, dz = pair((0, 0, 1), (0, 0, -1))
    jx = dx + (xyy + xzz)
    jy = dy + (xxy + yzz)
    jz = dz + (xxz + yyz)
    nxx = ax + (xxyy + xxzz)
    nyy = ay + (xxyy + yyzz)
    nzz = az + (xxzz + yyzz)
    rho = (f[(0, 0, 0)] + (ax + ay)) + (az + (xxyy + (xxzz + yyzz)))
    if known is not None:
        rho, jx, jy, jz = rho + known[0], jx + known[1], jy + known[2], jz + known[3]
    dxy, dxz, dyz = 0.3125 * xy, 0.3125 * xz, 0.3125 * yz
    dxyy, dxzz, dxxy = 0.3 * xyy, 0.3 * xzz, 0.3 * xxy
    dyzz, dxxz, dyyz = 0.3 * yzz, 0.3 * xxz, 0.3 * yyz
    dxxyy, dxxzz, dyyzz = 0.35 * xxyy, 0.35 * xxzz, 0.35 * yyzz
    if equilibrium:
        inv = 1.0 / rho
        ux, uy, uz = jx * inv, jy * inv, jz * inv
        qx, qy, qz = jx * ux, jy * uy, jz * uz
        third = rho * (1.0 / 3.0)
        nxx = nxx - (third + qx)
        nyy = nyy - (third + qy)
        nzz = nzz - (third + qz)
        dxy = 0.3125 * (xy - jx * uy)
        dxz = 0.3125 * (xz - jx * uz)
        dyz = 0.3125 * (yz - jy * uz)
        kx, ky, kz = jx * 0.1, jy * 0.1, jz * 0.1
        dxyy, dxzz = dxyy - kx, dxzz - kx
        dxxy, dyzz = dxxy - ky, dyzz - ky
        dxxz, dyyz = dxxz - kz, dyyz - kz
        base = (0.35 / 9.0) * rho + (0.35 / 3.0) * (qx + qy + qz)
        dxxyy = dxxyy - (base - 0.175 * qz)
        dxxzz = dxxzz - (base - 0.175 * qy)
        dyyzz = dyyzz - (base - 0.175 * qx)
    trace = nxx + nyy + nzz
    iso = trace * (-1.0 / 24.0)
    hxx = 0.625 * nxx + iso
    hyy = 0.625 * nyy + iso
    hzz = 0.625 * nzz + iso
    out = {}

    def less(d, v):
        return -v if f[d] is None else f[d] - v

    def diagonal(quad, cross, la, lb, da, db):
        t1, t2 = quad + cross, quad - cross
        v1, v2 = la + lb, la - lb
        out_dirs = []
        for sa, sb in ((1, 1), (-1, -1), (1, -1), (-1, 1)):
            e = tuple(sa * p + sb * q for p, q in zip(da, db))
            out_dirs.append(e)
        out[out_dirs[0]] = less(out_dirs[0], t1 + v1)
        out[out_dirs[1]] = less(out_dirs[1], t1 - v1)
        out[out_dirs[2]] = less(out_dirs[2], t2 + v2)
        out[out_dirs[3]] = less(out_dirs[3], t2 - v2)

    X, Y, Z = (1, 0, 0), (0, 1, 0), (0, 0, 1)
    diagonal(dxxyy, dxy, dxyy, dxxy, X, Y)
    diagonal(dxxzz, dxz, dxzz, dxxz, X, Z)
    diagonal(dyyzz, dyz, dyzz, dyyz, Y, Z)

    def axis(half, q1, q2, l1, l2, d):
        even = half - 2.0 * (q1 + q2)
        odd = 2.0 * (l1 + l2)
        out[d] = less(d, even - odd)
        out[neg(d)] = less(neg(d), even + odd)

    axis(hxx, dxxyy, dxxzz, dxyy, dxzz, X)
    axis(hyy, dxxyy, dyyzz, dxxy, dyzz, Y)
    axis(hzz, dxxzz, dyyzz, dxxz, dyyz, Z)
    out[(0, 0, 0)] = f[(0, 0, 0)] + trace - 4.0 * (dxxyy + dxxzz + dyyzz)
    return out, rho, (jx, jy, jz)


def gradient(ph, plane, row):
    def at(dx, dy):
        return ph[plane + dx, pl.ds(row + dy, 8), :]

    c = at(0, 0)
    xp, xm, yp, ym = at(1, 0), at(-1, 0), at(0, 1), at(0, -1)
    d1 = at(1, 1) - at(-1, -1)
    d2 = at(1, -1) - at(-1, 1)
    ex = xp - xm
    ey = yp - ym
    h = 2.0 * c + ((xp + xm) + (yp + ym))
    k = 1.0 / 12.0
    gx = k * ((2.0 * ex + (d1 + d2)) + (zroll(ex, 1) + zroll(ex, -1)))
    gy = k * ((2.0 * ey + (d1 - d2)) + (zroll(ey, 1) + zroll(ey, -1)))
    gz = k * (zroll(h, -1) - zroll(h, 1))
    return c, gx, gy, gz


def finish(dirs, s_of, ph, rho, fluid, plane, row, fp, red):
    p, gx, gy, gz = gradient(ph, plane + 1, row)
    g2 = gx * gx + gy * gy + gz * gz
    inv = lax.rsqrt(jnp.maximum(g2, 0.01)) * fluid
    h1 = (0.1 * W1) * inv
    h2 = (0.1 * W2) * inv
    cc = (0.175 * rho) * ((1.0 - p * p) * inv)
    c1 = W1 * cc
    c2 = W2 * cc
    frac = 0.5 + 0.5 * p
    comp = (gx, gy, gz)
    sums = {}
    cache = {}
    for d in dirs:
        moving = [k for k in range(3) if d[k] != 0]
        if not moving:
            q, c = h1 * (6.0 * g2), None
        else:
            sign = d[moving[0]]
            key = d if sign > 0 else neg(d)
            if key not in cache:
                if len(moving) == 1:
                    a = comp[moving[0]]
                    cache[key] = (h1 * (a * a - g2), c1 * a)
                else:
                    u, v = moving
                    a = comp[u] + comp[v] if key[v] > 0 else comp[u] - comp[v]
                    cache[key] = (h2 * (a * a - g2), c2 * a)
            q, c = cache[key]
        known = s_of(d)
        val = q if known is None else known + q
        fp[POS[d], plane, pl.ds(row, 8), :] = zroll(val, d[2])
        r = frac * val
        if c is not None:
            r = r + c if sign > 0 else r - c
        r = zroll(r, d[2])
        g = d[:2]
        sums[g] = r if g not in sums else sums[g] + r
    for g, r in sums.items():
        red[GPOS[g], plane, pl.ds(row, 8), :] = r


def arrived(d, fp, plane, row):
    return fp[POS[d], plane - d[0], pl.ds(row - d[1], 8), :]


def red_arrived(red, plane, row):
    total = None
    for g in GROUPS:
        v = red[GPOS[g], plane - g[0], pl.ds(row - g[1], 8), :]
        total = v if total is None else total + v
    return total


def tile_rows(t):
    return lax.broadcasted_iota(jnp.int32, (8, 128), 0) + (8 * t - 4)


def face(high):
    a = jnp.where(high, NXL - 1, 0)
    b = jnp.where(high, NXL - 2, 1)
    c = jnp.where(high, NXL - 3, 2)
    out = jnp.where(high, 5, 0)
    back = jnp.where(high, 0, 5)
    return a, b, c, out, back


def message_tile(high, row, s, rho, fl, ph, fp, red):
    a, b, c, out, back = face(high)
    gout = jnp.where(high, 3, 0)
    gback = jnp.where(high, 0, 3)
    rows = pl.ds(row - ROW0, 8)
    own = pl.ds(row, 8)

    def plain():
        v = [s[out + j, a, rows, :] for j in range(5)]
        return v, [rho[a, rows, :], ph[a + 2, own, :], ph[b + 2, own, :], fl[a, rows, :]]

    def moved():
        f = {}
        total = None
        for j in range(5):
            d = DIRS[5 + j]
            shifted = pl.ds(row - d[1], 8)
            f[d] = fp[out + j, b + 1, shifted, :]
            f[(-1, d[1], d[2])] = None
            v = fp[out + j, c + 1, shifted, :] + fp[back + j, a + 1, shifted, :]
            total = v if total is None else total + v
        for j in range(10, 19):
            shifted = pl.ds(row - DIRS[j][1], 8)
            f[DIRS[j]] = fp[j, a + 1, shifted, :]
            total = total + fp[j, b + 1, shifted, :]
        linear, dens, mom = collide(f, equilibrium=False)
        at_a, at_b = None, None
        for j in range(3):
            shifted = pl.ds(row - GROUPS[j][1], 8)
            v = red[gout + j, b + 1, shifted, :] + red[6 + j, a + 1, shifted, :]
            at_a = v if at_a is None else at_a + v
            v = (red[gout + j, c + 1, shifted, :] + red[gback + j, a + 1, shifted, :]) + red[
                6 + j, b + 1, shifted, :
            ]
            at_b = v if at_b is None else at_b + v
        return [linear[DIRS[5 + j]] for j in range(5)] + [dens, *mom], [at_a, total, at_b]

    return plain, moved


PLAIN = [0, 1, 2, 3, 4, 14, 15, 16, 17]
MOVED = [5, 6, 7, 8, 9, 10, 11, 12, 13, 18, 19, 20]


def main_message(msg, high, state):
    for n in range(NYL // 8):
        plain, moved = message_tile(high, ROW0 + 4 + 8 * n, *state)
        for kinds, part in ((PLAIN, plain()), (MOVED, moved())):
            for j, v in zip(kinds, part[0] + part[1]):
                msg[j, pl.ds(8 * n, 8), :] = v


def corner_message(msg, high, state):
    for n, (first, second) in enumerate(((0, 2), (EXT - 8, EXT - 6))):
        plain, _ = message_tile(high, ROW0 + first, *state)
        _, moved = message_tile(high, ROW0 + second, *state)
        for kinds, part, r in ((PLAIN, plain(), 4 * n), (MOVED, moved(), 0)):
            for j, v in zip(kinds, part[0] + part[1]):
                msg[j, pl.ds(4 * n, 4), :] = v[r:r + 4]


def inner_step(tiles, s, rho, fl, ph, fp, red):
    def plane(x, carry):
        for t in tiles:
            rows = pl.ds(8 * t, 8)
            finish(
                DIRS, lambda d: s[POS[d], x, rows, :], ph, rho[x, rows, :],
                fl[x, rows, :], x + 1, ROW0 + 8 * t, fp, red,
            )
        return carry

    lax.fori_loop(1, NXL - 1, plane, 0)
    for x, base in ((0, 5), (NXL - 1, 0)):
        for t in tiles:
            row = ROW0 + 8 * t
            frac = 0.5 + 0.5 * ph[x + 2, pl.ds(row, 8), :]
            sums = {}
            for d in DIRS[base:base + 5] + DIRS[10:]:
                v = s[POS[d], x, pl.ds(8 * t, 8), :]
                fp[POS[d], x + 1, pl.ds(row, 8), :] = zroll(v, d[2])
                r = zroll(frac * v, d[2])
                sums[d[:2]] = r if d[:2] not in sums else sums[d[:2]] + r
            for g, r in sums.items():
                red[GPOS[g], x + 1, pl.ds(row, 8), :] = r


def pack_kernel(pops_hbm, labels_hbm, solid_hbm, ya, yb, pops, labels, solid, sems):
    odd = lax.axis_index("gy") % 2
    copies = []
    for k, r in enumerate((0, NYL - 8)):
        ends = pl.ds(r, 8)
        part = pl.ds(8 * k, 8)
        copies += [
            pltpu.make_async_copy(pops_hbm.at[:, :, ends], pops.at[:, :, part], sems.at[3 * k]),
            pltpu.make_async_copy(labels_hbm.at[:, ends], labels.at[:, part], sems.at[3 * k + 1]),
            pltpu.make_async_copy(solid_hbm.at[:, ends], solid.at[:, part], sems.at[3 * k + 2]),
        ]
    for c in copies:
        c.start()
    for c in copies:
        c.wait()

    def pack(out, high):
        three = pl.ds(13 if high else 0, 3)
        four = pl.ds(12 if high else 0, 4)
        for i in range(19):
            for x in range(NXL):
                out[pl.ds(i * 12 + x * 3, 3), :] = pops[i, x, three, :]
        for x in range(NXL):
            out[pl.ds(228 + x * 4, 4), :] = labels[x, four, :].astype(jnp.float32)
            out[pl.ds(244 + x * 3, 3), :] = solid[x, three, :].astype(jnp.float32)

    @pl.when(odd == 0)
    def _():
        pack(ya, True)
        pack(yb, False)

    @pl.when(odd == 1)
    def _():
        pack(ya, False)
        pack(yb, True)


def start_kernel(pops_hbm, labels_hbm, solid_hbm, s, rho, fl, ph, fp, red, xa, xb,
                 pops, labels, solid, sems):
    gy = lax.axis_index("gy")
    copies = [
        pltpu.make_async_copy(labels_hbm, labels, sems.at[0]),
        pltpu.make_async_copy(solid_hbm, solid, sems.at[1]),
    ] + [
        pltpu.make_async_copy(pops_hbm.at[:, x], pops.at[:, x], sems.at[2 + x])
        for x in range(NXL)
    ]
    for c in copies:
        c.start()
    for c in copies:
        c.wait()

    low_edge = gy == 0
    high_edge = gy == lax.axis_size("gy") - 1

    def plane(x, carry):
        for t in range(NYL // 8):
            own = pl.ds(8 * t, 8)
            rows = pl.ds(8 * t + 4, 8)
            f = {d: pops[REF_OF[k], x, own, :] for k, d in enumerate(DIRS)}
            is_solid = solid[x, own, :] > 0
            y = lax.broadcasted_iota(jnp.int32, (8, 128), 0) + 8 * t
            if t == 0:
                is_solid = is_solid | ((y == 0) & low_edge)
            if t == NYL // 8 - 1:
                is_solid = is_solid | ((y == NYL - 1) & high_edge)
            relaxed, total, _ = collide(f)
            for d in DIRS:
                s[POS[d], x, rows, :] = jnp.where(is_solid, f[neg(d)], relaxed[d])
            rho[x, rows, :] = total
            fl[x, rows, :] = jnp.where(is_solid, 0.0, 1.0)
            ph[x + 2, pl.ds(ROW0 + 4 + 8 * t, 8), :] = jnp.where(labels[x, own, :] > 0, 1.0, -1.0)
        return carry

    lax.fori_loop(0, NXL, plane, 0)
    inner_step(range(NT), s, rho, fl, ph, fp, red)
    low_a = lax.axis_index("gx") % 2 == 1
    main_message(xb, low_a, (s, rho, fl, ph, fp, red))
    main_message(xa, jnp.logical_not(low_a), (s, rho, fl, ph, fp, red))


def edge_kernel(ya, yb, s_in, rho_in, fl_in, ph_in, fp_in, red_in,
                s, rho, fl, ph, fp, red, xd, xc, raw):
    gy = lax.axis_index("gy")
    odd = gy % 2
    low_edge = gy == 0
    high_edge = gy == lax.axis_size("gy") - 1

    def unpack(src, top):
        r = 1 if top else 4
        for x in range(NXL):
            for i in range(19):
                raw[i, x, pl.ds(r, 3), :] = src[pl.ds(i * 12 + x * 3, 3), :]
            raw[19, x, pl.ds(0 if top else 4, 4), :] = src[pl.ds(228 + x * 4, 4), :]
            raw[20, x, pl.ds(r, 3), :] = src[pl.ds(244 + x * 3, 3), :]

    @pl.when(odd == 0)
    def _():
        unpack(ya, False)
        unpack(yb, True)

    @pl.when(odd == 1)
    def _():
        unpack(ya, True)
        unpack(yb, False)

    row = lax.broadcasted_iota(jnp.int32, (8, 128), 0)
    inside = jnp.where(row < 4, jnp.where(low_edge, 0, 1), jnp.where(high_edge, 0, 1)) > 0

    def plane(x, carry):
        def put(ref, base, v):
            ref[pl.ds(base, 4), :] = v[0:4]
            ref[pl.ds(base + NYL + 4, 4), :] = v[4:8]

        f = {d: raw[REF_OF[k], x] for k, d in enumerate(DIRS)}
        is_solid = raw[20, x] > 0.5
        relaxed, total, _ = collide(f)
        for d in DIRS:
            v = jnp.where(is_solid, f[neg(d)], relaxed[d])
            put(s.at[POS[d], x], 0, jnp.where(inside, v, 0.0))
        put(rho.at[x], 0, total)
        put(fl.at[x], 0, jnp.where(inside & jnp.logical_not(is_solid), 1.0, 0.0))
        p = jnp.where(raw[19, x] > 0.5, 1.0, -1.0)
        put(ph.at[x + 2], ROW0, jnp.where(inside, p, 0.0))
        return carry

    lax.fori_loop(0, NXL, plane, 0)
    inner_step((0, NT - 1), s, rho, fl, ph, fp, red)
    low_a = lax.axis_index("gx") % 2 == 1
    corner_message(xc, low_a, (s, rho, fl, ph, fp, red))
    corner_message(xd, jnp.logical_not(low_a), (s, rho, fl, ph, fp, red))


def last_kernel(s, rho, fl, ph_in, fp_in, red_in, xa, xb, xc, xd,
                pops_hbm, phase_hbm, ph, fp, red, hx, s2, rho2, pops_out, phase_out, sems):
    gy = lax.axis_index("gy")
    low_edge = gy == 0
    high_edge = gy == lax.axis_size("gy") - 1
    side_a = 1 - lax.axis_index("gx") % 2

    def put(src, side, corner):
        near = jnp.where(side == 1, NXL + 2, 1)
        far = jnp.where(side == 1, NXL + 3, 0)
        for j in range(21):
            moved = 2 if corner and j in MOVED else 0
            if corner:
                spans = ((moved, 0, 4), (EXT - 4 - moved, 4, 4))
            else:
                spans = [(4 + 8 * n, 8 * n, 8) for n in range(NYL // 8)]
            for to, part, n in spans:
                v = src[j, pl.ds(part, n), :]
                if j in (15, 16):
                    ph[near if j == 15 else far, pl.ds(ROW0 + to, n), :] = v
                else:
                    hx[side, j, pl.ds(to, n), :] = v

    put(xa, side_a, False)
    put(xb, 1 - side_a, False)
    put(xd, side_a, True)
    put(xc, 1 - side_a, True)

    def mask(t):
        y = tile_rows(t)
        if t == 0:
            return (y >= 0) | jnp.logical_not(low_edge)
        if t == NT - 1:
            return (y < NYL) | jnp.logical_not(high_edge)
        return None

    sides = ((0, 0, DIRS[5:10], DIRS[0:5]), (1, NXL + 1, DIRS[0:5], DIRS[5:10]))

    for x in (0, NXL - 1):
        for t in range(NT):
            rows = pl.ds(8 * t, 8)
            finish(
                DIRS, lambda d: s[POS[d], x, rows, :], ph, rho[x, rows, :],
                fl[x, rows, :], x + 1, ROW0 + 8 * t, fp, red,
            )
    for side, plane_index, towards, back in sides:
        for t in range(NT):
            rows = pl.ds(8 * t, 8)

            def value(d):
                return hx[side, towards.index(d), rows, :] if d in towards else None

            finish(
                DIRS, value, ph, hx[side, 14, rows, :], hx[side, 17, rows, :],
                plane_index, ROW0 + 8 * t, fp, red,
            )

    def plane(x, carry):
        for t in range(NT):
            row = ROW0 + 8 * t
            rows = pl.ds(8 * t, 8)
            f = {d: arrived(d, fp, x + 1, row) for d in DIRS}
            relaxed, total, _ = collide(f)
            p = 2.0 * red_arrived(red, x + 1, row) / total - 1.0
            inside = mask(t)
            if inside is not None:
                p = jnp.where(inside, p, 0.0)
            is_fluid = fl[x, rows, :] > 0.5
            for d in DIRS:
                v = jnp.where(is_fluid, relaxed[d], f[neg(d)])
                if inside is not None:
                    v = jnp.where(inside, v, 0.0)
                s2[POS[d], x + 1, rows, :] = v
            rho2[x + 1, rows, :] = total
            ph[x + 2, pl.ds(row, 8), :] = p
        return carry

    lax.fori_loop(0, NXL, plane, 0)
    for side, index, towards, back in sides:
        near, far = (NXL + 2, NXL + 3) if side == 1 else (1, 0)
        for t in range(NT):
            row = ROW0 + 8 * t
            rows = pl.ds(8 * t, 8)
            f = {d: None if d in towards else arrived(d, fp, index, row) for d in DIRS}
            outwards = 1.0 if towards[0][0] > 0 else -1.0
            known = (
                hx[side, 10, rows, :], outwards * hx[side, 11, rows, :],
                hx[side, 12, rows, :], hx[side, 13, rows, :],
            )
            relaxed, total, _ = collide(f, known)
            rsum = hx[side, 18, rows, :]
            rfar = hx[side, 20, rows, :]
            for g in GROUPS:
                shifted = pl.ds(row - g[1], 8)
                if g[0] != towards[0][0]:
                    rsum = rsum + red[GPOS[g], index - g[0], shifted, :]
                if g[0] == back[0][0]:
                    rfar = rfar + red[GPOS[g], index, shifted, :]
            ffar = hx[side, 19, rows, :]
            for d in back:
                ffar = ffar + fp[POS[d], index, pl.ds(row - d[1], 8), :]
            p = 2.0 * rsum / total - 1.0
            pfar = 2.0 * rfar / ffar - 1.0
            inside = mask(t)
            if inside is not None:
                p = jnp.where(inside, p, 0.0)
                pfar = jnp.where(inside, pfar, 0.0)
            is_fluid = hx[side, 17, rows, :] > 0.5
            for j, d in enumerate(towards):
                v = jnp.where(is_fluid, relaxed[d] + hx[side, 5 + j, rows, :], f[neg(d)])
                if inside is not None:
                    v = jnp.where(inside, v, 0.0)
                s2[POS[d], index, rows, :] = v
            rho2[index, rows, :] = total
            ph[near, pl.ds(row, 8), :] = p
            ph[far, pl.ds(row, 8), :] = pfar

    def second(x, carry):
        for t in range(NT):
            rows = pl.ds(8 * t, 8)
            finish(
                DIRS, lambda d: s2[POS[d], x + 1, rows, :], ph, rho2[x + 1, rows, :],
                fl[x, rows, :], x + 1, ROW0 + 8 * t, fp, red,
            )
        return carry

    lax.fori_loop(0, NXL, second, 0)
    for side, index, towards, back in sides:
        for t in range(NT):
            rows = pl.ds(8 * t, 8)
            finish(
                towards, lambda d: s2[POS[d], index, rows, :], ph, rho2[index, rows, :],
                hx[side, 17, rows, :], index, ROW0 + 8 * t, fp, red,
            )

    def out_copies(x):
        return (
            pltpu.make_async_copy(pops_out.at[:, x], pops_hbm.at[:, x], sems.at[2 * x]),
            pltpu.make_async_copy(phase_out.at[x], phase_hbm.at[x], sems.at[2 * x + 1]),
        )

    def final(x, carry):
        for t in range(NYL // 8):
            row = ROW0 + 4 + 8 * t
            rows = pl.ds(8 * t, 8)
            total = None
            for d in DIRS:
                v = arrived(d, fp, x + 1, row)
                pops_out[REF_OF[POS[d]], x, rows, :] = v
                total = v if total is None else total + v
            phase_out[x, rows, :] = 2.0 * red_arrived(red, x + 1, row) / total - 1.0
        return carry

    for x in range(NXL):
        final(x, 0)
        for copy in out_copies(x):
            copy.start()
    for x in range(NXL):
        for copy in out_copies(x):
            copy.wait()


F32 = jnp.float32
VM = pl.BlockSpec(memory_space=pltpu.VMEM)
HB = pl.BlockSpec(memory_space=pltpu.HBM)
MIB = 1024 * 1024


def shaped(*dims):
    return jax.ShapeDtypeStruct(dims, F32)


def call(kernel, in_specs, outs, scratch, name, aliases=None, vmem=40, cost=0,
         out_specs=None):
    return pl.pallas_call(
        kernel,
        in_specs=in_specs,
        out_specs=out_specs or [VM] * len(outs),
        out_shape=outs,
        scratch_shapes=scratch,
        input_output_aliases=aliases or {},
        compiler_params=pltpu.CompilerParams(vmem_limit_bytes=vmem * MIB),
        cost_estimate=pl.CostEstimate(flops=cost, bytes_accessed=cost, transcendentals=0),
        name=name,
    )


def pairs(count, first):
    out = []
    for i in range(first, count + first, 2):
        a, b = i % count, (i + 1) % count
        out += [(a, b), (b, a)]
    return out


def swap(value, axis, first):
    return lax.ppermute(value, axis, pairs(lax.axis_size(axis), first))


def on_device(populations, labels, solid_mask):
    state = [
        shaped(19, NXL, EXT, 128), shaped(NXL, EXT, 128), shaped(NXL, EXT, 128),
        shaped(NXL + 4, SROWS, 128), shaped(19, NXL + 2, SROWS, 128),
        shaped(9, NXL + 2, SROWS, 128),
    ]
    inputs = [
        pltpu.with_memory_space_constraint(v, pltpu.HBM)
        for v in (populations, labels, solid_mask)
    ]

    def staging(rows):
        return [
            pltpu.VMEM((19, NXL, rows, 128), F32), pltpu.VMEM((NXL, rows, 128), jnp.int32),
            pltpu.VMEM((NXL, rows, 128), jnp.int32), pltpu.SemaphoreType.DMA((6,)),
        ]

    ya, yb = call(
        pack_kernel, [HB] * 3, [shaped(YROWS, 128)] * 2, staging(16), "pack",
    )(*inputs)
    ya = swap(ya, "gy", 0)
    yb = swap(yb, "gy", 1)
    *mid, xa, xb = call(
        start_kernel, [HB] * 3, state + [shaped(21, NYL, 128)] * 2, staging(NYL), "start",
    )(*inputs)
    xb = swap(xb, "gx", 1)
    xa = swap(xa, "gx", 0)
    *mid, xd, xc = call(
        edge_kernel, [VM] * 8, state + [shaped(21, 8, 128)] * 2,
        [pltpu.VMEM((21, NXL, 8, 128), F32)], "edge", {2 + i: i for i in range(6)},
    )(ya, yb, *mid)
    xc = swap(xc, "gx", 1)
    xd = swap(xd, "gx", 0)
    out = call(
        last_kernel, [VM] * 10,
        [shaped(19, NXL, NYL, 128), shaped(NXL, NYL, 128)] + state[3:],
        [
            pltpu.VMEM((2, 21, EXT, 128), F32), pltpu.VMEM((19, NXL + 2, EXT, 128), F32),
            pltpu.VMEM((NXL + 2, EXT, 128), F32), pltpu.VMEM((19, NXL, NYL, 128), F32),
            pltpu.VMEM((NXL, NYL, 128), F32), pltpu.SemaphoreType.DMA((2 * NXL,)),
        ],
        "last", {3: 2, 4: 3, 5: 4}, out_specs=[HB] * 2 + [VM] * 3,
    )(*mid, xa, xb, xc, xd)
    return out[0], out[1]


def solution(mesh):
    in_specs = (P(None, "gx", "gy", None), P("gx", "gy", None), P("gx", "gy", None))
    out_specs = (P(None, "gx", "gy", None), P("gx", "gy", None))

    def run(populations, labels, solid_mask):
        new, phase = on_device(populations, labels, solid_mask)
        return new, phase

    return jax.shard_map(
        run, mesh=mesh, in_specs=in_specs, out_specs=out_specs, check_vma=False
    )
```

```python
import jax
import jax.numpy as jnp
import numpy as np
from jax import lax
from jax.experimental import pallas as pl
from jax.experimental.pallas import tpu as pltpu
from jax.sharding import PartitionSpec as P

VELOCITY_SET = [
    (0, 0, 0), (1, 0, 0), (-1, 0, 0), (0, 1, 0), (0, -1, 0), (0, 0, 1), (0, 0, -1),
    (1, 1, 0), (-1, -1, 0), (1, -1, 0), (-1, 1, 0), (1, 0, 1), (-1, 0, -1), (1, 0, -1),
    (-1, 0, 1), (0, 1, 1), (0, -1, -1), (0, 1, -1), (0, -1, 1),
]
DIRS = [
    (-1, 0, 0), (-1, 1, 0), (-1, -1, 0), (-1, 0, 1), (-1, 0, -1),
    (1, 0, 0), (1, 1, 0), (1, -1, 0), (1, 0, 1), (1, 0, -1),
    (0, 0, 0), (0, 1, 0), (0, -1, 0), (0, 0, 1), (0, 0, -1),
    (0, 1, 1), (0, -1, -1), (0, 1, -1), (0, -1, 1),
]
REF_OF = [VELOCITY_SET.index(d) for d in DIRS]
POS = {d: k for k, d in enumerate(DIRS)}
GROUPS = [(-1, 0), (-1, 1), (-1, -1), (1, 0), (1, 1), (1, -1), (0, 0), (0, 1), (0, -1)]
GPOS = {g: k for k, g in enumerate(GROUPS)}
NXL = 4
NYL = 32
EXT = 40
NT = 5
ROW0 = 8
SROWS = 56
YROWS = 256
W1 = 1.0 / 18.0
W2 = 1.0 / 36.0


def neg(d):
    return (-d[0], -d[1], -d[2])


def zroll(v, shift):
    if shift == 0:
        return v
    return pltpu.roll(v, shift % 128, 1)


def collide(f, known=None, equilibrium=True):
    def pair(a, b):
        pa, pb = f[a], f[b]
        if pb is None:
            return pa, pa
        if pa is None:
            return pb, -pb
        return pa + pb, pa - pb

    s1, d1 = pair((1, 1, 0), (-1, -1, 0))
    s2, d2 = pair((1, -1, 0), (-1, 1, 0))
    xxyy, xy, xyy, xxy = s1 + s2, s1 - s2, d1 + d2, d1 - d2
    s1, d1 = pair((1, 0, 1), (-1, 0, -1))
    s2, d2 = pair((1, 0, -1), (-1, 0, 1))
    xxzz, xz, xzz, xxz = s1 + s2, s1 - s2, d1 + d2, d1 - d2
    s1, d1 = pair((0, 1, 1), (0, -1, -1))
    s2, d2 = pair((0, 1, -1), (0, -1, 1))
    yyzz, yz, yzz, yyz = s1 + s2, s1 - s2, d1 + d2, d1 - d2
    ax, dx = pair((1, 0, 0), (-1, 0, 0))
    ay, dy = pair((0, 1, 0), (0, -1, 0))
    az, dz = pair((0, 0, 1), (0, 0, -1))
    jx = dx + (xyy + xzz)
    jy = dy + (xxy + yzz)
    jz = dz + (xxz + yyz)
    nxx = ax + (xxyy + xxzz)
    nyy = ay + (xxyy + yyzz)
    nzz = az + (xxzz + yyzz)
    rho = (f[(0, 0, 0)] + (ax + ay)) + (az + (xxyy + (xxzz + yyzz)))
    if known is not None:
        rho, jx, jy, jz = rho + known[0], jx + known[1], jy + known[2], jz + known[3]
    dxy, dxz, dyz = 0.3125 * xy, 0.3125 * xz, 0.3125 * yz
    dxyy, dxzz, dxxy = 0.3 * xyy, 0.3 * xzz, 0.3 * xxy
    dyzz, dxxz, dyyz = 0.3 * yzz, 0.3 * xxz, 0.3 * yyz
    dxxyy, dxxzz, dyyzz = 0.35 * xxyy, 0.35 * xxzz, 0.35 * yyzz
    if equilibrium:
        inv = 1.0 / rho
        ux, uy, uz = jx * inv, jy * inv, jz * inv
        qx, qy, qz = jx * ux, jy * uy, jz * uz
        third = rho * (1.0 / 3.0)
        nxx = nxx - (third + qx)
        nyy = nyy - (third + qy)
        nzz = nzz - (third + qz)
        dxy = 0.3125 * (xy - jx * uy)
        dxz = 0.3125 * (xz - jx * uz)
        dyz = 0.3125 * (yz - jy * uz)
        kx, ky, kz = jx * 0.1, jy * 0.1, jz * 0.1
        dxyy, dxzz = dxyy - kx, dxzz - kx
        dxxy, dyzz = dxxy - ky, dyzz - ky
        dxxz, dyyz = dxxz - kz, dyyz - kz
        base = (0.35 / 9.0) * rho + (0.35 / 3.0) * (qx + qy + qz)
        dxxyy = dxxyy - (base - 0.175 * qz)
        dxxzz = dxxzz - (base - 0.175 * qy)
        dyyzz = dyyzz - (base - 0.175 * qx)
    trace = nxx + nyy + nzz
    iso = trace * (-1.0 / 24.0)
    hxx = 0.625 * nxx + iso
    hyy = 0.625 * nyy + iso
    hzz = 0.625 * nzz + iso
    out = {}

    def less(d, v):
        return -v if f[d] is None else f[d] - v

    def diagonal(quad, cross, la, lb, da, db):
        t1, t2 = quad + cross, quad - cross
        v1, v2 = la + lb, la - lb
        out_dirs = []
        for sa, sb in ((1, 1), (-1, -1), (1, -1), (-1, 1)):
            e = tuple(sa * p + sb * q for p, q in zip(da, db))
            out_dirs.append(e)
        out[out_dirs[0]] = less(out_dirs[0], t1 + v1)
        out[out_dirs[1]] = less(out_dirs[1], t1 - v1)
        out[out_dirs[2]] = less(out_dirs[2], t2 + v2)
        out[out_dirs[3]] = less(out_dirs[3], t2 - v2)

    X, Y, Z = (1, 0, 0), (0, 1, 0), (0, 0, 1)
    diagonal(dxxyy, dxy, dxyy, dxxy, X, Y)
    diagonal(dxxzz, dxz, dxzz, dxxz, X, Z)
    diagonal(dyyzz, dyz, dyzz, dyyz, Y, Z)

    def axis(half, q1, q2, l1, l2, d):
        even = half - 2.0 * (q1 + q2)
        odd = 2.0 * (l1 + l2)
        out[d] = less(d, even - odd)
        out[neg(d)] = less(neg(d), even + odd)

    axis(hxx, dxxyy, dxxzz, dxyy, dxzz, X)
    axis(hyy, dxxyy, dyyzz, dxxy, dyzz, Y)
    axis(hzz, dxxzz, dyyzz, dxxz, dyyz, Z)
    out[(0, 0, 0)] = f[(0, 0, 0)] + trace - 4.0 * (dxxyy + dxxzz + dyyzz)
    return out, rho, (jx, jy, jz)


def gradient(ph, plane, row):
    def at(dx, dy):
        return ph[plane + dx, pl.ds(row + dy, 8), :]

    c = at(0, 0)
    xp, xm, yp, ym = at(1, 0), at(-1, 0), at(0, 1), at(0, -1)
    d1 = at(1, 1) - at(-1, -1)
    d2 = at(1, -1) - at(-1, 1)
    ex = xp - xm
    ey = yp - ym
    h = 2.0 * c + ((xp + xm) + (yp + ym))
    k = 1.0 / 12.0
    gx = k * ((2.0 * ex + (d1 + d2)) + (zroll(ex, 1) + zroll(ex, -1)))
    gy = k * ((2.0 * ey + (d1 - d2)) + (zroll(ey, 1) + zroll(ey, -1)))
    gz = k * (zroll(h, -1) - zroll(h, 1))
    return c, gx, gy, gz


def finish(dirs, s_of, ph, rho, fluid, plane, row, fp, red):
    p, gx, gy, gz = gradient(ph, plane + 1, row)
    g2 = gx * gx + gy * gy + gz * gz
    inv = lax.rsqrt(jnp.maximum(g2, 0.01)) * fluid
    h1 = (0.1 * W1) * inv
    h2 = (0.1 * W2) * inv
    cc = (0.175 * rho) * ((1.0 - p * p) * inv)
    c1 = W1 * cc
    c2 = W2 * cc
    frac = 0.5 + 0.5 * p
    comp = (gx, gy, gz)
    sums = {}
    cache = {}
    for d in dirs:
        moving = [k for k in range(3) if d[k] != 0]
        if not moving:
            q, c = h1 * (6.0 * g2), None
        else:
            sign = d[moving[0]]
            key = d if sign > 0 else neg(d)
            if key not in cache:
                if len(moving) == 1:
                    a = comp[moving[0]]
                    cache[key] = (h1 * (a * a - g2), c1 * a)
                else:
                    u, v = moving
                    a = comp[u] + comp[v] if key[v] > 0 else comp[u] - comp[v]
                    cache[key] = (h2 * (a * a - g2), c2 * a)
            q, c = cache[key]
        known = s_of(d)
        val = q if known is None else known + q
        fp[POS[d], plane, pl.ds(row, 8), :] = zroll(val, d[2])
        r = frac * val
        if c is not None:
            r = r + c if sign > 0 else r - c
        r = zroll(r, d[2])
        g = d[:2]
        sums[g] = r if g not in sums else sums[g] + r
    for g, r in sums.items():
        red[GPOS[g], plane, pl.ds(row, 8), :] = r


def arrived(d, fp, plane, row):
    return fp[POS[d], plane - d[0], pl.ds(row - d[1], 8), :]


def red_arrived(red, plane, row):
    total = None
    for g in GROUPS:
        v = red[GPOS[g], plane - g[0], pl.ds(row - g[1], 8), :]
        total = v if total is None else total + v
    return total


def tile_rows(t):
    return lax.broadcasted_iota(jnp.int32, (8, 128), 0) + (8 * t - 4)


def face(high):
    a = jnp.where(high, NXL - 1, 0)
    b = jnp.where(high, NXL - 2, 1)
    c = jnp.where(high, NXL - 3, 2)
    out = jnp.where(high, 5, 0)
    back = jnp.where(high, 0, 5)
    return a, b, c, out, back


def message_tile(high, row, s, rho, fl, ph, fp, red):
    a, b, c, out, back = face(high)
    gout = jnp.where(high, 3, 0)
    gback = jnp.where(high, 0, 3)
    rows = pl.ds(row - ROW0, 8)
    own = pl.ds(row, 8)

    def plain():
        v = [s[out + j, a, rows, :] for j in range(5)]
        return v, [rho[a, rows, :], ph[a + 2, own, :], ph[b + 2, own, :], fl[a, rows, :]]

    def moved():
        f = {}
        total = None
        for j in range(5):
            d = DIRS[5 + j]
            shifted = pl.ds(row - d[1], 8)
            f[d] = fp[out + j, b + 1, shifted, :]
            f[(-1, d[1], d[2])] = None
            v = fp[out + j, c + 1, shifted, :] + fp[back + j, a + 1, shifted, :]
            total = v if total is None else total + v
        for j in range(10, 19):
            shifted = pl.ds(row - DIRS[j][1], 8)
            f[DIRS[j]] = fp[j, a + 1, shifted, :]
            total = total + fp[j, b + 1, shifted, :]
        linear, dens, mom = collide(f, equilibrium=False)
        at_a, at_b = None, None
        for j in range(3):
            shifted = pl.ds(row - GROUPS[j][1], 8)
            v = red[gout + j, b + 1, shifted, :] + red[6 + j, a + 1, shifted, :]
            at_a = v if at_a is None else at_a + v
            v = (red[gout + j, c + 1, shifted, :] + red[gback + j, a + 1, shifted, :]) + red[
                6 + j, b + 1, shifted, :
            ]
            at_b = v if at_b is None else at_b + v
        return [linear[DIRS[5 + j]] for j in range(5)] + [dens, *mom], [at_a, total, at_b]

    return plain, moved


PLAIN = [0, 1, 2, 3, 4, 14, 15, 16, 17]
MOVED = [5, 6, 7, 8, 9, 10, 11, 12, 13, 18, 19, 20]


def main_message(msg, high, state):
    for n in range(NYL // 8):
        plain, moved = message_tile(high, ROW0 + 4 + 8 * n, *state)
        for kinds, part in ((PLAIN, plain()), (MOVED, moved())):
            for j, v in zip(kinds, part[0] + part[1]):
                msg[j, pl.ds(8 * n, 8), :] = v


def corner_message(msg, high, state):
    for n, (first, second) in enumerate(((0, 2), (EXT - 8, EXT - 6))):
        plain, _ = message_tile(high, ROW0 + first, *state)
        _, moved = message_tile(high, ROW0 + second, *state)
        for kinds, part, r in ((PLAIN, plain(), 4 * n), (MOVED, moved(), 0)):
            for j, v in zip(kinds, part[0] + part[1]):
                msg[j, pl.ds(4 * n, 4), :] = v[r:r + 4]


def inner_step(tiles, s, rho, fl, ph, fp, red):
    def plane(x, carry):
        for t in tiles:
            rows = pl.ds(8 * t, 8)
            finish(
                DIRS, lambda d: s[POS[d], x, rows, :], ph, rho[x, rows, :],
                fl[x, rows, :], x + 1, ROW0 + 8 * t, fp, red,
            )
        return carry

    lax.fori_loop(1, NXL - 1, plane, 0)
    for x, base in ((0, 5), (NXL - 1, 0)):
        for t in tiles:
            row = ROW0 + 8 * t
            frac = 0.5 + 0.5 * ph[x + 2, pl.ds(row, 8), :]
            sums = {}
            for d in DIRS[base:base + 5] + DIRS[10:]:
                v = s[POS[d], x, pl.ds(8 * t, 8), :]
                fp[POS[d], x + 1, pl.ds(row, 8), :] = zroll(v, d[2])
                r = zroll(frac * v, d[2])
                sums[d[:2]] = r if d[:2] not in sums else sums[d[:2]] + r
            for g, r in sums.items():
                red[GPOS[g], x + 1, pl.ds(row, 8), :] = r


def pack_kernel(pops_hbm, labels_hbm, solid_hbm, ya, yb, pops, labels, solid, sems):
    odd = lax.axis_index("gy") % 2
    copies = []
    for k, r in enumerate((0, NYL - 8)):
        ends = pl.ds(r, 8)
        part = pl.ds(8 * k, 8)
        copies += [
            pltpu.make_async_copy(pops_hbm.at[:, :, ends], pops.at[:, :, part], sems.at[3 * k]),
            pltpu.make_async_copy(labels_hbm.at[:, ends], labels.at[:, part], sems.at[3 * k + 1]),
            pltpu.make_async_copy(solid_hbm.at[:, ends], solid.at[:, part], sems.at[3 * k + 2]),
        ]
    for c in copies:
        c.start()
    for c in copies:
        c.wait()

    def pack(out, high):
        three = pl.ds(13 if high else 0, 3)
        four = pl.ds(12 if high else 0, 4)
        for i in range(19):
            for x in range(NXL):
                out[pl.ds(i * 12 + x * 3, 3), :] = pops[i, x, three, :]
        for x in range(NXL):
            out[pl.ds(228 + x * 4, 4), :] = labels[x, four, :].astype(jnp.float32)
            out[pl.ds(244 + x * 3, 3), :] = solid[x, three, :].astype(jnp.float32)

    @pl.when(odd == 0)
    def _():
        pack(ya, True)
        pack(yb, False)

    @pl.when(odd == 1)
    def _():
        pack(ya, False)
        pack(yb, True)


def start_kernel(pops_hbm, labels_hbm, solid_hbm, after, s, rho, fl, ph, fp, red, xa, xb,
                 pops, labels, solid, sems):
    gy = lax.axis_index("gy")
    copies = [
        pltpu.make_async_copy(labels_hbm, labels, sems.at[0]),
        pltpu.make_async_copy(solid_hbm, solid, sems.at[1]),
    ] + [
        pltpu.make_async_copy(pops_hbm.at[:, x], pops.at[:, x], sems.at[2 + x])
        for x in range(NXL)
    ]
    for c in copies:
        c.start()
    for c in copies:
        c.wait()

    low_edge = gy == 0
    high_edge = gy == lax.axis_size("gy") - 1

    def plane(x, carry):
        for t in range(NYL // 8):
            own = pl.ds(8 * t, 8)
            rows = pl.ds(8 * t + 4, 8)
            f = {d: pops[REF_OF[k], x, own, :] for k, d in enumerate(DIRS)}
            is_solid = solid[x, own, :] > 0
            y = lax.broadcasted_iota(jnp.int32, (8, 128), 0) + 8 * t
            if t == 0:
                is_solid = is_solid | ((y == 0) & low_edge)
            if t == NYL // 8 - 1:
                is_solid = is_solid | ((y == NYL - 1) & high_edge)
            relaxed, total, _ = collide(f)
            for d in DIRS:
                s[POS[d], x, rows, :] = jnp.where(is_solid, f[neg(d)], relaxed[d])
            rho[x, rows, :] = total
            fl[x, rows, :] = jnp.where(is_solid, 0.0, 1.0)
            ph[x + 2, pl.ds(ROW0 + 4 + 8 * t, 8), :] = jnp.where(labels[x, own, :] > 0, 1.0, -1.0)
        return carry

    lax.fori_loop(0, NXL, plane, 0)
    inner_step(range(NT), s, rho, fl, ph, fp, red)
    low_a = lax.axis_index("gx") % 2 == 1
    main_message(xb, low_a, (s, rho, fl, ph, fp, red))
    main_message(xa, jnp.logical_not(low_a), (s, rho, fl, ph, fp, red))


def edge_kernel(ya, yb, s_in, rho_in, fl_in, ph_in, fp_in, red_in,
                s, rho, fl, ph, fp, red, xd, xc, raw):
    gy = lax.axis_index("gy")
    odd = gy % 2
    low_edge = gy == 0
    high_edge = gy == lax.axis_size("gy") - 1

    def unpack(src, top):
        r = 1 if top else 4
        for x in range(NXL):
            for i in range(19):
                raw[i, x, pl.ds(r, 3), :] = src[pl.ds(i * 12 + x * 3, 3), :]
            raw[19, x, pl.ds(0 if top else 4, 4), :] = src[pl.ds(228 + x * 4, 4), :]
            raw[20, x, pl.ds(r, 3), :] = src[pl.ds(244 + x * 3, 3), :]

    @pl.when(odd == 0)
    def _():
        unpack(ya, False)
        unpack(yb, True)

    @pl.when(odd == 1)
    def _():
        unpack(ya, True)
        unpack(yb, False)

    row = lax.broadcasted_iota(jnp.int32, (8, 128), 0)
    inside = jnp.where(row < 4, jnp.where(low_edge, 0, 1), jnp.where(high_edge, 0, 1)) > 0

    def plane(x, carry):
        def put(ref, base, v):
            ref[pl.ds(base, 4), :] = v[0:4]
            ref[pl.ds(base + NYL + 4, 4), :] = v[4:8]

        f = {d: raw[REF_OF[k], x] for k, d in enumerate(DIRS)}
        is_solid = raw[20, x] > 0.5
        relaxed, total, _ = collide(f)
        for d in DIRS:
            v = jnp.where(is_solid, f[neg(d)], relaxed[d])
            put(s.at[POS[d], x], 0, jnp.where(inside, v, 0.0))
        put(rho.at[x], 0, total)
        put(fl.at[x], 0, jnp.where(inside & jnp.logical_not(is_solid), 1.0, 0.0))
        p = jnp.where(raw[19, x] > 0.5, 1.0, -1.0)
        put(ph.at[x + 2], ROW0, jnp.where(inside, p, 0.0))
        return carry

    lax.fori_loop(0, NXL, plane, 0)
    inner_step((0, NT - 1), s, rho, fl, ph, fp, red)
    low_a = lax.axis_index("gx") % 2 == 1
    corner_message(xc, low_a, (s, rho, fl, ph, fp, red))
    corner_message(xd, jnp.logical_not(low_a), (s, rho, fl, ph, fp, red))


def last_kernel(s, rho, fl, ph_in, fp_in, red_in, xa, xb, xc, xd,
                pops_hbm, phase_hbm, ph, fp, red, hx, s2, rho2, pops_out, phase_out, sems):
    gy = lax.axis_index("gy")
    low_edge = gy == 0
    high_edge = gy == lax.axis_size("gy") - 1
    side_a = 1 - lax.axis_index("gx") % 2

    def put(src, side, corner):
        near = jnp.where(side == 1, NXL + 2, 1)
        far = jnp.where(side == 1, NXL + 3, 0)
        for j in range(21):
            moved = 2 if corner and j in MOVED else 0
            if corner:
                spans = ((moved, 0, 4), (EXT - 4 - moved, 4, 4))
            else:
                spans = [(4 + 8 * n, 8 * n, 8) for n in range(NYL // 8)]
            for to, part, n in spans:
                v = src[j, pl.ds(part, n), :]
                if j in (15, 16):
                    ph[near if j == 15 else far, pl.ds(ROW0 + to, n), :] = v
                else:
                    hx[side, j, pl.ds(to, n), :] = v

    put(xa, side_a, False)
    put(xb, 1 - side_a, False)
    put(xd, side_a, True)
    put(xc, 1 - side_a, True)

    def mask(t):
        y = tile_rows(t)
        if t == 0:
            return (y >= 0) | jnp.logical_not(low_edge)
        if t == NT - 1:
            return (y < NYL) | jnp.logical_not(high_edge)
        return None

    sides = ((0, 0, DIRS[5:10], DIRS[0:5]), (1, NXL + 1, DIRS[0:5], DIRS[5:10]))

    for x in (0, NXL - 1):
        for t in range(NT):
            rows = pl.ds(8 * t, 8)
            finish(
                DIRS, lambda d: s[POS[d], x, rows, :], ph, rho[x, rows, :],
                fl[x, rows, :], x + 1, ROW0 + 8 * t, fp, red,
            )
    for side, plane_index, towards, back in sides:
        for t in range(NT):
            rows = pl.ds(8 * t, 8)

            def value(d):
                return hx[side, towards.index(d), rows, :] if d in towards else None

            finish(
                DIRS, value, ph, hx[side, 14, rows, :], hx[side, 17, rows, :],
                plane_index, ROW0 + 8 * t, fp, red,
            )

    def plane(x, carry):
        for t in range(NT):
            row = ROW0 + 8 * t
            rows = pl.ds(8 * t, 8)
            f = {d: arrived(d, fp, x + 1, row) for d in DIRS}
            relaxed, total, _ = collide(f)
            p = 2.0 * red_arrived(red, x + 1, row) / total - 1.0
            inside = mask(t)
            if inside is not None:
                p = jnp.where(inside, p, 0.0)
            is_fluid = fl[x, rows, :] > 0.5
            for d in DIRS:
                v = jnp.where(is_fluid, relaxed[d], f[neg(d)])
                if inside is not None:
                    v = jnp.where(inside, v, 0.0)
                s2[POS[d], x + 1, rows, :] = v
            rho2[x + 1, rows, :] = total
            ph[x + 2, pl.ds(row, 8), :] = p
        return carry

    lax.fori_loop(0, NXL, plane, 0)
    for side, index, towards, back in sides:
        near, far = (NXL + 2, NXL + 3) if side == 1 else (1, 0)
        for t in range(NT):
            row = ROW0 + 8 * t
            rows = pl.ds(8 * t, 8)
            f = {d: None if d in towards else arrived(d, fp, index, row) for d in DIRS}
            outwards = 1.0 if towards[0][0] > 0 else -1.0
            known = (
                hx[side, 10, rows, :], outwards * hx[side, 11, rows, :],
                hx[side, 12, rows, :], hx[side, 13, rows, :],
            )
            relaxed, total, _ = collide(f, known)
            rsum = hx[side, 18, rows, :]
            rfar = hx[side, 20, rows, :]
            for g in GROUPS:
                shifted = pl.ds(row - g[1], 8)
                if g[0] != towards[0][0]:
                    rsum = rsum + red[GPOS[g], index - g[0], shifted, :]
                if g[0] == back[0][0]:
                    rfar = rfar + red[GPOS[g], index, shifted, :]
            ffar = hx[side, 19, rows, :]
            for d in back:
                ffar = ffar + fp[POS[d], index, pl.ds(row - d[1], 8), :]
            p = 2.0 * rsum / total - 1.0
            pfar = 2.0 * rfar / ffar - 1.0
            inside = mask(t)
            if inside is not None:
                p = jnp.where(inside, p, 0.0)
                pfar = jnp.where(inside, pfar, 0.0)
            is_fluid = hx[side, 17, rows, :] > 0.5
            for j, d in enumerate(towards):
                v = jnp.where(is_fluid, relaxed[d] + hx[side, 5 + j, rows, :], f[neg(d)])
                if inside is not None:
                    v = jnp.where(inside, v, 0.0)
                s2[POS[d], index, rows, :] = v
            rho2[index, rows, :] = total
            ph[near, pl.ds(row, 8), :] = p
            ph[far, pl.ds(row, 8), :] = pfar

    def second(x, carry):
        for t in range(NT):
            rows = pl.ds(8 * t, 8)
            finish(
                DIRS, lambda d: s2[POS[d], x + 1, rows, :], ph, rho2[x + 1, rows, :],
                fl[x, rows, :], x + 1, ROW0 + 8 * t, fp, red,
            )
        return carry

    lax.fori_loop(0, NXL, second, 0)
    for side, index, towards, back in sides:
        for t in range(NT):
            rows = pl.ds(8 * t, 8)
            finish(
                towards, lambda d: s2[POS[d], index, rows, :], ph, rho2[index, rows, :],
                hx[side, 17, rows, :], index, ROW0 + 8 * t, fp, red,
            )

    def out_copies(x):
        return (
            pltpu.make_async_copy(pops_out.at[:, x], pops_hbm.at[:, x], sems.at[2 * x]),
            pltpu.make_async_copy(phase_out.at[x], phase_hbm.at[x], sems.at[2 * x + 1]),
        )

    def final(x, carry):
        for t in range(NYL // 8):
            row = ROW0 + 4 + 8 * t
            rows = pl.ds(8 * t, 8)
            total = None
            for d in DIRS:
                v = arrived(d, fp, x + 1, row)
                pops_out[REF_OF[POS[d]], x, rows, :] = v
                total = v if total is None else total + v
            phase_out[x, rows, :] = 2.0 * red_arrived(red, x + 1, row) / total - 1.0
        return carry

    for x in range(NXL):
        final(x, 0)
        for copy in out_copies(x):
            copy.start()
    for x in range(NXL):
        for copy in out_copies(x):
            copy.wait()


F32 = jnp.float32
VM = pl.BlockSpec(memory_space=pltpu.VMEM)
HB = pl.BlockSpec(memory_space=pltpu.HBM)
MIB = 1024 * 1024


def shaped(*dims):
    return jax.ShapeDtypeStruct(dims, F32)


def call(kernel, in_specs, outs, scratch, name, aliases=None, vmem=40, cost=0,
         out_specs=None):
    return pl.pallas_call(
        kernel,
        in_specs=in_specs,
        out_specs=out_specs or [VM] * len(outs),
        out_shape=outs,
        scratch_shapes=scratch,
        input_output_aliases=aliases or {},
        compiler_params=pltpu.CompilerParams(vmem_limit_bytes=vmem * MIB),
        cost_estimate=pl.CostEstimate(flops=cost, bytes_accessed=cost, transcendentals=0),
        name=name,
    )


def pairs(count, first):
    out = []
    for i in range(first, count + first, 2):
        a, b = i % count, (i + 1) % count
        out += [(a, b), (b, a)]
    return out


def swap(value, axis, first):
    return lax.ppermute(value, axis, pairs(lax.axis_size(axis), first))


def on_device(populations, labels, solid_mask):
    state = [
        shaped(19, NXL, EXT, 128), shaped(NXL, EXT, 128), shaped(NXL, EXT, 128),
        shaped(NXL + 4, SROWS, 128), shaped(19, NXL + 2, SROWS, 128),
        shaped(9, NXL + 2, SROWS, 128),
    ]
    inputs = [
        pltpu.with_memory_space_constraint(v, pltpu.HBM)
        for v in (populations, labels, solid_mask)
    ]

    def staging(rows):
        return [
            pltpu.VMEM((19, NXL, rows, 128), F32), pltpu.VMEM((NXL, rows, 128), jnp.int32),
            pltpu.VMEM((NXL, rows, 128), jnp.int32), pltpu.SemaphoreType.DMA((6,)),
        ]

    ya, yb = call(
        pack_kernel, [HB] * 3, [shaped(YROWS, 128)] * 2, staging(16), "pack",
    )(*inputs)
    packed = ya
    ya = swap(ya, "gy", 0)
    yb = swap(yb, "gy", 1)
    *mid, xa, xb = call(
        start_kernel, [HB] * 3 + [VM], state + [shaped(21, NYL, 128)] * 2, staging(NYL), "start",
    )(*inputs, packed)
    xb = swap(xb, "gx", 1)
    xa = swap(xa, "gx", 0)
    *mid, xd, xc = call(
        edge_kernel, [VM] * 8, state + [shaped(21, 8, 128)] * 2,
        [pltpu.VMEM((21, NXL, 8, 128), F32)], "edge", {2 + i: i for i in range(6)}, cost=10 ** 10,
    )(ya, yb, *mid)
    xc = swap(xc, "gx", 1)
    xd = swap(xd, "gx", 0)
    out = call(
        last_kernel, [VM] * 10,
        [shaped(19, NXL, NYL, 128), shaped(NXL, NYL, 128)] + state[3:],
        [
            pltpu.VMEM((2, 21, EXT, 128), F32), pltpu.VMEM((19, NXL + 2, EXT, 128), F32),
            pltpu.VMEM((NXL + 2, EXT, 128), F32), pltpu.VMEM((19, NXL, NYL, 128), F32),
            pltpu.VMEM((NXL, NYL, 128), F32), pltpu.SemaphoreType.DMA((2 * NXL,)),
        ],
        "last", {3: 2, 4: 3, 5: 4}, out_specs=[HB] * 2 + [VM] * 3,
    )(*mid, xa, xb, xc, xd)
    return out[0], out[1]


def solution(mesh):
    in_specs = (P(None, "gx", "gy", None), P("gx", "gy", None), P("gx", "gy", None))
    out_specs = (P(None, "gx", "gy", None), P("gx", "gy", None))

    def run(populations, labels, solid_mask):
        new, phase = on_device(populations, labels, solid_mask)
        return new, phase

    return jax.shard_map(
        run, mesh=mesh, in_specs=in_specs, out_specs=out_specs, check_vma=False
    )
```

```python
import jax
import jax.numpy as jnp
import numpy as np
from jax import lax
from jax.experimental import pallas as pl
from jax.experimental.pallas import tpu as pltpu
from jax.sharding import PartitionSpec as P

VELOCITY_SET = [
    (0, 0, 0), (1, 0, 0), (-1, 0, 0), (0, 1, 0), (0, -1, 0), (0, 0, 1), (0, 0, -1),
    (1, 1, 0), (-1, -1, 0), (1, -1, 0), (-1, 1, 0), (1, 0, 1), (-1, 0, -1), (1, 0, -1),
    (-1, 0, 1), (0, 1, 1), (0, -1, -1), (0, 1, -1), (0, -1, 1),
]
DIRS = [
    (-1, 0, 0), (-1, 1, 0), (-1, -1, 0), (-1, 0, 1), (-1, 0, -1),
    (1, 0, 0), (1, 1, 0), (1, -1, 0), (1, 0, 1), (1, 0, -1),
    (0, 0, 0), (0, 1, 0), (0, -1, 0), (0, 0, 1), (0, 0, -1),
    (0, 1, 1), (0, -1, -1), (0, 1, -1), (0, -1, 1),
]
REF_OF = [VELOCITY_SET.index(d) for d in DIRS]
POS = {d: k for k, d in enumerate(DIRS)}
GROUPS = [(-1, 0), (-1, 1), (-1, -1), (1, 0), (1, 1), (1, -1), (0, 0), (0, 1), (0, -1)]
GPOS = {g: k for k, g in enumerate(GROUPS)}
NXL = 4
NYL = 32
EXT = 40
NT = 5
ROW0 = 8
SROWS = 56
YROWS = 256
W1 = 1.0 / 18.0
W2 = 1.0 / 36.0


def neg(d):
    return (-d[0], -d[1], -d[2])


def zroll(v, shift):
    if shift == 0:
        return v
    return pltpu.roll(v, shift % 128, 1)


def collide(f, known=None, equilibrium=True):
    def pair(a, b):
        pa, pb = f[a], f[b]
        if pb is None:
            return pa, pa
        if pa is None:
            return pb, -pb
        return pa + pb, pa - pb

    s1, d1 = pair((1, 1, 0), (-1, -1, 0))
    s2, d2 = pair((1, -1, 0), (-1, 1, 0))
    xxyy, xy, xyy, xxy = s1 + s2, s1 - s2, d1 + d2, d1 - d2
    s1, d1 = pair((1, 0, 1), (-1, 0, -1))
    s2, d2 = pair((1, 0, -1), (-1, 0, 1))
    xxzz, xz, xzz, xxz = s1 + s2, s1 - s2, d1 + d2, d1 - d2
    s1, d1 = pair((0, 1, 1), (0, -1, -1))
    s2, d2 = pair((0, 1, -1), (0, -1, 1))
    yyzz, yz, yzz, yyz = s1 + s2, s1 - s2, d1 + d2, d1 - d2
    ax, dx = pair((1, 0, 0), (-1, 0, 0))
    ay, dy = pair((0, 1, 0), (0, -1, 0))
    az, dz = pair((0, 0, 1), (0, 0, -1))
    jx = dx + (xyy + xzz)
    jy = dy + (xxy + yzz)
    jz = dz + (xxz + yyz)
    nxx = ax + (xxyy + xxzz)
    nyy = ay + (xxyy + yyzz)
    nzz = az + (xxzz + yyzz)
    rho = (f[(0, 0, 0)] + (ax + ay)) + (az + (xxyy + (xxzz + yyzz)))
    if known is not None:
        rho, jx, jy, jz = rho + known[0], jx + known[1], jy + known[2], jz + known[3]
    dxy, dxz, dyz = 0.3125 * xy, 0.3125 * xz, 0.3125 * yz
    dxyy, dxzz, dxxy = 0.3 * xyy, 0.3 * xzz, 0.3 * xxy
    dyzz, dxxz, dyyz = 0.3 * yzz, 0.3 * xxz, 0.3 * yyz
    dxxyy, dxxzz, dyyzz = 0.35 * xxyy, 0.35 * xxzz, 0.35 * yyzz
    if equilibrium:
        inv = 1.0 / rho
        ux, uy, uz = jx * inv, jy * inv, jz * inv
        qx, qy, qz = jx * ux, jy * uy, jz * uz
        third = rho * (1.0 / 3.0)
        nxx = nxx - (third + qx)
        nyy = nyy - (third + qy)
        nzz = nzz - (third + qz)
        dxy = 0.3125 * (xy - jx * uy)
        dxz = 0.3125 * (xz - jx * uz)
        dyz = 0.3125 * (yz - jy * uz)
        kx, ky, kz = jx * 0.1, jy * 0.1, jz * 0.1
        dxyy, dxzz = dxyy - kx, dxzz - kx
        dxxy, dyzz = dxxy - ky, dyzz - ky
        dxxz, dyyz = dxxz - kz, dyyz - kz
        base = (0.35 / 9.0) * rho + (0.35 / 3.0) * (qx + qy + qz)
        dxxyy = dxxyy - (base - 0.175 * qz)
        dxxzz = dxxzz - (base - 0.175 * qy)
        dyyzz = dyyzz - (base - 0.175 * qx)
    trace = nxx + nyy + nzz
    iso = trace * (-1.0 / 24.0)
    hxx = 0.625 * nxx + iso
    hyy = 0.625 * nyy + iso
    hzz = 0.625 * nzz + iso
    out = {}

    def less(d, v):
        return -v if f[d] is None else f[d] - v

    def diagonal(quad, cross, la, lb, da, db):
        t1, t2 = quad + cross, quad - cross
        v1, v2 = la + lb, la - lb
        out_dirs = []
        for sa, sb in ((1, 1), (-1, -1), (1, -1), (-1, 1)):
            e = tuple(sa * p + sb * q for p, q in zip(da, db))
            out_dirs.append(e)
        out[out_dirs[0]] = less(out_dirs[0], t1 + v1)
        out[out_dirs[1]] = less(out_dirs[1], t1 - v1)
        out[out_dirs[2]] = less(out_dirs[2], t2 + v2)
        out[out_dirs[3]] = less(out_dirs[3], t2 - v2)

    X, Y, Z = (1, 0, 0), (0, 1, 0), (0, 0, 1)
    diagonal(dxxyy, dxy, dxyy, dxxy, X, Y)
    diagonal(dxxzz, dxz, dxzz, dxxz, X, Z)
    diagonal(dyyzz, dyz, dyzz, dyyz, Y, Z)

    def axis(half, q1, q2, l1, l2, d):
        even = half - 2.0 * (q1 + q2)
        odd = 2.0 * (l1 + l2)
        out[d] = less(d, even - odd)
        out[neg(d)] = less(neg(d), even + odd)

    axis(hxx, dxxyy, dxxzz, dxyy, dxzz, X)
    axis(hyy, dxxyy, dyyzz, dxxy, dyzz, Y)
    axis(hzz, dxxzz, dyyzz, dxxz, dyyz, Z)
    out[(0, 0, 0)] = f[(0, 0, 0)] + trace - 4.0 * (dxxyy + dxxzz + dyyzz)
    return out, rho, (jx, jy, jz)


def gradient(ph, plane, row):
    def at(dx, dy):
        return ph[plane + dx, pl.ds(row + dy, 8), :]

    c = at(0, 0)
    xp, xm, yp, ym = at(1, 0), at(-1, 0), at(0, 1), at(0, -1)
    d1 = at(1, 1) - at(-1, -1)
    d2 = at(1, -1) - at(-1, 1)
    ex = xp - xm
    ey = yp - ym
    h = 2.0 * c + ((xp + xm) + (yp + ym))
    k = 1.0 / 12.0
    gx = k * ((2.0 * ex + (d1 + d2)) + (zroll(ex, 1) + zroll(ex, -1)))
    gy = k * ((2.0 * ey + (d1 - d2)) + (zroll(ey, 1) + zroll(ey, -1)))
    gz = k * (zroll(h, -1) - zroll(h, 1))
    return c, gx, gy, gz


def finish(dirs, s_of, ph, rho, fluid, plane, row, fp, red):
    p, gx, gy, gz = gradient(ph, plane + 1, row)
    g2 = gx * gx + gy * gy + gz * gz
    inv = lax.rsqrt(jnp.maximum(g2, 0.01)) * fluid
    h1 = (0.1 * W1) * inv
    h2 = (0.1 * W2) * inv
    cc = (0.175 * rho) * ((1.0 - p * p) * inv)
    c1 = W1 * cc
    c2 = W2 * cc
    frac = 0.5 + 0.5 * p
    comp = (gx, gy, gz)
    sums = {}
    cache = {}
    for d in dirs:
        moving = [k for k in range(3) if d[k] != 0]
        if not moving:
            q, c = h1 * (6.0 * g2), None
        else:
            sign = d[moving[0]]
            key = d if sign > 0 else neg(d)
            if key not in cache:
                if len(moving) == 1:
                    a = comp[moving[0]]
                    cache[key] = (h1 * (a * a - g2), c1 * a)
                else:
                    u, v = moving
                    a = comp[u] + comp[v] if key[v] > 0 else comp[u] - comp[v]
                    cache[key] = (h2 * (a * a - g2), c2 * a)
            q, c = cache[key]
        known = s_of(d)
        val = q if known is None else known + q
        fp[POS[d], plane, pl.ds(row, 8), :] = zroll(val, d[2])
        r = frac * val
        if c is not None:
            r = r + c if sign > 0 else r - c
        r = zroll(r, d[2])
        g = d[:2]
        sums[g] = r if g not in sums else sums[g] + r
    for g, r in sums.items():
        red[GPOS[g], plane, pl.ds(row, 8), :] = r


def arrived(d, fp, plane, row):
    return fp[POS[d], plane - d[0], pl.ds(row - d[1], 8), :]


def red_arrived(red, plane, row):
    total = None
    for g in GROUPS:
        v = red[GPOS[g], plane - g[0], pl.ds(row - g[1], 8), :]
        total = v if total is None else total + v
    return total


def tile_rows(t):
    return lax.broadcasted_iota(jnp.int32, (8, 128), 0) + (8 * t - 4)


def face(high):
    a = jnp.where(high, NXL - 1, 0)
    b = jnp.where(high, NXL - 2, 1)
    c = jnp.where(high, NXL - 3, 2)
    out = jnp.where(high, 5, 0)
    back = jnp.where(high, 0, 5)
    return a, b, c, out, back


def message_tile(high, row, s, rho, fl, ph, fp, red):
    a, b, c, out, back = face(high)
    gout = jnp.where(high, 3, 0)
    gback = jnp.where(high, 0, 3)
    rows = pl.ds(row - ROW0, 8)
    own = pl.ds(row, 8)

    def plain():
        v = [s[out + j, a, rows, :] for j in range(5)]
        return v, [rho[a, rows, :], ph[a + 2, own, :], ph[b + 2, own, :], fl[a, rows, :]]

    def moved():
        f = {}
        total = None
        for j in range(5):
            d = DIRS[5 + j]
            shifted = pl.ds(row - d[1], 8)
            f[d] = fp[out + j, b + 1, shifted, :]
            f[(-1, d[1], d[2])] = None
            v = fp[out + j, c + 1, shifted, :] + fp[back + j, a + 1, shifted, :]
            total = v if total is None else total + v
        for j in range(10, 19):
            shifted = pl.ds(row - DIRS[j][1], 8)
            f[DIRS[j]] = fp[j, a + 1, shifted, :]
            total = total + fp[j, b + 1, shifted, :]
        linear, dens, mom = collide(f, equilibrium=False)
        at_a, at_b = None, None
        for j in range(3):
            shifted = pl.ds(row - GROUPS[j][1], 8)
            v = red[gout + j, b + 1, shifted, :] + red[6 + j, a + 1, shifted, :]
            at_a = v if at_a is None else at_a + v
            v = (red[gout + j, c + 1, shifted, :] + red[gback + j, a + 1, shifted, :]) + red[
                6 + j, b + 1, shifted, :
            ]
            at_b = v if at_b is None else at_b + v
        return [linear[DIRS[5 + j]] for j in range(5)] + [dens, *mom], [at_a, total, at_b]

    return plain, moved


PLAIN = [0, 1, 2, 3, 4, 14, 15, 16, 17]
MOVED = [5, 6, 7, 8, 9, 10, 11, 12, 13, 18, 19, 20]


def main_message(msg, high, state):
    for n in range(NYL // 8):
        plain, moved = message_tile(high, ROW0 + 4 + 8 * n, *state)
        for kinds, part in ((PLAIN, plain()), (MOVED, moved())):
            for j, v in zip(kinds, part[0] + part[1]):
                msg[j, pl.ds(8 * n, 8), :] = v


def corner_message(msg, high, state):
    for n, (first, second) in enumerate(((0, 2), (EXT - 8, EXT - 6))):
        plain, _ = message_tile(high, ROW0 + first, *state)
        _, moved = message_tile(high, ROW0 + second, *state)
        for kinds, part, r in ((PLAIN, plain(), 4 * n), (MOVED, moved(), 0)):
            for j, v in zip(kinds, part[0] + part[1]):
                msg[j, pl.ds(4 * n, 4), :] = v[r:r + 4]


def inner_step(tiles, s, rho, fl, ph, fp, red):
    def plane(x, carry):
        for t in tiles:
            rows = pl.ds(8 * t, 8)
            finish(
                DIRS, lambda d: s[POS[d], x, rows, :], ph, rho[x, rows, :],
                fl[x, rows, :], x + 1, ROW0 + 8 * t, fp, red,
            )
        return carry

    lax.fori_loop(1, NXL - 1, plane, 0)
    for x, base in ((0, 5), (NXL - 1, 0)):
        for t in tiles:
            row = ROW0 + 8 * t
            frac = 0.5 + 0.5 * ph[x + 2, pl.ds(row, 8), :]
            sums = {}
            for d in DIRS[base:base + 5] + DIRS[10:]:
                v = s[POS[d], x, pl.ds(8 * t, 8), :]
                fp[POS[d], x + 1, pl.ds(row, 8), :] = zroll(v, d[2])
                r = zroll(frac * v, d[2])
                sums[d[:2]] = r if d[:2] not in sums else sums[d[:2]] + r
            for g, r in sums.items():
                red[GPOS[g], x + 1, pl.ds(row, 8), :] = r


def pack_kernel(pops_hbm, labels_hbm, solid_hbm, ya, yb, pops, labels, solid, sems):
    odd = lax.axis_index("gy") % 2
    copies = [
        pltpu.make_async_copy(labels_hbm, labels, sems.at[0]),
        pltpu.make_async_copy(solid_hbm, solid, sems.at[1]),
    ] + [
        pltpu.make_async_copy(pops_hbm.at[:, x], pops.at[:, x], sems.at[2 + x])
        for x in range(NXL)
    ]
    for c in copies:
        c.start()
    for c in copies:
        c.wait()

    def pack(out, high):
        three = pl.ds(NYL - 3 if high else 0, 3)
        four = pl.ds(NYL - 4 if high else 0, 4)
        for i in range(19):
            for x in range(NXL):
                out[pl.ds(i * 12 + x * 3, 3), :] = pops[i, x, three, :]
        for x in range(NXL):
            out[pl.ds(228 + x * 4, 4), :] = labels[x, four, :].astype(jnp.float32)
            out[pl.ds(244 + x * 3, 3), :] = solid[x, three, :].astype(jnp.float32)

    @pl.when(odd == 0)
    def _():
        pack(ya, True)
        pack(yb, False)

    @pl.when(odd == 1)
    def _():
        pack(ya, False)
        pack(yb, True)


def start_kernel(pops, labels, solid, s, rho, fl, ph, fp, red, xa, xb):
    gy = lax.axis_index("gy")
    low_edge = gy == 0
    high_edge = gy == lax.axis_size("gy") - 1

    def plane(x, carry):
        for t in range(NYL // 8):
            own = pl.ds(8 * t, 8)
            rows = pl.ds(8 * t + 4, 8)
            f = {d: pops[REF_OF[k], x, own, :] for k, d in enumerate(DIRS)}
            is_solid = solid[x, own, :] > 0
            y = lax.broadcasted_iota(jnp.int32, (8, 128), 0) + 8 * t
            if t == 0:
                is_solid = is_solid | ((y == 0) & low_edge)
            if t == NYL // 8 - 1:
                is_solid = is_solid | ((y == NYL - 1) & high_edge)
            relaxed, total, _ = collide(f)
            for d in DIRS:
                s[POS[d], x, rows, :] = jnp.where(is_solid, f[neg(d)], relaxed[d])
            rho[x, rows, :] = total
            fl[x, rows, :] = jnp.where(is_solid, 0.0, 1.0)
            ph[x + 2, pl.ds(ROW0 + 4 + 8 * t, 8), :] = jnp.where(labels[x, own, :] > 0, 1.0, -1.0)
        return carry

    lax.fori_loop(0, NXL, plane, 0)
    inner_step(range(NT), s, rho, fl, ph, fp, red)
    low_a = lax.axis_index("gx") % 2 == 1
    main_message(xb, low_a, (s, rho, fl, ph, fp, red))
    main_message(xa, jnp.logical_not(low_a), (s, rho, fl, ph, fp, red))


def edge_kernel(ya, yb, s_in, rho_in, fl_in, ph_in, fp_in, red_in,
                s, rho, fl, ph, fp, red, xd, xc, raw):
    gy = lax.axis_index("gy")
    odd = gy % 2
    low_edge = gy == 0
    high_edge = gy == lax.axis_size("gy") - 1

    def unpack(src, top):
        r = 1 if top else 4
        for x in range(NXL):
            for i in range(19):
                raw[i, x, pl.ds(r, 3), :] = src[pl.ds(i * 12 + x * 3, 3), :]
            raw[19, x, pl.ds(0 if top else 4, 4), :] = src[pl.ds(228 + x * 4, 4), :]
            raw[20, x, pl.ds(r, 3), :] = src[pl.ds(244 + x * 3, 3), :]

    @pl.when(odd == 0)
    def _():
        unpack(ya, False)
        unpack(yb, True)

    @pl.when(odd == 1)
    def _():
        unpack(ya, True)
        unpack(yb, False)

    row = lax.broadcasted_iota(jnp.int32, (8, 128), 0)
    inside = jnp.where(row < 4, jnp.where(low_edge, 0, 1), jnp.where(high_edge, 0, 1)) > 0

    def plane(x, carry):
        def put(ref, base, v):
            ref[pl.ds(base, 4), :] = v[0:4]
            ref[pl.ds(base + NYL + 4, 4), :] = v[4:8]

        f = {d: raw[REF_OF[k], x] for k, d in enumerate(DIRS)}
        is_solid = raw[20, x] > 0.5
        relaxed, total, _ = collide(f)
        for d in DIRS:
            v = jnp.where(is_solid, f[neg(d)], relaxed[d])
            put(s.at[POS[d], x], 0, jnp.where(inside, v, 0.0))
        put(rho.at[x], 0, total)
        put(fl.at[x], 0, jnp.where(inside & jnp.logical_not(is_solid), 1.0, 0.0))
        p = jnp.where(raw[19, x] > 0.5, 1.0, -1.0)
        put(ph.at[x + 2], ROW0, jnp.where(inside, p, 0.0))
        return carry

    lax.fori_loop(0, NXL, plane, 0)
    inner_step((0, NT - 1), s, rho, fl, ph, fp, red)
    low_a = lax.axis_index("gx") % 2 == 1
    corner_message(xc, low_a, (s, rho, fl, ph, fp, red))
    corner_message(xd, jnp.logical_not(low_a), (s, rho, fl, ph, fp, red))


def last_kernel(s, rho, fl, ph_in, fp_in, red_in, xb, xa, xc, xd,
                pops_hbm, phase_hbm, ph, fp, red, hx, s2, rho2, pops_out, phase_out, sems):
    gy = lax.axis_index("gy")
    low_edge = gy == 0
    high_edge = gy == lax.axis_size("gy") - 1
    side_a = 1 - lax.axis_index("gx") % 2

    def put(src, side, corner):
        near = jnp.where(side == 1, NXL + 2, 1)
        far = jnp.where(side == 1, NXL + 3, 0)
        for j in range(21):
            moved = 2 if corner and j in MOVED else 0
            if corner:
                spans = ((moved, 0, 4), (EXT - 4 - moved, 4, 4))
            else:
                spans = [(4 + 8 * n, 8 * n, 8) for n in range(NYL // 8)]
            for to, part, n in spans:
                v = src[j, pl.ds(part, n), :]
                if j in (15, 16):
                    ph[near if j == 15 else far, pl.ds(ROW0 + to, n), :] = v
                else:
                    hx[side, j, pl.ds(to, n), :] = v

    put(xa, side_a, False)
    put(xb, 1 - side_a, False)
    put(xd, side_a, True)
    put(xc, 1 - side_a, True)

    def mask(t):
        y = tile_rows(t)
        if t == 0:
            return (y >= 0) | jnp.logical_not(low_edge)
        if t == NT - 1:
            return (y < NYL) | jnp.logical_not(high_edge)
        return None

    sides = ((0, 0, DIRS[5:10], DIRS[0:5]), (1, NXL + 1, DIRS[0:5], DIRS[5:10]))

    for x in (0, NXL - 1):
        for t in range(NT):
            rows = pl.ds(8 * t, 8)
            finish(
                DIRS, lambda d: s[POS[d], x, rows, :], ph, rho[x, rows, :],
                fl[x, rows, :], x + 1, ROW0 + 8 * t, fp, red,
            )
    for side, plane_index, towards, back in sides:
        for t in range(NT):
            rows = pl.ds(8 * t, 8)

            def value(d):
                return hx[side, towards.index(d), rows, :] if d in towards else None

            finish(
                DIRS, value, ph, hx[side, 14, rows, :], hx[side, 17, rows, :],
                plane_index, ROW0 + 8 * t, fp, red,
            )

    def plane(x, carry):
        for t in range(NT):
            row = ROW0 + 8 * t
            rows = pl.ds(8 * t, 8)
            f = {d: arrived(d, fp, x + 1, row) for d in DIRS}
            relaxed, total, _ = collide(f)
            p = 2.0 * red_arrived(red, x + 1, row) / total - 1.0
            inside = mask(t)
            if inside is not None:
                p = jnp.where(inside, p, 0.0)
            is_fluid = fl[x, rows, :] > 0.5
            for d in DIRS:
                v = jnp.where(is_fluid, relaxed[d], f[neg(d)])
                if inside is not None:
                    v = jnp.where(inside, v, 0.0)
                s2[POS[d], x + 1, rows, :] = v
            rho2[x + 1, rows, :] = total
            ph[x + 2, pl.ds(row, 8), :] = p
        return carry

    lax.fori_loop(0, NXL, plane, 0)
    for side, index, towards, back in sides:
        near, far = (NXL + 2, NXL + 3) if side == 1 else (1, 0)
        for t in range(NT):
            row = ROW0 + 8 * t
            rows = pl.ds(8 * t, 8)
            f = {d: None if d in towards else arrived(d, fp, index, row) for d in DIRS}
            outwards = 1.0 if towards[0][0] > 0 else -1.0
            known = (
                hx[side, 10, rows, :], outwards * hx[side, 11, rows, :],
                hx[side, 12, rows, :], hx[side, 13, rows, :],
            )
            relaxed, total, _ = collide(f, known)
            rsum = hx[side, 18, rows, :]
            rfar = hx[side, 20, rows, :]
            for g in GROUPS:
                shifted = pl.ds(row - g[1], 8)
                if g[0] != towards[0][0]:
                    rsum = rsum + red[GPOS[g], index - g[0], shifted, :]
                if g[0] == back[0][0]:
                    rfar = rfar + red[GPOS[g], index, shifted, :]
            ffar = hx[side, 19, rows, :]
            for d in back:
                ffar = ffar + fp[POS[d], index, pl.ds(row - d[1], 8), :]
            p = 2.0 * rsum / total - 1.0
            pfar = 2.0 * rfar / ffar - 1.0
            inside = mask(t)
            if inside is not None:
                p = jnp.where(inside, p, 0.0)
                pfar = jnp.where(inside, pfar, 0.0)
            is_fluid = hx[side, 17, rows, :] > 0.5
            for j, d in enumerate(towards):
                v = jnp.where(is_fluid, relaxed[d] + hx[side, 5 + j, rows, :], f[neg(d)])
                if inside is not None:
                    v = jnp.where(inside, v, 0.0)
                s2[POS[d], index, rows, :] = v
            rho2[index, rows, :] = total
            ph[near, pl.ds(row, 8), :] = p
            ph[far, pl.ds(row, 8), :] = pfar

    def second(x, carry):
        for t in range(NT):
            rows = pl.ds(8 * t, 8)
            finish(
                DIRS, lambda d: s2[POS[d], x + 1, rows, :], ph, rho2[x + 1, rows, :],
                fl[x, rows, :], x + 1, ROW0 + 8 * t, fp, red,
            )
        return carry

    lax.fori_loop(0, NXL, second, 0)
    for side, index, towards, back in sides:
        for t in range(NT):
            rows = pl.ds(8 * t, 8)
            finish(
                towards, lambda d: s2[POS[d], index, rows, :], ph, rho2[index, rows, :],
                hx[side, 17, rows, :], index, ROW0 + 8 * t, fp, red,
            )

    def out_copies(x):
        return (
            pltpu.make_async_copy(pops_out.at[:, x], pops_hbm.at[:, x], sems.at[2 * x]),
            pltpu.make_async_copy(phase_out.at[x], phase_hbm.at[x], sems.at[2 * x + 1]),
        )

    def final(x, carry):
        for t in range(NYL // 8):
            row = ROW0 + 4 + 8 * t
            rows = pl.ds(8 * t, 8)
            total = None
            for d in DIRS:
                v = arrived(d, fp, x + 1, row)
                pops_out[REF_OF[POS[d]], x, rows, :] = v
                total = v if total is None else total + v
            phase_out[x, rows, :] = 2.0 * red_arrived(red, x + 1, row) / total - 1.0
        return carry

    for x in range(NXL):
        final(x, 0)
        for copy in out_copies(x):
            copy.start()
    for x in range(NXL):
        for copy in out_copies(x):
            copy.wait()


F32 = jnp.float32
VM = pl.BlockSpec(memory_space=pltpu.VMEM)
HB = pl.BlockSpec(memory_space=pltpu.HBM)
MIB = 1024 * 1024


def shaped(*dims):
    return jax.ShapeDtypeStruct(dims, F32)


def call(kernel, in_specs, outs, scratch, name, aliases=None, vmem=40, cost=0,
         out_specs=None):
    return pl.pallas_call(
        kernel,
        in_specs=in_specs,
        out_specs=out_specs or [VM] * len(outs),
        out_shape=outs,
        scratch_shapes=scratch,
        input_output_aliases=aliases or {},
        compiler_params=pltpu.CompilerParams(vmem_limit_bytes=vmem * MIB),
        cost_estimate=pl.CostEstimate(flops=cost, bytes_accessed=cost, transcendentals=0),
        name=name,
    )


def pairs(count, first):
    out = []
    for i in range(first, count + first, 2):
        a, b = i % count, (i + 1) % count
        out += [(a, b), (b, a)]
    return out


def swap(value, axis, first):
    return lax.ppermute(value, axis, pairs(lax.axis_size(axis), first))


def on_device(populations, labels, solid_mask):
    state = [
        shaped(19, NXL, EXT, 128), shaped(NXL, EXT, 128), shaped(NXL, EXT, 128),
        shaped(NXL + 4, SROWS, 128), shaped(19, NXL + 2, SROWS, 128),
        shaped(9, NXL + 2, SROWS, 128),
    ]
    inputs = [
        pltpu.with_memory_space_constraint(v, pltpu.HBM)
        for v in (populations, labels, solid_mask)
    ]

    whole = [
        shaped(19, NXL, NYL, 128), jax.ShapeDtypeStruct((NXL, NYL, 128), jnp.int32),
        jax.ShapeDtypeStruct((NXL, NYL, 128), jnp.int32),
    ]
    ya, yb, *held = call(
        pack_kernel, [HB] * 3, [shaped(YROWS, 128)] * 2 + whole,
        [pltpu.SemaphoreType.DMA((6,))], "pack",
    )(*inputs)
    ya = swap(ya, "gy", 0)
    yb = swap(yb, "gy", 1)
    *mid, xa, xb = call(
        start_kernel, [VM] * 3, state + [shaped(21, NYL, 128)] * 2, [], "start",
    )(*held)
    xb = swap(xb, "gx", 1)
    xa = swap(xa, "gx", 0)
    *mid, xd, xc = call(
        edge_kernel, [VM] * 8, state + [shaped(21, 8, 128)] * 2,
        [pltpu.VMEM((21, NXL, 8, 128), F32)], "edge", {2 + i: i for i in range(6)}, cost=10 ** 10,
    )(ya, yb, *mid)
    xc = swap(xc, "gx", 1)
    xd = swap(xd, "gx", 0)
    out = call(
        last_kernel, [VM] * 10,
        [shaped(19, NXL, NYL, 128), shaped(NXL, NYL, 128)] + state[3:],
        [
            pltpu.VMEM((2, 21, EXT, 128), F32), pltpu.VMEM((19, NXL + 2, EXT, 128), F32),
            pltpu.VMEM((NXL + 2, EXT, 128), F32), pltpu.VMEM((19, NXL, NYL, 128), F32),
            pltpu.VMEM((NXL, NYL, 128), F32), pltpu.SemaphoreType.DMA((2 * NXL,)),
        ],
        "last", {3: 2, 4: 3, 5: 4}, out_specs=[HB] * 2 + [VM] * 3,
    )(*mid, xb, xa, xc, xd)
    return out[0], out[1]


def solution(mesh):
    in_specs = (P(None, "gx", "gy", None), P("gx", "gy", None), P("gx", "gy", None))
    out_specs = (P(None, "gx", "gy", None), P("gx", "gy", None))

    def run(populations, labels, solid_mask):
        new, phase = on_device(populations, labels, solid_mask)
        return new, phase

    return jax.shard_map(
        run, mesh=mesh, in_specs=in_specs, out_specs=out_specs, check_vma=False
    )
```

```python
import jax
import jax.numpy as jnp
import numpy as np
from jax import lax
from jax.experimental import pallas as pl
from jax.experimental.pallas import tpu as pltpu
from jax.sharding import PartitionSpec as P

VELOCITY_SET = [
    (0, 0, 0), (1, 0, 0), (-1, 0, 0), (0, 1, 0), (0, -1, 0), (0, 0, 1), (0, 0, -1),
    (1, 1, 0), (-1, -1, 0), (1, -1, 0), (-1, 1, 0), (1, 0, 1), (-1, 0, -1), (1, 0, -1),
    (-1, 0, 1), (0, 1, 1), (0, -1, -1), (0, 1, -1), (0, -1, 1),
]
DIRS = [
    (-1, 0, 0), (-1, 1, 0), (-1, -1, 0), (-1, 0, 1), (-1, 0, -1),
    (1, 0, 0), (1, 1, 0), (1, -1, 0), (1, 0, 1), (1, 0, -1),
    (0, 0, 0), (0, 1, 0), (0, -1, 0), (0, 0, 1), (0, 0, -1),
    (0, 1, 1), (0, -1, -1), (0, 1, -1), (0, -1, 1),
]
REF_OF = [VELOCITY_SET.index(d) for d in DIRS]
POS = {d: k for k, d in enumerate(DIRS)}
GROUPS = [(-1, 0), (-1, 1), (-1, -1), (1, 0), (1, 1), (1, -1), (0, 0), (0, 1), (0, -1)]
GPOS = {g: k for k, g in enumerate(GROUPS)}
NXL = 4
NYL = 32
EXT = 40
NT = 5
ROW0 = 8
SROWS = 56
HALF = 11
YROWS = 256
W1 = 1.0 / 18.0
W2 = 1.0 / 36.0


def neg(d):
    return (-d[0], -d[1], -d[2])


def zroll(v, shift):
    if shift == 0:
        return v
    return pltpu.roll(v, shift % 128, 1)


def collide(f, known=None, equilibrium=True):
    def pair(a, b):
        pa, pb = f[a], f[b]
        if pb is None:
            return pa, pa
        if pa is None:
            return pb, -pb
        return pa + pb, pa - pb

    s1, d1 = pair((1, 1, 0), (-1, -1, 0))
    s2, d2 = pair((1, -1, 0), (-1, 1, 0))
    xxyy, xy, xyy, xxy = s1 + s2, s1 - s2, d1 + d2, d1 - d2
    s1, d1 = pair((1, 0, 1), (-1, 0, -1))
    s2, d2 = pair((1, 0, -1), (-1, 0, 1))
    xxzz, xz, xzz, xxz = s1 + s2, s1 - s2, d1 + d2, d1 - d2
    s1, d1 = pair((0, 1, 1), (0, -1, -1))
    s2, d2 = pair((0, 1, -1), (0, -1, 1))
    yyzz, yz, yzz, yyz = s1 + s2, s1 - s2, d1 + d2, d1 - d2
    ax, dx = pair((1, 0, 0), (-1, 0, 0))
    ay, dy = pair((0, 1, 0), (0, -1, 0))
    az, dz = pair((0, 0, 1), (0, 0, -1))
    jx = dx + (xyy + xzz)
    jy = dy + (xxy + yzz)
    jz = dz + (xxz + yyz)
    nxx = ax + (xxyy + xxzz)
    nyy = ay + (xxyy + yyzz)
    nzz = az + (xxzz + yyzz)
    rho = (f[(0, 0, 0)] + (ax + ay)) + (az + (xxyy + (xxzz + yyzz)))
    if known is not None:
        rho, jx, jy, jz = rho + known[0], jx + known[1], jy + known[2], jz + known[3]
    dxy, dxz, dyz = 0.3125 * xy, 0.3125 * xz, 0.3125 * yz
    dxyy, dxzz, dxxy = 0.3 * xyy, 0.3 * xzz, 0.3 * xxy
    dyzz, dxxz, dyyz = 0.3 * yzz, 0.3 * xxz, 0.3 * yyz
    dxxyy, dxxzz, dyyzz = 0.35 * xxyy, 0.35 * xxzz, 0.35 * yyzz
    if equilibrium:
        inv = 1.0 / rho
        ux, uy, uz = jx * inv, jy * inv, jz * inv
        qx, qy, qz = jx * ux, jy * uy, jz * uz
        third = rho * (1.0 / 3.0)
        nxx = nxx - (third + qx)
        nyy = nyy - (third + qy)
        nzz = nzz - (third + qz)
        dxy = 0.3125 * (xy - jx * uy)
        dxz = 0.3125 * (xz - jx * uz)
        dyz = 0.3125 * (yz - jy * uz)
        kx, ky, kz = jx * 0.1, jy * 0.1, jz * 0.1
        dxyy, dxzz = dxyy - kx, dxzz - kx
        dxxy, dyzz = dxxy - ky, dyzz - ky
        dxxz, dyyz = dxxz - kz, dyyz - kz
        base = (0.35 / 9.0) * rho + (0.35 / 3.0) * (qx + qy + qz)
        dxxyy = dxxyy - (base - 0.175 * qz)
        dxxzz = dxxzz - (base - 0.175 * qy)
        dyyzz = dyyzz - (base - 0.175 * qx)
    trace = nxx + nyy + nzz
    iso = trace * (-1.0 / 24.0)
    hxx = 0.625 * nxx + iso
    hyy = 0.625 * nyy + iso
    hzz = 0.625 * nzz + iso
    out = {}

    def less(d, v):
        return -v if f[d] is None else f[d] - v

    def diagonal(quad, cross, la, lb, da, db):
        t1, t2 = quad + cross, quad - cross
        v1, v2 = la + lb, la - lb
        out_dirs = []
        for sa, sb in ((1, 1), (-1, -1), (1, -1), (-1, 1)):
            e = tuple(sa * p + sb * q for p, q in zip(da, db))
            out_dirs.append(e)
        out[out_dirs[0]] = less(out_dirs[0], t1 + v1)
        out[out_dirs[1]] = less(out_dirs[1], t1 - v1)
        out[out_dirs[2]] = less(out_dirs[2], t2 + v2)
        out[out_dirs[3]] = less(out_dirs[3], t2 - v2)

    X, Y, Z = (1, 0, 0), (0, 1, 0), (0, 0, 1)
    diagonal(dxxyy, dxy, dxyy, dxxy, X, Y)
    diagonal(dxxzz, dxz, dxzz, dxxz, X, Z)
    diagonal(dyyzz, dyz, dyzz, dyyz, Y, Z)

    def axis(half, q1, q2, l1, l2, d):
        even = half - 2.0 * (q1 + q2)
        odd = 2.0 * (l1 + l2)
        out[d] = less(d, even - odd)
        out[neg(d)] = less(neg(d), even + odd)

    axis(hxx, dxxyy, dxxzz, dxyy, dxzz, X)
    axis(hyy, dxxyy, dyyzz, dxxy, dyzz, Y)
    axis(hzz, dxxzz, dyyzz, dxxz, dyyz, Z)
    out[(0, 0, 0)] = f[(0, 0, 0)] + trace - 4.0 * (dxxyy + dxxzz + dyyzz)
    return out, rho, (jx, jy, jz)


def gradient(ph, plane, row):
    def at(dx, dy):
        return ph[plane + dx, pl.ds(row + dy, 8), :]

    c = at(0, 0)
    xp, xm, yp, ym = at(1, 0), at(-1, 0), at(0, 1), at(0, -1)
    d1 = at(1, 1) - at(-1, -1)
    d2 = at(1, -1) - at(-1, 1)
    ex = xp - xm
    ey = yp - ym
    h = 2.0 * c + ((xp + xm) + (yp + ym))
    k = 1.0 / 12.0
    gx = k * ((2.0 * ex + (d1 + d2)) + (zroll(ex, 1) + zroll(ex, -1)))
    gy = k * ((2.0 * ey + (d1 - d2)) + (zroll(ey, 1) + zroll(ey, -1)))
    gz = k * (zroll(h, -1) - zroll(h, 1))
    return c, gx, gy, gz


def finish(dirs, s_of, ph, rho, fluid, plane, row, fp, red):
    p, gx, gy, gz = gradient(ph, plane + 1, row)
    g2 = gx * gx + gy * gy + gz * gz
    inv = lax.rsqrt(jnp.maximum(g2, 0.01)) * fluid
    h1 = (0.1 * W1) * inv
    h2 = (0.1 * W2) * inv
    cc = (0.175 * rho) * ((1.0 - p * p) * inv)
    c1 = W1 * cc
    c2 = W2 * cc
    frac = 0.5 + 0.5 * p
    comp = (gx, gy, gz)
    sums = {}
    cache = {}
    for d in dirs:
        moving = [k for k in range(3) if d[k] != 0]
        if not moving:
            q, c = h1 * (6.0 * g2), None
        else:
            sign = d[moving[0]]
            key = d if sign > 0 else neg(d)
            if key not in cache:
                if len(moving) == 1:
                    a = comp[moving[0]]
                    cache[key] = (h1 * (a * a - g2), c1 * a)
                else:
                    u, v = moving
                    a = comp[u] + comp[v] if key[v] > 0 else comp[u] - comp[v]
                    cache[key] = (h2 * (a * a - g2), c2 * a)
            q, c = cache[key]
        known = s_of(d)
        val = q if known is None else known + q
        fp[POS[d], plane, pl.ds(row, 8), :] = zroll(val, d[2])
        r = frac * val
        if c is not None:
            r = r + c if sign > 0 else r - c
        r = zroll(r, d[2])
        g = d[:2]
        sums[g] = r if g not in sums else sums[g] + r
    for g, r in sums.items():
        red[GPOS[g], plane, pl.ds(row, 8), :] = r


def arrived(d, fp, plane, row):
    return fp[POS[d], plane - d[0], pl.ds(row - d[1], 8), :]


def red_arrived(red, plane, row):
    total = None
    for g in GROUPS:
        v = red[GPOS[g], plane - g[0], pl.ds(row - g[1], 8), :]
        total = v if total is None else total + v
    return total


def tile_rows(t):
    return lax.broadcasted_iota(jnp.int32, (8, 128), 0) + (8 * t - 4)


def face(high):
    a = jnp.where(high, NXL - 1, 0)
    b = jnp.where(high, NXL - 2, 1)
    c = jnp.where(high, NXL - 3, 2)
    out = jnp.where(high, 5, 0)
    back = jnp.where(high, 0, 5)
    return a, b, c, out, back


def message_tile(high, row, s, rho, fl, ph, fp, red):
    a, b, c, out, back = face(high)
    gout = jnp.where(high, 3, 0)
    gback = jnp.where(high, 0, 3)
    rows = pl.ds(row - ROW0, 8)
    own = pl.ds(row, 8)

    def plain():
        v = [s[out + j, a, rows, :] for j in range(5)]
        return v, [rho[a, rows, :], ph[a + 2, own, :], ph[b + 2, own, :], fl[a, rows, :]]

    def moved():
        f = {}
        total = None
        for j in range(5):
            d = DIRS[5 + j]
            shifted = pl.ds(row - d[1], 8)
            f[d] = fp[out + j, b + 1, shifted, :]
            f[(-1, d[1], d[2])] = None
            v = fp[out + j, c + 1, shifted, :] + fp[back + j, a + 1, shifted, :]
            total = v if total is None else total + v
        for j in range(10, 19):
            shifted = pl.ds(row - DIRS[j][1], 8)
            f[DIRS[j]] = fp[j, a + 1, shifted, :]
            total = total + fp[j, b + 1, shifted, :]
        linear, dens, mom = collide(f, equilibrium=False)
        at_a, at_b = None, None
        for j in range(3):
            shifted = pl.ds(row - GROUPS[j][1], 8)
            v = red[gout + j, b + 1, shifted, :] + red[6 + j, a + 1, shifted, :]
            at_a = v if at_a is None else at_a + v
            v = (red[gout + j, c + 1, shifted, :] + red[gback + j, a + 1, shifted, :]) + red[
                6 + j, b + 1, shifted, :
            ]
            at_b = v if at_b is None else at_b + v
        return [linear[DIRS[5 + j]] for j in range(5)] + [dens, *mom], [at_a, total, at_b]

    return plain, moved


PLAIN = [0, 1, 2, 3, 4, 14, 15, 16, 17]
MOVED = [5, 6, 7, 8, 9, 10, 11, 12, 13, 18, 19, 20]


def plane_of(msg, j):
    if not isinstance(msg, tuple):
        return msg.at[j]
    return msg[0].at[j] if j < HALF else msg[1].at[j - HALF]


def main_message(msg, high, state):
    for n in range(NYL // 8):
        plain, moved = message_tile(high, ROW0 + 4 + 8 * n, *state)
        for kinds, part in ((PLAIN, plain()), (MOVED, moved())):
            for j, v in zip(kinds, part[0] + part[1]):
                plane_of(msg, j)[pl.ds(8 * n, 8), :] = v


def corner_message(msg, base, high, state):
    for n, (first, second) in enumerate(((0, 2), (EXT - 8, EXT - 6))):
        plain, _ = message_tile(high, ROW0 + first, *state)
        _, moved = message_tile(high, ROW0 + second, *state)
        for kinds, part, r in ((PLAIN, plain(), 4 * n), (MOVED, moved(), 0)):
            for j, v in zip(kinds, part[0] + part[1]):
                plane_of(msg, j)[pl.ds(base + 4 * n, 4), :] = v[r:r + 4]


def inner_step(tiles, s, rho, fl, ph, fp, red):
    def plane(x, carry):
        for t in tiles:
            rows = pl.ds(8 * t, 8)
            finish(
                DIRS, lambda d: s[POS[d], x, rows, :], ph, rho[x, rows, :],
                fl[x, rows, :], x + 1, ROW0 + 8 * t, fp, red,
            )
        return carry

    lax.fori_loop(1, NXL - 1, plane, 0)
    for x, base in ((0, 5), (NXL - 1, 0)):
        for t in tiles:
            row = ROW0 + 8 * t
            frac = 0.5 + 0.5 * ph[x + 2, pl.ds(row, 8), :]
            sums = {}
            for d in DIRS[base:base + 5] + DIRS[10:]:
                v = s[POS[d], x, pl.ds(8 * t, 8), :]
                fp[POS[d], x + 1, pl.ds(row, 8), :] = zroll(v, d[2])
                r = zroll(frac * v, d[2])
                sums[d[:2]] = r if d[:2] not in sums else sums[d[:2]] + r
            for g, r in sums.items():
                red[GPOS[g], x + 1, pl.ds(row, 8), :] = r


def pack_kernel(pops_hbm, labels_hbm, solid_hbm, ya, yb, pops, labels, solid, sems):
    odd = lax.axis_index("gy") % 2
    copies = [
        pltpu.make_async_copy(labels_hbm, labels, sems.at[0]),
        pltpu.make_async_copy(solid_hbm, solid, sems.at[1]),
    ] + [
        pltpu.make_async_copy(pops_hbm.at[:, x], pops.at[:, x], sems.at[2 + x])
        for x in range(NXL)
    ]
    for c in copies:
        c.start()
    for c in copies:
        c.wait()

    def pack(out, high):
        three = pl.ds(NYL - 3 if high else 0, 3)
        four = pl.ds(NYL - 4 if high else 0, 4)
        for i in range(19):
            for x in range(NXL):
                out[pl.ds(i * 12 + x * 3, 3), :] = pops[i, x, three, :]
        for x in range(NXL):
            out[pl.ds(228 + x * 4, 4), :] = labels[x, four, :].astype(jnp.float32)
            out[pl.ds(244 + x * 3, 3), :] = solid[x, three, :].astype(jnp.float32)

    @pl.when(odd == 0)
    def _():
        pack(ya, True)
        pack(yb, False)

    @pl.when(odd == 1)
    def _():
        pack(ya, False)
        pack(yb, True)


def start_kernel(pops, labels, solid, s, rho, fl, ph, fp, red, xa, xd, xb):
    gy = lax.axis_index("gy")
    low_edge = gy == 0
    high_edge = gy == lax.axis_size("gy") - 1

    def plane(x, carry):
        for t in range(NYL // 8):
            own = pl.ds(8 * t, 8)
            rows = pl.ds(8 * t + 4, 8)
            f = {d: pops[REF_OF[k], x, own, :] for k, d in enumerate(DIRS)}
            is_solid = solid[x, own, :] > 0
            y = lax.broadcasted_iota(jnp.int32, (8, 128), 0) + 8 * t
            if t == 0:
                is_solid = is_solid | ((y == 0) & low_edge)
            if t == NYL // 8 - 1:
                is_solid = is_solid | ((y == NYL - 1) & high_edge)
            relaxed, total, _ = collide(f)
            for d in DIRS:
                s[POS[d], x, rows, :] = jnp.where(is_solid, f[neg(d)], relaxed[d])
            rho[x, rows, :] = total
            fl[x, rows, :] = jnp.where(is_solid, 0.0, 1.0)
            ph[x + 2, pl.ds(ROW0 + 4 + 8 * t, 8), :] = jnp.where(labels[x, own, :] > 0, 1.0, -1.0)
        return carry

    lax.fori_loop(0, NXL, plane, 0)
    inner_step(range(NT), s, rho, fl, ph, fp, red)
    low_a = lax.axis_index("gx") % 2 == 1
    main_message(xb, low_a, (s, rho, fl, ph, fp, red))
    main_message((xa, xd), jnp.logical_not(low_a), (s, rho, fl, ph, fp, red))


def edge_kernel(ya, yb, s_in, rho_in, fl_in, ph_in, fp_in, red_in, xa_in, xd_in,
                s, rho, fl, ph, fp, red, xa, xd, xc, raw):
    gy = lax.axis_index("gy")
    odd = gy % 2
    low_edge = gy == 0
    high_edge = gy == lax.axis_size("gy") - 1

    def unpack(src, top):
        r = 1 if top else 4
        for x in range(NXL):
            for i in range(19):
                raw[i, x, pl.ds(r, 3), :] = src[pl.ds(i * 12 + x * 3, 3), :]
            raw[19, x, pl.ds(0 if top else 4, 4), :] = src[pl.ds(228 + x * 4, 4), :]
            raw[20, x, pl.ds(r, 3), :] = src[pl.ds(244 + x * 3, 3), :]

    @pl.when(odd == 0)
    def _():
        unpack(ya, False)
        unpack(yb, True)

    @pl.when(odd == 1)
    def _():
        unpack(ya, True)
        unpack(yb, False)

    row = lax.broadcasted_iota(jnp.int32, (8, 128), 0)
    inside = jnp.where(row < 4, jnp.where(low_edge, 0, 1), jnp.where(high_edge, 0, 1)) > 0

    def plane(x, carry):
        def put(ref, base, v):
            ref[pl.ds(base, 4), :] = v[0:4]
            ref[pl.ds(base + NYL + 4, 4), :] = v[4:8]

        f = {d: raw[REF_OF[k], x] for k, d in enumerate(DIRS)}
        is_solid = raw[20, x] > 0.5
        relaxed, total, _ = collide(f)
        for d in DIRS:
            v = jnp.where(is_solid, f[neg(d)], relaxed[d])
            put(s.at[POS[d], x], 0, jnp.where(inside, v, 0.0))
        put(rho.at[x], 0, total)
        put(fl.at[x], 0, jnp.where(inside & jnp.logical_not(is_solid), 1.0, 0.0))
        p = jnp.where(raw[19, x] > 0.5, 1.0, -1.0)
        put(ph.at[x + 2], ROW0, jnp.where(inside, p, 0.0))
        return carry

    lax.fori_loop(0, NXL, plane, 0)
    inner_step((0, NT - 1), s, rho, fl, ph, fp, red)
    low_a = lax.axis_index("gx") % 2 == 1
    corner_message(xc, 0, low_a, (s, rho, fl, ph, fp, red))
    corner_message((xa, xd), NYL, jnp.logical_not(low_a), (s, rho, fl, ph, fp, red))


def edges():
    gy = lax.axis_index("gy")
    low_edge = gy == 0
    high_edge = gy == lax.axis_size("gy") - 1

    def mask(t):
        y = tile_rows(t)
        if t == 0:
            return (y >= 0) | jnp.logical_not(low_edge)
        if t == NT - 1:
            return (y < NYL) | jnp.logical_not(high_edge)
        return None

    return mask


def put_message(src, base, side, corner, hx, ph):
    near = jnp.where(side == 1, NXL + 2, 1)
    far = jnp.where(side == 1, NXL + 3, 0)
    for j in range(21):
        moved = 2 if corner and j in MOVED else 0
        if corner:
            spans = ((moved, 0, 4), (EXT - 4 - moved, 4, 4))
        else:
            spans = [(4 + 8 * n, 8 * n, 8) for n in range(NYL // 8)]
        for to, part, n in spans:
            v = plane_of(src, j)[pl.ds(base + part, n), :]
            if j in (15, 16):
                ph[near if j == 15 else far, pl.ds(ROW0 + to, n), :] = v
            else:
                hx[j, pl.ds(to, n), :] = v


def by_side(side, step):
    for k in (0, 1):
        pl.when(side == k)(lambda: step(k))


def side_dirs(side):
    if side == 0:
        return 0, DIRS[5:10], DIRS[0:5]
    return NXL + 1, DIRS[0:5], DIRS[5:10]


def halo_first(side, hx, ph, fp, red):
    index, towards, _ = side_dirs(side)
    for t in range(NT):
        rows = pl.ds(8 * t, 8)
        finish(
            DIRS, lambda d: hx[towards.index(d), rows, :] if d in towards else None, ph,
            hx[14, rows, :], hx[17, rows, :], index, ROW0 + 8 * t, fp, red,
        )


def halo_collide(side, hx, fp, red, ph, s2, rho2):
    mask = edges()
    index, towards, back = side_dirs(side)
    near, far = (NXL + 2, NXL + 3) if side == 1 else (1, 0)
    outwards = 1.0 if side == 0 else -1.0
    for t in range(NT):
        row = ROW0 + 8 * t
        rows = pl.ds(8 * t, 8)
        f = {d: None if d in towards else arrived(d, fp, index, row) for d in DIRS}
        known = (
            hx[10, rows, :], outwards * hx[11, rows, :], hx[12, rows, :], hx[13, rows, :],
        )
        relaxed, total, _ = collide(f, known)
        rsum = hx[18, rows, :]
        rfar = hx[20, rows, :]
        for g in GROUPS:
            shifted = pl.ds(row - g[1], 8)
            if g[0] != towards[0][0]:
                rsum = rsum + red[GPOS[g], index - g[0], shifted, :]
            if g[0] == back[0][0]:
                rfar = rfar + red[GPOS[g], index, shifted, :]
        ffar = hx[19, rows, :]
        for d in back:
            ffar = ffar + fp[POS[d], index, pl.ds(row - d[1], 8), :]
        p = 2.0 * rsum / total - 1.0
        pfar = 2.0 * rfar / ffar - 1.0
        inside = mask(t)
        if inside is not None:
            p = jnp.where(inside, p, 0.0)
            pfar = jnp.where(inside, pfar, 0.0)
        is_fluid = hx[17, rows, :] > 0.5
        for j, d in enumerate(towards):
            v = jnp.where(is_fluid, relaxed[d] + hx[5 + j, rows, :], f[neg(d)])
            if inside is not None:
                v = jnp.where(inside, v, 0.0)
            s2[POS[d], index, rows, :] = v
        rho2[index, rows, :] = total
        ph[near, pl.ds(row, 8), :] = p
        ph[far, pl.ds(row, 8), :] = pfar


def halo_second(side, hx, s2, rho2, ph, fp, red):
    index, towards, _ = side_dirs(side)
    for t in range(NT):
        rows = pl.ds(8 * t, 8)
        finish(
            towards, lambda d: s2[POS[d], index, rows, :], ph, rho2[index, rows, :],
            hx[17, rows, :], index, ROW0 + 8 * t, fp, red,
        )


def own_finish(x, s, k, rho, fl, ph, fp, red):
    for t in range(NT):
        rows = pl.ds(8 * t, 8)
        finish(
            DIRS, lambda d: s[POS[d], k, rows, :], ph, rho[k, rows, :], fl[x, rows, :],
            x + 1, ROW0 + 8 * t, fp, red,
        )


def own_collide(x, k, fl, fp, red, ph, s2, rho2):
    mask = edges()
    for t in range(NT):
        row = ROW0 + 8 * t
        rows = pl.ds(8 * t, 8)
        f = {d: arrived(d, fp, x + 1, row) for d in DIRS}
        relaxed, total, _ = collide(f)
        p = 2.0 * red_arrived(red, x + 1, row) / total - 1.0
        inside = mask(t)
        if inside is not None:
            p = jnp.where(inside, p, 0.0)
        is_fluid = fl[x, rows, :] > 0.5
        for d in DIRS:
            v = jnp.where(is_fluid, relaxed[d], f[neg(d)])
            if inside is not None:
                v = jnp.where(inside, v, 0.0)
            s2[POS[d], k, rows, :] = v
        rho2[k, rows, :] = total
        ph[x + 2, pl.ds(row, 8), :] = p


def two_planes(side, step):
    def body(k, carry):
        step(jnp.where(side == 1, NXL - 1 - k, k), k)
        return carry

    lax.fori_loop(0, 2, body, 0)


def near_kernel(s, rho, fl, ph_in, fp_in, red_in, xa, xd,
                fp, red, fp2, red2, ph2, s2_next, rho2_next, ph, hx, s2, rho2, own2, orho2):
    side = 1 - lax.axis_index("gx") % 2
    ph[...] = ph_in[...]
    put_message((xa, xd), 0, side, False, hx, ph)
    put_message((xa, xd), NYL, side, True, hx, ph)
    first = jnp.where(side == 1, NXL - 1, 0)
    own_finish(first, s, first, rho, fl, ph, fp, red)
    by_side(side, lambda k: halo_first(k, hx, ph, fp, red))
    two_planes(side, lambda x, k: own_collide(x, k, fl, fp, red, ph2, own2, orho2))
    by_side(side, lambda k: halo_collide(k, hx, fp, red, ph2, s2, rho2))
    own_finish(first, own2, 0, orho2, fl, ph2, fp2, red2)
    by_side(side, lambda k: halo_second(k, hx, s2, rho2, ph2, fp2, red2))
    s2_next[...] = own2[:, 1]
    rho2_next[...] = orho2[1]


def far_kernel(s, rho, fl, ph_in, fp_in, red_in, fp2_in, red2_in, ph2_in, s2_next, rho2_next,
               xb, xc, pops_hbm, phase_hbm, fp, red, fp2, red2,
               ph, ph2, hx, s2, rho2, own2, orho2, pops_out, phase_out, sems):
    side = lax.axis_index("gx") % 2
    ph[...] = ph_in[...]
    ph2[...] = ph2_in[...]
    put_message(xb, 0, side, False, hx, ph)
    put_message(xc, 0, side, True, hx, ph)
    first = jnp.where(side == 1, NXL - 1, 0)
    own_finish(first, s, first, rho, fl, ph, fp, red)
    by_side(side, lambda k: halo_first(k, hx, ph, fp, red))
    two_planes(side, lambda x, k: own_collide(x, k, fl, fp, red, ph2, own2, orho2))
    by_side(side, lambda k: halo_collide(k, hx, fp, red, ph2, s2, rho2))
    own2[:, 2] = s2_next[...]
    orho2[2] = rho2_next[...]

    def second(k, carry):
        own_finish(
            jnp.where(side == 1, NXL - 1 - k, k), own2, k, orho2, fl, ph2, fp2, red2
        )
        return carry

    lax.fori_loop(0, 3, second, 0)
    by_side(side, lambda k: halo_second(k, hx, s2, rho2, ph2, fp2, red2))

    def out_copies(x):
        return (
            pltpu.make_async_copy(pops_out.at[:, x], pops_hbm.at[:, x], sems.at[2 * x]),
            pltpu.make_async_copy(phase_out.at[x], phase_hbm.at[x], sems.at[2 * x + 1]),
        )

    for x in range(NXL):
        for t in range(NYL // 8):
            row = ROW0 + 4 + 8 * t
            rows = pl.ds(8 * t, 8)
            total = None
            for d in DIRS:
                v = arrived(d, fp2, x + 1, row)
                pops_out[REF_OF[POS[d]], x, rows, :] = v
                total = v if total is None else total + v
            phase_out[x, rows, :] = 2.0 * red_arrived(red2, x + 1, row) / total - 1.0
        for copy in out_copies(x):
            copy.start()
    for x in range(NXL):
        for copy in out_copies(x):
            copy.wait()


F32 = jnp.float32
VM = pl.BlockSpec(memory_space=pltpu.VMEM)
HB = pl.BlockSpec(memory_space=pltpu.HBM)
MIB = 1024 * 1024


def shaped(*dims):
    return jax.ShapeDtypeStruct(dims, F32)


def call(kernel, in_specs, outs, scratch, name, aliases=None, vmem=40, cost=0,
         out_specs=None):
    return pl.pallas_call(
        kernel,
        in_specs=in_specs,
        out_specs=out_specs or [VM] * len(outs),
        out_shape=outs,
        scratch_shapes=scratch,
        input_output_aliases=aliases or {},
        compiler_params=pltpu.CompilerParams(vmem_limit_bytes=vmem * MIB),
        cost_estimate=pl.CostEstimate(flops=cost, bytes_accessed=cost, transcendentals=0),
        name=name,
    )


def pairs(count, first):
    out = []
    for i in range(first, count + first, 2):
        a, b = i % count, (i + 1) % count
        out += [(a, b), (b, a)]
    return out


def swap(value, axis, first):
    return lax.ppermute(value, axis, pairs(lax.axis_size(axis), first))


def on_device(populations, labels, solid_mask):
    state = [
        shaped(19, NXL, EXT, 128), shaped(NXL, EXT, 128), shaped(NXL, EXT, 128),
        shaped(NXL + 4, SROWS, 128), shaped(19, NXL + 2, SROWS, 128),
        shaped(9, NXL + 2, SROWS, 128),
    ]
    inputs = [
        pltpu.with_memory_space_constraint(v, pltpu.HBM)
        for v in (populations, labels, solid_mask)
    ]

    split = [shaped(HALF, EXT, 128), shaped(21 - HALF, EXT, 128)]
    whole = [
        shaped(19, NXL, NYL, 128), jax.ShapeDtypeStruct((NXL, NYL, 128), jnp.int32),
        jax.ShapeDtypeStruct((NXL, NYL, 128), jnp.int32),
    ]
    ya, yb, *held = call(
        pack_kernel, [HB] * 3, [shaped(YROWS, 128)] * 2 + whole,
        [pltpu.SemaphoreType.DMA((6,))], "pack",
    )(*inputs)
    ya = swap(ya, "gy", 0)
    yb = swap(yb, "gy", 1)
    *mid, xa, xd, xb = call(
        start_kernel, [VM] * 3, state + split + [shaped(21, NYL, 128)], [], "start",
    )(*held)
    xb = swap(xb, "gx", 1)
    *mid, xa, xd, xc = call(
        edge_kernel, [VM] * 10, state + split + [shaped(21, 8, 128)],
        [pltpu.VMEM((21, NXL, 8, 128), F32)], "edge", {2 + i: i for i in range(8)},
        cost=10 ** 10,
    )(ya, yb, *mid, xa, xd)
    xc = swap(xc, "gx", 1)
    xa = swap(xa, "gx", 0)
    xd = swap(xd, "gx", 0)
    s, rho, fl, ph, fp, red = mid
    halo = [
        pltpu.VMEM((21, EXT, 128), F32), pltpu.VMEM((19, NXL + 2, EXT, 128), F32),
        pltpu.VMEM((NXL + 2, EXT, 128), F32), pltpu.VMEM((19, 3, EXT, 128), F32),
        pltpu.VMEM((3, EXT, 128), F32),
    ]
    phases = pltpu.VMEM((NXL + 4, SROWS, 128), F32)
    fp, red, fp2, red2, ph2, s2_next, rho2_next = call(
        near_kernel, [VM] * 8,
        [state[4], state[5], state[4], state[5], state[3], shaped(19, EXT, 128),
         shaped(EXT, 128)],
        [phases] + halo, "near", {4: 0, 5: 1}, cost=0,
    )(s, rho, fl, ph, fp, red, xa, xd)
    out = call(
        far_kernel, [VM] * 13,
        [shaped(19, NXL, NYL, 128), shaped(NXL, NYL, 128), state[4], state[5], state[4],
         state[5]],
        [phases, phases] + halo + [
            pltpu.VMEM((19, NXL, NYL, 128), F32), pltpu.VMEM((NXL, NYL, 128), F32),
            pltpu.SemaphoreType.DMA((2 * NXL,)),
        ],
        "far", {4: 2, 5: 3, 6: 4, 7: 5}, out_specs=[HB] * 2 + [VM] * 4,
    )(s, rho, fl, ph, fp, red, fp2, red2, ph2, s2_next, rho2_next, xb, xc)
    return out[0], out[1]


def solution(mesh):
    in_specs = (P(None, "gx", "gy", None), P("gx", "gy", None), P("gx", "gy", None))
    out_specs = (P(None, "gx", "gy", None), P("gx", "gy", None))

    def run(populations, labels, solid_mask):
        new, phase = on_device(populations, labels, solid_mask)
        return new, phase

    return jax.shard_map(
        run, mesh=mesh, in_specs=in_specs, out_specs=out_specs, check_vma=False
    )
```

```python
import jax
import jax.numpy as jnp
import numpy as np
from jax import lax
from jax.experimental import pallas as pl
from jax.experimental.pallas import tpu as pltpu
from jax.sharding import PartitionSpec as P

VELOCITY_SET = [
    (0, 0, 0), (1, 0, 0), (-1, 0, 0), (0, 1, 0), (0, -1, 0), (0, 0, 1), (0, 0, -1),
    (1, 1, 0), (-1, -1, 0), (1, -1, 0), (-1, 1, 0), (1, 0, 1), (-1, 0, -1), (1, 0, -1),
    (-1, 0, 1), (0, 1, 1), (0, -1, -1), (0, 1, -1), (0, -1, 1),
]
DIRS = [
    (-1, 0, 0), (-1, 1, 0), (-1, -1, 0), (-1, 0, 1), (-1, 0, -1),
    (1, 0, 0), (1, 1, 0), (1, -1, 0), (1, 0, 1), (1, 0, -1),
    (0, 0, 0), (0, 1, 0), (0, -1, 0), (0, 0, 1), (0, 0, -1),
    (0, 1, 1), (0, -1, -1), (0, 1, -1), (0, -1, 1),
]
REF_OF = [VELOCITY_SET.index(d) for d in DIRS]
POS = {d: k for k, d in enumerate(DIRS)}
GROUPS = [(-1, 0), (-1, 1), (-1, -1), (1, 0), (1, 1), (1, -1), (0, 0), (0, 1), (0, -1)]
GPOS = {g: k for k, g in enumerate(GROUPS)}
NXL = 4
NYL = 32
EXT = 40
NT = 5
ROW0 = 8
SROWS = 56
HALF = 11
YROWS = 256
W1 = 1.0 / 18.0
W2 = 1.0 / 36.0


def neg(d):
    return (-d[0], -d[1], -d[2])


def zroll(v, shift):
    if shift == 0:
        return v
    return pltpu.roll(v, shift % 128, 1)


def collide(f, known=None, equilibrium=True):
    def pair(a, b):
        pa, pb = f[a], f[b]
        if pb is None:
            return pa, pa
        if pa is None:
            return pb, -pb
        return pa + pb, pa - pb

    s1, d1 = pair((1, 1, 0), (-1, -1, 0))
    s2, d2 = pair((1, -1, 0), (-1, 1, 0))
    xxyy, xy, xyy, xxy = s1 + s2, s1 - s2, d1 + d2, d1 - d2
    s1, d1 = pair((1, 0, 1), (-1, 0, -1))
    s2, d2 = pair((1, 0, -1), (-1, 0, 1))
    xxzz, xz, xzz, xxz = s1 + s2, s1 - s2, d1 + d2, d1 - d2
    s1, d1 = pair((0, 1, 1), (0, -1, -1))
    s2, d2 = pair((0, 1, -1), (0, -1, 1))
    yyzz, yz, yzz, yyz = s1 + s2, s1 - s2, d1 + d2, d1 - d2
    ax, dx = pair((1, 0, 0), (-1, 0, 0))
    ay, dy = pair((0, 1, 0), (0, -1, 0))
    az, dz = pair((0, 0, 1), (0, 0, -1))
    jx = dx + (xyy + xzz)
    jy = dy + (xxy + yzz)
    jz = dz + (xxz + yyz)
    nxx = ax + (xxyy + xxzz)
    nyy = ay + (xxyy + yyzz)
    nzz = az + (xxzz + yyzz)
    rho = (f[(0, 0, 0)] + (ax + ay)) + (az + (xxyy + (xxzz + yyzz)))
    if known is not None:
        rho, jx, jy, jz = rho + known[0], jx + known[1], jy + known[2], jz + known[3]
    dxy, dxz, dyz = 0.3125 * xy, 0.3125 * xz, 0.3125 * yz
    dxyy, dxzz, dxxy = 0.3 * xyy, 0.3 * xzz, 0.3 * xxy
    dyzz, dxxz, dyyz = 0.3 * yzz, 0.3 * xxz, 0.3 * yyz
    dxxyy, dxxzz, dyyzz = 0.35 * xxyy, 0.35 * xxzz, 0.35 * yyzz
    if equilibrium:
        inv = 1.0 / rho
        ux, uy, uz = jx * inv, jy * inv, jz * inv
        qx, qy, qz = jx * ux, jy * uy, jz * uz
        third = rho * (1.0 / 3.0)
        nxx = nxx - (third + qx)
        nyy = nyy - (third + qy)
        nzz = nzz - (third + qz)
        dxy = 0.3125 * (xy - jx * uy)
        dxz = 0.3125 * (xz - jx * uz)
        dyz = 0.3125 * (yz - jy * uz)
        kx, ky, kz = jx * 0.1, jy * 0.1, jz * 0.1
        dxyy, dxzz = dxyy - kx, dxzz - kx
        dxxy, dyzz = dxxy - ky, dyzz - ky
        dxxz, dyyz = dxxz - kz, dyyz - kz
        base = (0.35 / 9.0) * rho + (0.35 / 3.0) * (qx + qy + qz)
        dxxyy = dxxyy - (base - 0.175 * qz)
        dxxzz = dxxzz - (base - 0.175 * qy)
        dyyzz = dyyzz - (base - 0.175 * qx)
    trace = nxx + nyy + nzz
    iso = trace * (-1.0 / 24.0)
    hxx = 0.625 * nxx + iso
    hyy = 0.625 * nyy + iso
    hzz = 0.625 * nzz + iso
    out = {}

    def less(d, v):
        return -v if f[d] is None else f[d] - v

    def diagonal(quad, cross, la, lb, da, db):
        t1, t2 = quad + cross, quad - cross
        v1, v2 = la + lb, la - lb
        out_dirs = []
        for sa, sb in ((1, 1), (-1, -1), (1, -1), (-1, 1)):
            e = tuple(sa * p + sb * q for p, q in zip(da, db))
            out_dirs.append(e)
        out[out_dirs[0]] = less(out_dirs[0], t1 + v1)
        out[out_dirs[1]] = less(out_dirs[1], t1 - v1)
        out[out_dirs[2]] = less(out_dirs[2], t2 + v2)
        out[out_dirs[3]] = less(out_dirs[3], t2 - v2)

    X, Y, Z = (1, 0, 0), (0, 1, 0), (0, 0, 1)
    diagonal(dxxyy, dxy, dxyy, dxxy, X, Y)
    diagonal(dxxzz, dxz, dxzz, dxxz, X, Z)
    diagonal(dyyzz, dyz, dyzz, dyyz, Y, Z)

    def axis(half, q1, q2, l1, l2, d):
        even = half - 2.0 * (q1 + q2)
        odd = 2.0 * (l1 + l2)
        out[d] = less(d, even - odd)
        out[neg(d)] = less(neg(d), even + odd)

    axis(hxx, dxxyy, dxxzz, dxyy, dxzz, X)
    axis(hyy, dxxyy, dyyzz, dxxy, dyzz, Y)
    axis(hzz, dxxzz, dyyzz, dxxz, dyyz, Z)
    out[(0, 0, 0)] = f[(0, 0, 0)] + trace - 4.0 * (dxxyy + dxxzz + dyyzz)
    return out, rho, (jx, jy, jz)


def gradient(ph, plane, row):
    def at(dx, dy):
        return ph[plane + dx, pl.ds(row + dy, 8), :]

    c = at(0, 0)
    xp, xm, yp, ym = at(1, 0), at(-1, 0), at(0, 1), at(0, -1)
    d1 = at(1, 1) - at(-1, -1)
    d2 = at(1, -1) - at(-1, 1)
    ex = xp - xm
    ey = yp - ym
    h = 2.0 * c + ((xp + xm) + (yp + ym))
    k = 1.0 / 12.0
    gx = k * ((2.0 * ex + (d1 + d2)) + (zroll(ex, 1) + zroll(ex, -1)))
    gy = k * ((2.0 * ey + (d1 - d2)) + (zroll(ey, 1) + zroll(ey, -1)))
    gz = k * (zroll(h, -1) - zroll(h, 1))
    return c, gx, gy, gz


def finish(dirs, s_of, ph, rho, fluid, plane, row, fp, red):
    p, gx, gy, gz = gradient(ph, plane + 1, row)
    g2 = gx * gx + gy * gy + gz * gz
    inv = lax.rsqrt(jnp.maximum(g2, 0.01)) * fluid
    h1 = (0.1 * W1) * inv
    h2 = (0.1 * W2) * inv
    cc = (0.175 * rho) * ((1.0 - p * p) * inv)
    c1 = W1 * cc
    c2 = W2 * cc
    frac = 0.5 + 0.5 * p
    comp = (gx, gy, gz)
    sums = {}
    cache = {}
    for d in dirs:
        moving = [k for k in range(3) if d[k] != 0]
        if not moving:
            q, c = h1 * (6.0 * g2), None
        else:
            sign = d[moving[0]]
            key = d if sign > 0 else neg(d)
            if key not in cache:
                if len(moving) == 1:
                    a = comp[moving[0]]
                    cache[key] = (h1 * (a * a - g2), c1 * a)
                else:
                    u, v = moving
                    a = comp[u] + comp[v] if key[v] > 0 else comp[u] - comp[v]
                    cache[key] = (h2 * (a * a - g2), c2 * a)
            q, c = cache[key]
        known = s_of(d)
        val = q if known is None else known + q
        fp[POS[d], plane, pl.ds(row, 8), :] = zroll(val, d[2])
        r = frac * val
        if c is not None:
            r = r + c if sign > 0 else r - c
        r = zroll(r, d[2])
        g = d[:2]
        sums[g] = r if g not in sums else sums[g] + r
    for g, r in sums.items():
        red[GPOS[g], plane, pl.ds(row, 8), :] = r


def arrived(d, fp, plane, row):
    return fp[POS[d], plane - d[0], pl.ds(row - d[1], 8), :]


def red_arrived(red, plane, row):
    total = None
    for g in GROUPS:
        v = red[GPOS[g], plane - g[0], pl.ds(row - g[1], 8), :]
        total = v if total is None else total + v
    return total


def tile_rows(t):
    return lax.broadcasted_iota(jnp.int32, (8, 128), 0) + (8 * t - 4)


def face(high):
    a = jnp.where(high, NXL - 1, 0)
    b = jnp.where(high, NXL - 2, 1)
    c = jnp.where(high, NXL - 3, 2)
    out = jnp.where(high, 5, 0)
    back = jnp.where(high, 0, 5)
    return a, b, c, out, back


def message_tile(high, row, s, rho, fl, ph, fp, red):
    a, b, c, out, back = face(high)
    gout = jnp.where(high, 3, 0)
    gback = jnp.where(high, 0, 3)
    rows = pl.ds(row - ROW0, 8)
    own = pl.ds(row, 8)

    def plain():
        v = [s[out + j, a, rows, :] for j in range(5)]
        return v, [rho[a, rows, :], ph[a + 2, own, :], ph[b + 2, own, :], fl[a, rows, :]]

    def moved():
        f = {}
        total = None
        for j in range(5):
            d = DIRS[5 + j]
            shifted = pl.ds(row - d[1], 8)
            f[d] = fp[out + j, b + 1, shifted, :]
            f[(-1, d[1], d[2])] = None
            v = fp[out + j, c + 1, shifted, :] + fp[back + j, a + 1, shifted, :]
            total = v if total is None else total + v
        for j in range(10, 19):
            shifted = pl.ds(row - DIRS[j][1], 8)
            f[DIRS[j]] = fp[j, a + 1, shifted, :]
            total = total + fp[j, b + 1, shifted, :]
        linear, dens, mom = collide(f, equilibrium=False)
        at_a, at_b = None, None
        for j in range(3):
            shifted = pl.ds(row - GROUPS[j][1], 8)
            v = red[gout + j, b + 1, shifted, :] + red[6 + j, a + 1, shifted, :]
            at_a = v if at_a is None else at_a + v
            v = (red[gout + j, c + 1, shifted, :] + red[gback + j, a + 1, shifted, :]) + red[
                6 + j, b + 1, shifted, :
            ]
            at_b = v if at_b is None else at_b + v
        return [linear[DIRS[5 + j]] for j in range(5)] + [dens, *mom], [at_a, total, at_b]

    return plain, moved


PLAIN = [0, 1, 2, 3, 4, 14, 15, 16, 17]
MOVED = [5, 6, 7, 8, 9, 10, 11, 12, 13, 18, 19, 20]


def plane_of(msg, j):
    if not isinstance(msg, tuple):
        return msg.at[j]
    return msg[0].at[j] if j < HALF else msg[1].at[j - HALF]


def main_message(msg, high, state):
    for n in range(NYL // 8):
        plain, moved = message_tile(high, ROW0 + 4 + 8 * n, *state)
        for kinds, part in ((PLAIN, plain()), (MOVED, moved())):
            for j, v in zip(kinds, part[0] + part[1]):
                plane_of(msg, j)[pl.ds(8 * n, 8), :] = v


def corner_message(msg, base, high, state):
    for n, (first, second) in enumerate(((0, 2), (EXT - 8, EXT - 6))):
        plain, _ = message_tile(high, ROW0 + first, *state)
        _, moved = message_tile(high, ROW0 + second, *state)
        for kinds, part, r in ((PLAIN, plain(), 4 * n), (MOVED, moved(), 0)):
            for j, v in zip(kinds, part[0] + part[1]):
                plane_of(msg, j)[pl.ds(base + 4 * n, 4), :] = v[r:r + 4]


def inner_step(tiles, s, rho, fl, ph, fp, red):
    def plane(x, carry):
        for t in tiles:
            rows = pl.ds(8 * t, 8)
            finish(
                DIRS, lambda d: s[POS[d], x, rows, :], ph, rho[x, rows, :],
                fl[x, rows, :], x + 1, ROW0 + 8 * t, fp, red,
            )
        return carry

    lax.fori_loop(1, NXL - 1, plane, 0)
    for x, base in ((0, 5), (NXL - 1, 0)):
        for t in tiles:
            row = ROW0 + 8 * t
            frac = 0.5 + 0.5 * ph[x + 2, pl.ds(row, 8), :]
            sums = {}
            for d in DIRS[base:base + 5] + DIRS[10:]:
                v = s[POS[d], x, pl.ds(8 * t, 8), :]
                fp[POS[d], x + 1, pl.ds(row, 8), :] = zroll(v, d[2])
                r = zroll(frac * v, d[2])
                sums[d[:2]] = r if d[:2] not in sums else sums[d[:2]] + r
            for g, r in sums.items():
                red[GPOS[g], x + 1, pl.ds(row, 8), :] = r


def pack_kernel(pops_hbm, labels_hbm, solid_hbm, ya, yb, pops, labels, solid, sems):
    odd = lax.axis_index("gy") % 2
    copies = [
        pltpu.make_async_copy(labels_hbm, labels, sems.at[0]),
        pltpu.make_async_copy(solid_hbm, solid, sems.at[1]),
    ] + [
        pltpu.make_async_copy(pops_hbm.at[:, x], pops.at[:, x], sems.at[2 + x])
        for x in range(NXL)
    ]
    for c in copies:
        c.start()
    for c in copies:
        c.wait()

    def pack(out, high):
        three = pl.ds(NYL - 3 if high else 0, 3)
        four = pl.ds(NYL - 4 if high else 0, 4)
        for i in range(19):
            for x in range(NXL):
                out[pl.ds(i * 12 + x * 3, 3), :] = pops[i, x, three, :]
        for x in range(NXL):
            out[pl.ds(228 + x * 4, 4), :] = labels[x, four, :].astype(jnp.float32)
            out[pl.ds(244 + x * 3, 3), :] = solid[x, three, :].astype(jnp.float32)

    @pl.when(odd == 0)
    def _():
        pack(ya, True)
        pack(yb, False)

    @pl.when(odd == 1)
    def _():
        pack(ya, False)
        pack(yb, True)


def start_kernel(pops, labels, solid, s, rho, fl, ph, fp, red, xa, xd, xb):
    gy = lax.axis_index("gy")
    low_edge = gy == 0
    high_edge = gy == lax.axis_size("gy") - 1

    def plane(x, carry):
        for t in range(NYL // 8):
            own = pl.ds(8 * t, 8)
            rows = pl.ds(8 * t + 4, 8)
            f = {d: pops[REF_OF[k], x, own, :] for k, d in enumerate(DIRS)}
            is_solid = solid[x, own, :] > 0
            y = lax.broadcasted_iota(jnp.int32, (8, 128), 0) + 8 * t
            if t == 0:
                is_solid = is_solid | ((y == 0) & low_edge)
            if t == NYL // 8 - 1:
                is_solid = is_solid | ((y == NYL - 1) & high_edge)
            relaxed, total, _ = collide(f)
            for d in DIRS:
                s[POS[d], x, rows, :] = jnp.where(is_solid, f[neg(d)], relaxed[d])
            rho[x, rows, :] = total
            fl[x, rows, :] = jnp.where(is_solid, 0.0, 1.0)
            ph[x + 2, pl.ds(ROW0 + 4 + 8 * t, 8), :] = jnp.where(labels[x, own, :] > 0, 1.0, -1.0)
        return carry

    lax.fori_loop(0, NXL, plane, 0)
    inner_step(range(NT), s, rho, fl, ph, fp, red)
    low_a = lax.axis_index("gx") % 2 == 1
    main_message(xb, low_a, (s, rho, fl, ph, fp, red))
    main_message((xa, xd), jnp.logical_not(low_a), (s, rho, fl, ph, fp, red))


def edge_kernel(ya, yb, s_in, rho_in, fl_in, ph_in, fp_in, red_in, xa_in, xd_in,
                s, rho, fl, ph, fp, red, xa, xd, xc, raw):
    gy = lax.axis_index("gy")
    odd = gy % 2
    low_edge = gy == 0
    high_edge = gy == lax.axis_size("gy") - 1

    def unpack(src, top):
        r = 1 if top else 4
        for x in range(NXL):
            for i in range(19):
                raw[i, x, pl.ds(r, 3), :] = src[pl.ds(i * 12 + x * 3, 3), :]
            raw[19, x, pl.ds(0 if top else 4, 4), :] = src[pl.ds(228 + x * 4, 4), :]
            raw[20, x, pl.ds(r, 3), :] = src[pl.ds(244 + x * 3, 3), :]

    @pl.when(odd == 0)
    def _():
        unpack(ya, False)
        unpack(yb, True)

    @pl.when(odd == 1)
    def _():
        unpack(ya, True)
        unpack(yb, False)

    row = lax.broadcasted_iota(jnp.int32, (8, 128), 0)
    inside = jnp.where(row < 4, jnp.where(low_edge, 0, 1), jnp.where(high_edge, 0, 1)) > 0

    def plane(x, carry):
        def put(ref, base, v):
            ref[pl.ds(base, 4), :] = v[0:4]
            ref[pl.ds(base + NYL + 4, 4), :] = v[4:8]

        f = {d: raw[REF_OF[k], x] for k, d in enumerate(DIRS)}
        is_solid = raw[20, x] > 0.5
        relaxed, total, _ = collide(f)
        for d in DIRS:
            v = jnp.where(is_solid, f[neg(d)], relaxed[d])
            put(s.at[POS[d], x], 0, jnp.where(inside, v, 0.0))
        put(rho.at[x], 0, total)
        put(fl.at[x], 0, jnp.where(inside & jnp.logical_not(is_solid), 1.0, 0.0))
        p = jnp.where(raw[19, x] > 0.5, 1.0, -1.0)
        put(ph.at[x + 2], ROW0, jnp.where(inside, p, 0.0))
        return carry

    lax.fori_loop(0, NXL, plane, 0)
    inner_step((0, NT - 1), s, rho, fl, ph, fp, red)
    low_a = lax.axis_index("gx") % 2 == 1
    corner_message(xc, 0, low_a, (s, rho, fl, ph, fp, red))
    corner_message((xa, xd), NYL, jnp.logical_not(low_a), (s, rho, fl, ph, fp, red))


def edges():
    gy = lax.axis_index("gy")
    low_edge = gy == 0
    high_edge = gy == lax.axis_size("gy") - 1

    def mask(t):
        y = tile_rows(t)
        if t == 0:
            return (y >= 0) | jnp.logical_not(low_edge)
        if t == NT - 1:
            return (y < NYL) | jnp.logical_not(high_edge)
        return None

    return mask


def put_message(src, base, side, corner, hx, ph):
    near = jnp.where(side == 1, NXL + 2, 1)
    far = jnp.where(side == 1, NXL + 3, 0)
    for j in range(21):
        moved = 2 if corner and j in MOVED else 0
        if corner:
            spans = ((moved, 0, 4), (EXT - 4 - moved, 4, 4))
        else:
            spans = [(4 + 8 * n, 8 * n, 8) for n in range(NYL // 8)]
        for to, part, n in spans:
            v = plane_of(src, j)[pl.ds(base + part, n), :]
            if j in (15, 16):
                ph[near if j == 15 else far, pl.ds(ROW0 + to, n), :] = v
            else:
                hx[j, pl.ds(to, n), :] = v


def by_side(side, step):
    for k in (0, 1):
        pl.when(side == k)(lambda: step(k))


def side_dirs(side):
    if side == 0:
        return 0, DIRS[5:10], DIRS[0:5]
    return NXL + 1, DIRS[0:5], DIRS[5:10]


def halo_first(side, hx, ph, fp, red, tiles=range(NT)):
    index, towards, _ = side_dirs(side)
    for t in tiles:
        rows = pl.ds(8 * t, 8)
        finish(
            DIRS, lambda d: hx[towards.index(d), rows, :] if d in towards else None, ph,
            hx[14, rows, :], hx[17, rows, :], index, ROW0 + 8 * t, fp, red,
        )


def halo_collide(side, hx, fp, red, ph, s2, rho2, tiles=range(NT)):
    mask = edges()
    index, towards, back = side_dirs(side)
    near, far = (NXL + 2, NXL + 3) if side == 1 else (1, 0)
    outwards = 1.0 if side == 0 else -1.0
    for t in tiles:
        row = ROW0 + 8 * t
        rows = pl.ds(8 * t, 8)
        f = {d: None if d in towards else arrived(d, fp, index, row) for d in DIRS}
        known = (
            hx[10, rows, :], outwards * hx[11, rows, :], hx[12, rows, :], hx[13, rows, :],
        )
        relaxed, total, _ = collide(f, known)
        rsum = hx[18, rows, :]
        rfar = hx[20, rows, :]
        for g in GROUPS:
            shifted = pl.ds(row - g[1], 8)
            if g[0] != towards[0][0]:
                rsum = rsum + red[GPOS[g], index - g[0], shifted, :]
            if g[0] == back[0][0]:
                rfar = rfar + red[GPOS[g], index, shifted, :]
        ffar = hx[19, rows, :]
        for d in back:
            ffar = ffar + fp[POS[d], index, pl.ds(row - d[1], 8), :]
        p = 2.0 * rsum / total - 1.0
        pfar = 2.0 * rfar / ffar - 1.0
        inside = mask(t)
        if inside is not None:
            p = jnp.where(inside, p, 0.0)
            pfar = jnp.where(inside, pfar, 0.0)
        is_fluid = hx[17, rows, :] > 0.5
        for j, d in enumerate(towards):
            v = jnp.where(is_fluid, relaxed[d] + hx[5 + j, rows, :], f[neg(d)])
            if inside is not None:
                v = jnp.where(inside, v, 0.0)
            s2[POS[d], index, rows, :] = v
        rho2[index, rows, :] = total
        ph[near, pl.ds(row, 8), :] = p
        ph[far, pl.ds(row, 8), :] = pfar


def halo_second(side, hx, s2, rho2, ph, fp, red, tiles=range(NT)):
    index, towards, _ = side_dirs(side)
    for t in tiles:
        rows = pl.ds(8 * t, 8)
        finish(
            towards, lambda d: s2[POS[d], index, rows, :], ph, rho2[index, rows, :],
            hx[17, rows, :], index, ROW0 + 8 * t, fp, red,
        )


def own_finish(x, s, k, rho, fl, ph, fp, red, tiles=range(NT)):
    for t in tiles:
        rows = pl.ds(8 * t, 8)
        finish(
            DIRS, lambda d: s[POS[d], k, rows, :], ph, rho[k, rows, :], fl[x, rows, :],
            x + 1, ROW0 + 8 * t, fp, red,
        )


def own_collide(x, k, fl, fp, red, ph, s2, rho2, tiles=range(NT)):
    mask = edges()
    for t in tiles:
        row = ROW0 + 8 * t
        rows = pl.ds(8 * t, 8)
        f = {d: arrived(d, fp, x + 1, row) for d in DIRS}
        relaxed, total, _ = collide(f)
        p = 2.0 * red_arrived(red, x + 1, row) / total - 1.0
        inside = mask(t)
        if inside is not None:
            p = jnp.where(inside, p, 0.0)
        is_fluid = fl[x, rows, :] > 0.5
        for d in DIRS:
            v = jnp.where(is_fluid, relaxed[d], f[neg(d)])
            if inside is not None:
                v = jnp.where(inside, v, 0.0)
            s2[POS[d], k, rows, :] = v
        rho2[k, rows, :] = total
        ph[x + 2, pl.ds(row, 8), :] = p


def two_planes(side, step):
    def body(k, carry):
        step(jnp.where(side == 1, NXL - 1 - k, k), k)
        return carry

    lax.fori_loop(0, 2, body, 0)


def near_kernel(s, rho, fl, ph_in, fp_in, red_in, xa, xd,
                fp, red, fp2, red2, ph2, s2_next, rho2_next, ph, hx, s2, rho2, own2, orho2):
    side = 1 - lax.axis_index("gx") % 2
    ph[...] = ph_in[...]
    put_message((xa, xd), 0, side, False, hx, ph)
    put_message((xa, xd), NYL, side, True, hx, ph)
    first = jnp.where(side == 1, NXL - 1, 0)
    own_finish(first, s, first, rho, fl, ph, fp, red)
    by_side(side, lambda k: halo_first(k, hx, ph, fp, red))
    two_planes(side, lambda x, k: own_collide(x, k, fl, fp, red, ph2, own2, orho2))
    by_side(side, lambda k: halo_collide(k, hx, fp, red, ph2, s2, rho2))
    own_finish(first, own2, 0, orho2, fl, ph2, fp2, red2)
    by_side(side, lambda k: halo_second(k, hx, s2, rho2, ph2, fp2, red2))
    s2_next[:, 0] = own2[:, 1]
    rho2_next[0] = orho2[1]


def far_half(tiles, s, rho, fl, ph, fp, red, fp2, red2, ph2, s2_next, rho2_next, hx, s2,
             rho2, own2, orho2):
    side = lax.axis_index("gx") % 2
    first = jnp.where(side == 1, NXL - 1, 0)
    third = jnp.where(side == 1, NXL - 3, 2)
    own_finish(first, s, first, rho, fl, ph, fp, red, tiles)
    by_side(side, lambda k: halo_first(k, hx, ph, fp, red, tiles))
    two_planes(side, lambda x, k: own_collide(x, k, fl, fp, red, ph2, own2, orho2, tiles))
    by_side(side, lambda k: halo_collide(k, hx, fp, red, ph2, s2, rho2, tiles))
    own_finish(third, s2_next, 0, rho2_next, fl, ph2, fp2, red2, tiles)
    two_planes(
        side, lambda x, k: own_finish(x, own2, k, orho2, fl, ph2, fp2, red2, tiles)
    )
    by_side(side, lambda k: halo_second(k, hx, s2, rho2, ph2, fp2, red2, tiles))


def write_out(starts, fp2, red2, pops_out, phase_out, pops_hbm, phase_hbm, sems):
    def copies(x):
        out = []
        for n, r in enumerate(starts):
            part, rows = pl.ds(8 * n, 8), pl.ds(r, 8)
            out += [
                pltpu.make_async_copy(
                    pops_out.at[:, x, part], pops_hbm.at[:, x, rows], sems.at[4 * x + n]
                ),
                pltpu.make_async_copy(
                    phase_out.at[x, part], phase_hbm.at[x, rows], sems.at[4 * x + 2 + n]
                ),
            ]
        return out

    for x in range(NXL):
        for n, r in enumerate(starts):
            row = ROW0 + 4 + r
            rows = pl.ds(8 * n, 8)
            total = None
            for d in DIRS:
                v = arrived(d, fp2, x + 1, row)
                pops_out[REF_OF[POS[d]], x, rows, :] = v
                total = v if total is None else total + v
            phase_out[x, rows, :] = 2.0 * red_arrived(red2, x + 1, row) / total - 1.0
        for copy in copies(x):
            copy.start()
    for x in range(NXL):
        for copy in copies(x):
            copy.wait()


def far_kernel(s, rho, fl, ph_in, fp_in, red_in, fp2_in, red2_in, ph2_in, s2_next, rho2_next,
               xb, pops_hbm, phase_hbm, fp, red, fp2, red2, ph, ph2, hx,
               s2, rho2, own2, orho2, pops_out, phase_out, sems):
    ph[...] = ph_in[...]
    ph2[...] = ph2_in[...]
    put_message(xb, 0, lax.axis_index("gx") % 2, False, hx, ph)
    far_half(
        range(NT), s, rho, fl, ph, fp, red, fp2, red2, ph2, s2_next, rho2_next, hx, s2,
        rho2, own2, orho2,
    )
    write_out((8, 16), fp2, red2, pops_out, phase_out, pops_hbm, phase_hbm, sems)


def end_kernel(s, rho, fl, s2_next, rho2_next, xc, pops_in, phase_in, fp_in, red_in, fp2_in,
               red2_in, ph_in, ph2_in, hx_in, pops_hbm, phase_hbm, fp, red, fp2, red2, ph, ph2,
               hx, s2, rho2, own2, orho2, pops_out, phase_out, sems):
    put_message(xc, 0, lax.axis_index("gx") % 2, True, hx, ph)
    far_half(
        (0, NT - 1), s, rho, fl, ph, fp, red, fp2, red2, ph2, s2_next, rho2_next, hx, s2,
        rho2, own2, orho2,
    )
    write_out((0, NYL - 8), fp2, red2, pops_out, phase_out, pops_hbm, phase_hbm, sems)


F32 = jnp.float32
VM = pl.BlockSpec(memory_space=pltpu.VMEM)
HB = pl.BlockSpec(memory_space=pltpu.HBM)
MIB = 1024 * 1024


def shaped(*dims):
    return jax.ShapeDtypeStruct(dims, F32)


def call(kernel, in_specs, outs, scratch, name, aliases=None, vmem=40, cost=0,
         out_specs=None):
    return pl.pallas_call(
        kernel,
        in_specs=in_specs,
        out_specs=out_specs or [VM] * len(outs),
        out_shape=outs,
        scratch_shapes=scratch,
        input_output_aliases=aliases or {},
        compiler_params=pltpu.CompilerParams(vmem_limit_bytes=vmem * MIB),
        cost_estimate=pl.CostEstimate(flops=cost, bytes_accessed=cost, transcendentals=0),
        name=name,
    )


def pairs(count, first):
    out = []
    for i in range(first, count + first, 2):
        a, b = i % count, (i + 1) % count
        out += [(a, b), (b, a)]
    return out


def swap(value, axis, first):
    return lax.ppermute(value, axis, pairs(lax.axis_size(axis), first))


def on_device(populations, labels, solid_mask):
    state = [
        shaped(19, NXL, EXT, 128), shaped(NXL, EXT, 128), shaped(NXL, EXT, 128),
        shaped(NXL + 4, SROWS, 128), shaped(19, NXL + 2, SROWS, 128),
        shaped(9, NXL + 2, SROWS, 128),
    ]
    inputs = [
        pltpu.with_memory_space_constraint(v, pltpu.HBM)
        for v in (populations, labels, solid_mask)
    ]

    split = [shaped(HALF, EXT, 128), shaped(21 - HALF, EXT, 128)]
    whole = [
        shaped(19, NXL, NYL, 128), jax.ShapeDtypeStruct((NXL, NYL, 128), jnp.int32),
        jax.ShapeDtypeStruct((NXL, NYL, 128), jnp.int32),
    ]
    ya, yb, *held = call(
        pack_kernel, [HB] * 3, [shaped(YROWS, 128)] * 2 + whole,
        [pltpu.SemaphoreType.DMA((6,))], "pack",
    )(*inputs)
    ya = swap(ya, "gy", 0)
    yb = swap(yb, "gy", 1)
    *mid, xa, xd, xb = call(
        start_kernel, [VM] * 3, state + split + [shaped(21, NYL, 128)], [], "start",
    )(*held)
    xb = swap(xb, "gx", 1)
    *mid, xa, xd, xc = call(
        edge_kernel, [VM] * 10, state + split + [shaped(21, 8, 128)],
        [pltpu.VMEM((21, NXL, 8, 128), F32)], "edge", {2 + i: i for i in range(8)},
        cost=10 ** 10,
    )(ya, yb, *mid, xa, xd)
    xc = swap(xc, "gx", 1)
    xa = swap(xa, "gx", 0)
    xd = swap(xd, "gx", 0)
    s, rho, fl, ph, fp, red = mid
    halo = [
        pltpu.VMEM((21, EXT, 128), F32), pltpu.VMEM((19, NXL + 2, EXT, 128), F32),
        pltpu.VMEM((NXL + 2, EXT, 128), F32), pltpu.VMEM((19, 2, EXT, 128), F32),
        pltpu.VMEM((2, EXT, 128), F32),
    ]
    phases = pltpu.VMEM((NXL + 4, SROWS, 128), F32)
    fp, red, fp2, red2, ph2, s2_next, rho2_next = call(
        near_kernel, [VM] * 8,
        [state[4], state[5], state[4], state[5], state[3], shaped(19, 1, EXT, 128),
         shaped(1, EXT, 128)],
        [phases] + halo, "near", {4: 0, 5: 1}, cost=0,
    )(s, rho, fl, ph, fp, red, xa, xd)
    results = [
        shaped(19, NXL, NYL, 128), shaped(NXL, NYL, 128), state[4], state[5], state[4],
        state[5], state[3], state[3], shaped(21, EXT, 128),
    ]
    work = halo[1:] + [
        pltpu.VMEM((19, NXL, 16, 128), F32), pltpu.VMEM((NXL, 16, 128), F32),
        pltpu.SemaphoreType.DMA((4 * NXL,)),
    ]
    spaces = [HB] * 2 + [VM] * 7
    out = call(
        far_kernel, [VM] * 12, results, work, "far", {4: 2, 5: 3, 6: 4, 7: 5},
        out_specs=spaces,
    )(s, rho, fl, ph, fp, red, fp2, red2, ph2, s2_next, rho2_next, xb)
    out = call(
        end_kernel, [VM] * 6 + spaces, results, work, "end", {6 + i: i for i in range(9)},
        out_specs=spaces,
    )(s, rho, fl, s2_next, rho2_next, xc, *out)
    return out[0], out[1]


def solution(mesh):
    in_specs = (P(None, "gx", "gy", None), P("gx", "gy", None), P("gx", "gy", None))
    out_specs = (P(None, "gx", "gy", None), P("gx", "gy", None))

    def run(populations, labels, solid_mask):
        new, phase = on_device(populations, labels, solid_mask)
        return new, phase

    return jax.shard_map(
        run, mesh=mesh, in_specs=in_specs, out_specs=out_specs, check_vma=False
    )
```

```python
import jax
import jax.numpy as jnp
import numpy as np
from jax import lax
from jax.experimental import pallas as pl
from jax.experimental.pallas import tpu as pltpu
from jax.sharding import PartitionSpec as P

VELOCITY_SET = [
    (0, 0, 0), (1, 0, 0), (-1, 0, 0), (0, 1, 0), (0, -1, 0), (0, 0, 1), (0, 0, -1),
    (1, 1, 0), (-1, -1, 0), (1, -1, 0), (-1, 1, 0), (1, 0, 1), (-1, 0, -1), (1, 0, -1),
    (-1, 0, 1), (0, 1, 1), (0, -1, -1), (0, 1, -1), (0, -1, 1),
]
DIRS = [
    (-1, 0, 0), (-1, 1, 0), (-1, -1, 0), (-1, 0, 1), (-1, 0, -1),
    (1, 0, 0), (1, 1, 0), (1, -1, 0), (1, 0, 1), (1, 0, -1),
    (0, 0, 0), (0, 1, 0), (0, -1, 0), (0, 0, 1), (0, 0, -1),
    (0, 1, 1), (0, -1, -1), (0, 1, -1), (0, -1, 1),
]
REF_OF = [VELOCITY_SET.index(d) for d in DIRS]
POS = {d: k for k, d in enumerate(DIRS)}
GROUPS = [(-1, 0), (-1, 1), (-1, -1), (1, 0), (1, 1), (1, -1), (0, 0), (0, 1), (0, -1)]
GPOS = {g: k for k, g in enumerate(GROUPS)}
NXL = 4
NYL = 32
EXT = 40
NT = 5
ROW0 = 8
SROWS = 56
HALF = 11
YROWS = 256
W1 = 1.0 / 18.0
W2 = 1.0 / 36.0


def neg(d):
    return (-d[0], -d[1], -d[2])


def zroll(v, shift):
    if shift == 0:
        return v
    return pltpu.roll(v, shift % 128, 1)


def collide(f, known=None, equilibrium=True):
    def pair(a, b):
        pa, pb = f[a], f[b]
        if pb is None:
            return pa, pa
        if pa is None:
            return pb, -pb
        return pa + pb, pa - pb

    s1, d1 = pair((1, 1, 0), (-1, -1, 0))
    s2, d2 = pair((1, -1, 0), (-1, 1, 0))
    xxyy, xy, xyy, xxy = s1 + s2, s1 - s2, d1 + d2, d1 - d2
    s1, d1 = pair((1, 0, 1), (-1, 0, -1))
    s2, d2 = pair((1, 0, -1), (-1, 0, 1))
    xxzz, xz, xzz, xxz = s1 + s2, s1 - s2, d1 + d2, d1 - d2
    s1, d1 = pair((0, 1, 1), (0, -1, -1))
    s2, d2 = pair((0, 1, -1), (0, -1, 1))
    yyzz, yz, yzz, yyz = s1 + s2, s1 - s2, d1 + d2, d1 - d2
    ax, dx = pair((1, 0, 0), (-1, 0, 0))
    ay, dy = pair((0, 1, 0), (0, -1, 0))
    az, dz = pair((0, 0, 1), (0, 0, -1))
    jx = dx + (xyy + xzz)
    jy = dy + (xxy + yzz)
    jz = dz + (xxz + yyz)
    nxx = ax + (xxyy + xxzz)
    nyy = ay + (xxyy + yyzz)
    nzz = az + (xxzz + yyzz)
    rho = (f[(0, 0, 0)] + (ax + ay)) + (az + (xxyy + (xxzz + yyzz)))
    if known is not None:
        rho, jx, jy, jz = rho + known[0], jx + known[1], jy + known[2], jz + known[3]
    dxy, dxz, dyz = 0.3125 * xy, 0.3125 * xz, 0.3125 * yz
    dxyy, dxzz, dxxy = 0.3 * xyy, 0.3 * xzz, 0.3 * xxy
    dyzz, dxxz, dyyz = 0.3 * yzz, 0.3 * xxz, 0.3 * yyz
    dxxyy, dxxzz, dyyzz = 0.35 * xxyy, 0.35 * xxzz, 0.35 * yyzz
    if equilibrium:
        inv = 1.0 / rho
        ux, uy, uz = jx * inv, jy * inv, jz * inv
        qx, qy, qz = jx * ux, jy * uy, jz * uz
        third = rho * (1.0 / 3.0)
        nxx = nxx - (third + qx)
        nyy = nyy - (third + qy)
        nzz = nzz - (third + qz)
        dxy = 0.3125 * (xy - jx * uy)
        dxz = 0.3125 * (xz - jx * uz)
        dyz = 0.3125 * (yz - jy * uz)
        kx, ky, kz = jx * 0.1, jy * 0.1, jz * 0.1
        dxyy, dxzz = dxyy - kx, dxzz - kx
        dxxy, dyzz = dxxy - ky, dyzz - ky
        dxxz, dyyz = dxxz - kz, dyyz - kz
        base = (0.35 / 9.0) * rho + (0.35 / 3.0) * (qx + qy + qz)
        dxxyy = dxxyy - (base - 0.175 * qz)
        dxxzz = dxxzz - (base - 0.175 * qy)
        dyyzz = dyyzz - (base - 0.175 * qx)
    trace = nxx + nyy + nzz
    iso = trace * (-1.0 / 24.0)
    hxx = 0.625 * nxx + iso
    hyy = 0.625 * nyy + iso
    hzz = 0.625 * nzz + iso
    out = {}

    def less(d, v):
        return -v if f[d] is None else f[d] - v

    def diagonal(quad, cross, la, lb, da, db):
        t1, t2 = quad + cross, quad - cross
        v1, v2 = la + lb, la - lb
        out_dirs = []
        for sa, sb in ((1, 1), (-1, -1), (1, -1), (-1, 1)):
            e = tuple(sa * p + sb * q for p, q in zip(da, db))
            out_dirs.append(e)
        out[out_dirs[0]] = less(out_dirs[0], t1 + v1)
        out[out_dirs[1]] = less(out_dirs[1], t1 - v1)
        out[out_dirs[2]] = less(out_dirs[2], t2 + v2)
        out[out_dirs[3]] = less(out_dirs[3], t2 - v2)

    X, Y, Z = (1, 0, 0), (0, 1, 0), (0, 0, 1)
    diagonal(dxxyy, dxy, dxyy, dxxy, X, Y)
    diagonal(dxxzz, dxz, dxzz, dxxz, X, Z)
    diagonal(dyyzz, dyz, dyzz, dyyz, Y, Z)

    def axis(half, q1, q2, l1, l2, d):
        even = half - 2.0 * (q1 + q2)
        odd = 2.0 * (l1 + l2)
        out[d] = less(d, even - odd)
        out[neg(d)] = less(neg(d), even + odd)

    axis(hxx, dxxyy, dxxzz, dxyy, dxzz, X)
    axis(hyy, dxxyy, dyyzz, dxxy, dyzz, Y)
    axis(hzz, dxxzz, dyyzz, dxxz, dyyz, Z)
    out[(0, 0, 0)] = f[(0, 0, 0)] + trace - 4.0 * (dxxyy + dxxzz + dyyzz)
    return out, rho, (jx, jy, jz)


def gradient(ph, plane, row):
    def at(dx, dy):
        return ph[plane + dx, pl.ds(row + dy, 8), :]

    c = at(0, 0)
    xp, xm, yp, ym = at(1, 0), at(-1, 0), at(0, 1), at(0, -1)
    d1 = at(1, 1) - at(-1, -1)
    d2 = at(1, -1) - at(-1, 1)
    ex = xp - xm
    ey = yp - ym
    h = 2.0 * c + ((xp + xm) + (yp + ym))
    k = 1.0 / 12.0
    gx = k * ((2.0 * ex + (d1 + d2)) + (zroll(ex, 1) + zroll(ex, -1)))
    gy = k * ((2.0 * ey + (d1 - d2)) + (zroll(ey, 1) + zroll(ey, -1)))
    gz = k * (zroll(h, -1) - zroll(h, 1))
    return c, gx, gy, gz


def finish(dirs, s_of, ph, rho, fluid, plane, row, fp, red):
    p, gx, gy, gz = gradient(ph, plane + 1, row)
    g2 = gx * gx + gy * gy + gz * gz
    inv = lax.rsqrt(jnp.maximum(g2, 0.01)) * fluid
    h1 = (0.1 * W1) * inv
    h2 = (0.1 * W2) * inv
    cc = (0.175 * rho) * ((1.0 - p * p) * inv)
    c1 = W1 * cc
    c2 = W2 * cc
    frac = 0.5 + 0.5 * p
    comp = (gx, gy, gz)
    sums = {}
    cache = {}
    for d in dirs:
        moving = [k for k in range(3) if d[k] != 0]
        if not moving:
            q, c = h1 * (6.0 * g2), None
        else:
            sign = d[moving[0]]
            key = d if sign > 0 else neg(d)
            if key not in cache:
                if len(moving) == 1:
                    a = comp[moving[0]]
                    cache[key] = (h1 * (a * a - g2), c1 * a)
                else:
                    u, v = moving
                    a = comp[u] + comp[v] if key[v] > 0 else comp[u] - comp[v]
                    cache[key] = (h2 * (a * a - g2), c2 * a)
            q, c = cache[key]
        known = s_of(d)
        val = q if known is None else known + q
        fp[POS[d], plane, pl.ds(row, 8), :] = zroll(val, d[2])
        r = frac * val
        if c is not None:
            r = r + c if sign > 0 else r - c
        r = zroll(r, d[2])
        g = d[:2]
        sums[g] = r if g not in sums else sums[g] + r
    for g, r in sums.items():
        red[GPOS[g], plane, pl.ds(row, 8), :] = r


def arrived(d, fp, plane, row):
    return fp[POS[d], plane - d[0], pl.ds(row - d[1], 8), :]


def red_arrived(red, plane, row):
    total = None
    for g in GROUPS:
        v = red[GPOS[g], plane - g[0], pl.ds(row - g[1], 8), :]
        total = v if total is None else total + v
    return total


def tile_rows(t):
    return lax.broadcasted_iota(jnp.int32, (8, 128), 0) + (8 * t - 4)


def face(high):
    a = jnp.where(high, NXL - 1, 0)
    b = jnp.where(high, NXL - 2, 1)
    c = jnp.where(high, NXL - 3, 2)
    out = jnp.where(high, 5, 0)
    back = jnp.where(high, 0, 5)
    return a, b, c, out, back


def message_tile(high, row, s, rho, fl, ph, fp, red):
    a, b, c, out, back = face(high)
    gout = jnp.where(high, 3, 0)
    gback = jnp.where(high, 0, 3)
    rows = pl.ds(row - ROW0, 8)
    own = pl.ds(row, 8)

    def plain():
        v = [s[out + j, a, rows, :] for j in range(5)]
        return v, [rho[a, rows, :], ph[a + 2, own, :], ph[b + 2, own, :], fl[a, rows, :]]

    def moved():
        f = {}
        total = None
        for j in range(5):
            d = DIRS[5 + j]
            shifted = pl.ds(row - d[1], 8)
            f[d] = fp[out + j, b + 1, shifted, :]
            f[(-1, d[1], d[2])] = None
            v = fp[out + j, c + 1, shifted, :] + fp[back + j, a + 1, shifted, :]
            total = v if total is None else total + v
        for j in range(10, 19):
            shifted = pl.ds(row - DIRS[j][1], 8)
            f[DIRS[j]] = fp[j, a + 1, shifted, :]
            total = total + fp[j, b + 1, shifted, :]
        linear, dens, mom = collide(f, equilibrium=False)
        at_a, at_b = None, None
        for j in range(3):
            shifted = pl.ds(row - GROUPS[j][1], 8)
            v = red[gout + j, b + 1, shifted, :] + red[6 + j, a + 1, shifted, :]
            at_a = v if at_a is None else at_a + v
            v = (red[gout + j, c + 1, shifted, :] + red[gback + j, a + 1, shifted, :]) + red[
                6 + j, b + 1, shifted, :
            ]
            at_b = v if at_b is None else at_b + v
        return [linear[DIRS[5 + j]] for j in range(5)] + [dens, *mom], [at_a, total, at_b]

    return plain, moved


PLAIN = [0, 1, 2, 3, 4, 14, 15, 16, 17]
MOVED = [5, 6, 7, 8, 9, 10, 11, 12, 13, 18, 19, 20]


def plane_of(msg, j):
    if not isinstance(msg, tuple):
        return msg.at[j]
    return msg[0].at[j] if j < HALF else msg[1].at[j - HALF]


def main_message(msg, high, state):
    for n in range(NYL // 8):
        plain, moved = message_tile(high, ROW0 + 4 + 8 * n, *state)
        for kinds, part in ((PLAIN, plain()), (MOVED, moved())):
            for j, v in zip(kinds, part[0] + part[1]):
                plane_of(msg, j)[pl.ds(8 * n, 8), :] = v


def far_spans():
    out = []
    for i, j in enumerate(PLAIN):
        out += [(j, NYL * i + r, r) for r in range(0, NYL, 8)]
    base = NYL * len(PLAIN)
    for i, j in enumerate(MOVED):
        out += [(j, base + (NYL - 4) * i + r - 2, r) for r in (2, 10, 18, 22)]
    return out


FAR_ROWS = NYL * len(PLAIN) + (NYL - 4) * len(MOVED)


def far_message(msg, high, state):
    values = {}
    for r in range(0, NYL, 8):
        part = message_tile(high, ROW0 + 4 + r, *state)[0]()
        values.update({(j, r): v for j, v in zip(PLAIN, part[0] + part[1])})
    for r in (2, 10, 18, 22):
        part = message_tile(high, ROW0 + 4 + r, *state)[1]()
        values.update({(j, r): v for j, v in zip(MOVED, part[0] + part[1])})
    for j, row, r in far_spans():
        msg[pl.ds(row, 8), :] = values[j, r]


def corner_message(msg, base, high, state):
    for n, (first, second) in enumerate(((0, 2), (EXT - 8, EXT - 6))):
        plain, _ = message_tile(high, ROW0 + first, *state)
        _, moved = message_tile(high, ROW0 + second, *state)
        for kinds, part, r in ((PLAIN, plain(), 4 * n), (MOVED, moved(), 0)):
            for j, v in zip(kinds, part[0] + part[1]):
                plane_of(msg, j)[pl.ds(base + 4 * n, 4), :] = v[r:r + 4]


def inner_step(tiles, s, rho, fl, ph, fp, red):
    def plane(x, carry):
        for t in tiles:
            rows = pl.ds(8 * t, 8)
            finish(
                DIRS, lambda d: s[POS[d], x, rows, :], ph, rho[x, rows, :],
                fl[x, rows, :], x + 1, ROW0 + 8 * t, fp, red,
            )
        return carry

    lax.fori_loop(1, NXL - 1, plane, 0)
    for x, base in ((0, 5), (NXL - 1, 0)):
        for t in tiles:
            row = ROW0 + 8 * t
            frac = 0.5 + 0.5 * ph[x + 2, pl.ds(row, 8), :]
            sums = {}
            for d in DIRS[base:base + 5] + DIRS[10:]:
                v = s[POS[d], x, pl.ds(8 * t, 8), :]
                fp[POS[d], x + 1, pl.ds(row, 8), :] = zroll(v, d[2])
                r = zroll(frac * v, d[2])
                sums[d[:2]] = r if d[:2] not in sums else sums[d[:2]] + r
            for g, r in sums.items():
                red[GPOS[g], x + 1, pl.ds(row, 8), :] = r


def pack_kernel(pops_hbm, labels_hbm, solid_hbm, ya, yb, pops, labels, solid, sems):
    odd = lax.axis_index("gy") % 2
    copies = [
        pltpu.make_async_copy(labels_hbm, labels, sems.at[0]),
        pltpu.make_async_copy(solid_hbm, solid, sems.at[1]),
    ] + [
        pltpu.make_async_copy(pops_hbm.at[:, x], pops.at[:, x], sems.at[2 + x])
        for x in range(NXL)
    ]
    for c in copies:
        c.start()
    for c in copies:
        c.wait()

    def pack(out, high):
        three = pl.ds(NYL - 3 if high else 0, 3)
        four = pl.ds(NYL - 4 if high else 0, 4)
        for i in range(19):
            for x in range(NXL):
                out[pl.ds(i * 12 + x * 3, 3), :] = pops[i, x, three, :]
        for x in range(NXL):
            out[pl.ds(228 + x * 4, 4), :] = labels[x, four, :].astype(jnp.float32)
            out[pl.ds(244 + x * 3, 3), :] = solid[x, three, :].astype(jnp.float32)

    @pl.when(odd == 0)
    def _():
        pack(ya, True)
        pack(yb, False)

    @pl.when(odd == 1)
    def _():
        pack(ya, False)
        pack(yb, True)


def start_kernel(pops, labels, solid, s, rho, fl, ph, fp, red, xa, xd, xb):
    gy = lax.axis_index("gy")
    low_edge = gy == 0
    high_edge = gy == lax.axis_size("gy") - 1

    def plane(x, carry):
        for t in range(NYL // 8):
            own = pl.ds(8 * t, 8)
            rows = pl.ds(8 * t + 4, 8)
            f = {d: pops[REF_OF[k], x, own, :] for k, d in enumerate(DIRS)}
            is_solid = solid[x, own, :] > 0
            y = lax.broadcasted_iota(jnp.int32, (8, 128), 0) + 8 * t
            if t == 0:
                is_solid = is_solid | ((y == 0) & low_edge)
            if t == NYL // 8 - 1:
                is_solid = is_solid | ((y == NYL - 1) & high_edge)
            relaxed, total, _ = collide(f)
            for d in DIRS:
                s[POS[d], x, rows, :] = jnp.where(is_solid, f[neg(d)], relaxed[d])
            rho[x, rows, :] = total
            fl[x, rows, :] = jnp.where(is_solid, 0.0, 1.0)
            ph[x + 2, pl.ds(ROW0 + 4 + 8 * t, 8), :] = jnp.where(labels[x, own, :] > 0, 1.0, -1.0)
        return carry

    lax.fori_loop(0, NXL, plane, 0)
    inner_step(range(NT), s, rho, fl, ph, fp, red)
    low_a = lax.axis_index("gx") % 2 == 1
    far_message(xb, low_a, (s, rho, fl, ph, fp, red))
    main_message((xa, xd), jnp.logical_not(low_a), (s, rho, fl, ph, fp, red))


def edge_kernel(ya, yb, s_in, rho_in, fl_in, ph_in, fp_in, red_in, xa_in, xd_in,
                s, rho, fl, ph, fp, red, xa, xd, xc, raw):
    gy = lax.axis_index("gy")
    odd = gy % 2
    low_edge = gy == 0
    high_edge = gy == lax.axis_size("gy") - 1

    def unpack(src, top):
        r = 1 if top else 4
        for x in range(NXL):
            for i in range(19):
                raw[i, x, pl.ds(r, 3), :] = src[pl.ds(i * 12 + x * 3, 3), :]
            raw[19, x, pl.ds(0 if top else 4, 4), :] = src[pl.ds(228 + x * 4, 4), :]
            raw[20, x, pl.ds(r, 3), :] = src[pl.ds(244 + x * 3, 3), :]

    @pl.when(odd == 0)
    def _():
        unpack(ya, False)
        unpack(yb, True)

    @pl.when(odd == 1)
    def _():
        unpack(ya, True)
        unpack(yb, False)

    row = lax.broadcasted_iota(jnp.int32, (8, 128), 0)
    inside = jnp.where(row < 4, jnp.where(low_edge, 0, 1), jnp.where(high_edge, 0, 1)) > 0

    def plane(x, carry):
        def put(ref, base, v):
            ref[pl.ds(base, 4), :] = v[0:4]
            ref[pl.ds(base + NYL + 4, 4), :] = v[4:8]

        f = {d: raw[REF_OF[k], x] for k, d in enumerate(DIRS)}
        is_solid = raw[20, x] > 0.5
        relaxed, total, _ = collide(f)
        for d in DIRS:
            v = jnp.where(is_solid, f[neg(d)], relaxed[d])
            put(s.at[POS[d], x], 0, jnp.where(inside, v, 0.0))
        put(rho.at[x], 0, total)
        put(fl.at[x], 0, jnp.where(inside & jnp.logical_not(is_solid), 1.0, 0.0))
        p = jnp.where(raw[19, x] > 0.5, 1.0, -1.0)
        put(ph.at[x + 2], ROW0, jnp.where(inside, p, 0.0))
        return carry

    lax.fori_loop(0, NXL, plane, 0)
    inner_step((0, NT - 1), s, rho, fl, ph, fp, red)
    low_a = lax.axis_index("gx") % 2 == 1
    corner_message(xc, 0, low_a, (s, rho, fl, ph, fp, red))
    corner_message((xa, xd), NYL, jnp.logical_not(low_a), (s, rho, fl, ph, fp, red))


def edges():
    gy = lax.axis_index("gy")
    low_edge = gy == 0
    high_edge = gy == lax.axis_size("gy") - 1

    def mask(t):
        y = tile_rows(t)
        if t == 0:
            return (y >= 0) | jnp.logical_not(low_edge)
        if t == NT - 1:
            return (y < NYL) | jnp.logical_not(high_edge)
        return None

    return mask


def put_message(src, base, side, corner, hx, ph):
    near = jnp.where(side == 1, NXL + 2, 1)
    far = jnp.where(side == 1, NXL + 3, 0)
    for j in range(21):
        moved = 2 if corner and j in MOVED else 0
        if corner:
            spans = ((moved, 0, 4), (EXT - 4 - moved, 4, 4))
        else:
            spans = [(4 + 8 * n, 8 * n, 8) for n in range(NYL // 8)]
        for to, part, n in spans:
            v = plane_of(src, j)[pl.ds(base + part, n), :]
            if j in (15, 16):
                ph[near if j == 15 else far, pl.ds(ROW0 + to, n), :] = v
            else:
                hx[j, pl.ds(to, n), :] = v


def put_far(src, side, hx, ph):
    near = jnp.where(side == 1, NXL + 2, 1)
    far = jnp.where(side == 1, NXL + 3, 0)
    for j, row, r in far_spans():
        v = src[pl.ds(row, 8), :]
        if j in (15, 16):
            ph[near if j == 15 else far, pl.ds(ROW0 + 4 + r, 8), :] = v
        else:
            hx[j, pl.ds(4 + r, 8), :] = v


def by_side(side, step):
    for k in (0, 1):
        pl.when(side == k)(lambda: step(k))


def side_dirs(side):
    if side == 0:
        return 0, DIRS[5:10], DIRS[0:5]
    return NXL + 1, DIRS[0:5], DIRS[5:10]


def halo_first(side, hx, ph, fp, red, tiles=range(NT)):
    index, towards, _ = side_dirs(side)
    for t in tiles:
        rows = pl.ds(8 * t, 8)
        finish(
            DIRS, lambda d: hx[towards.index(d), rows, :] if d in towards else None, ph,
            hx[14, rows, :], hx[17, rows, :], index, ROW0 + 8 * t, fp, red,
        )


def halo_collide(side, hx, fp, red, ph, s2, rho2, tiles=range(NT)):
    mask = edges()
    index, towards, back = side_dirs(side)
    near, far = (NXL + 2, NXL + 3) if side == 1 else (1, 0)
    outwards = 1.0 if side == 0 else -1.0
    for t in tiles:
        row = ROW0 + 8 * t
        rows = pl.ds(8 * t, 8)
        f = {d: None if d in towards else arrived(d, fp, index, row) for d in DIRS}
        known = (
            hx[10, rows, :], outwards * hx[11, rows, :], hx[12, rows, :], hx[13, rows, :],
        )
        relaxed, total, _ = collide(f, known)
        rsum = hx[18, rows, :]
        rfar = hx[20, rows, :]
        for g in GROUPS:
            shifted = pl.ds(row - g[1], 8)
            if g[0] != towards[0][0]:
                rsum = rsum + red[GPOS[g], index - g[0], shifted, :]
            if g[0] == back[0][0]:
                rfar = rfar + red[GPOS[g], index, shifted, :]
        ffar = hx[19, rows, :]
        for d in back:
            ffar = ffar + fp[POS[d], index, pl.ds(row - d[1], 8), :]
        p = 2.0 * rsum / total - 1.0
        pfar = 2.0 * rfar / ffar - 1.0
        inside = mask(t)
        if inside is not None:
            p = jnp.where(inside, p, 0.0)
            pfar = jnp.where(inside, pfar, 0.0)
        is_fluid = hx[17, rows, :] > 0.5
        for j, d in enumerate(towards):
            v = jnp.where(is_fluid, relaxed[d] + hx[5 + j, rows, :], f[neg(d)])
            if inside is not None:
                v = jnp.where(inside, v, 0.0)
            s2[POS[d], index, rows, :] = v
        rho2[index, rows, :] = total
        ph[near, pl.ds(row, 8), :] = p
        ph[far, pl.ds(row, 8), :] = pfar


def halo_second(side, hx, s2, rho2, ph, fp, red, tiles=range(NT)):
    index, towards, _ = side_dirs(side)
    for t in tiles:
        rows = pl.ds(8 * t, 8)
        finish(
            towards, lambda d: s2[POS[d], index, rows, :], ph, rho2[index, rows, :],
            hx[17, rows, :], index, ROW0 + 8 * t, fp, red,
        )


def own_finish(x, s, k, rho, fl, ph, fp, red, tiles=range(NT)):
    for t in tiles:
        rows = pl.ds(8 * t, 8)
        finish(
            DIRS, lambda d: s[POS[d], k, rows, :], ph, rho[k, rows, :], fl[x, rows, :],
            x + 1, ROW0 + 8 * t, fp, red,
        )


def own_collide(x, k, fl, fp, red, ph, s2, rho2, tiles=range(NT)):
    mask = edges()
    for t in tiles:
        row = ROW0 + 8 * t
        rows = pl.ds(8 * t, 8)
        f = {d: arrived(d, fp, x + 1, row) for d in DIRS}
        relaxed, total, _ = collide(f)
        p = 2.0 * red_arrived(red, x + 1, row) / total - 1.0
        inside = mask(t)
        if inside is not None:
            p = jnp.where(inside, p, 0.0)
        is_fluid = fl[x, rows, :] > 0.5
        for d in DIRS:
            v = jnp.where(is_fluid, relaxed[d], f[neg(d)])
            if inside is not None:
                v = jnp.where(inside, v, 0.0)
            s2[POS[d], k, rows, :] = v
        rho2[k, rows, :] = total
        ph[x + 2, pl.ds(row, 8), :] = p


def two_planes(side, step):
    def body(k, carry):
        step(jnp.where(side == 1, NXL - 1 - k, k), k)
        return carry

    lax.fori_loop(0, 2, body, 0)


def near_kernel(s, rho, fl, ph_in, fp_in, red_in, xa, xd,
                fp, red, fp2, red2, ph2, s2_next, rho2_next, ph, hx, s2, rho2, own2, orho2):
    side = 1 - lax.axis_index("gx") % 2
    ph[...] = ph_in[...]
    put_message((xa, xd), 0, side, False, hx, ph)
    put_message((xa, xd), NYL, side, True, hx, ph)
    first = jnp.where(side == 1, NXL - 1, 0)
    own_finish(first, s, first, rho, fl, ph, fp, red)
    by_side(side, lambda k: halo_first(k, hx, ph, fp, red))
    two_planes(side, lambda x, k: own_collide(x, k, fl, fp, red, ph2, own2, orho2))
    by_side(side, lambda k: halo_collide(k, hx, fp, red, ph2, s2, rho2))
    own_finish(first, own2, 0, orho2, fl, ph2, fp2, red2)
    by_side(side, lambda k: halo_second(k, hx, s2, rho2, ph2, fp2, red2))
    s2_next[:, 0] = own2[:, 1]
    rho2_next[0] = orho2[1]


def far_half(tiles, s, rho, fl, ph, fp, red, fp2, red2, ph2, s2_next, rho2_next, hx, s2,
             rho2, own2, orho2):
    side = lax.axis_index("gx") % 2
    first = jnp.where(side == 1, NXL - 1, 0)
    third = jnp.where(side == 1, NXL - 3, 2)
    own_finish(first, s, first, rho, fl, ph, fp, red, tiles)
    by_side(side, lambda k: halo_first(k, hx, ph, fp, red, tiles))
    two_planes(side, lambda x, k: own_collide(x, k, fl, fp, red, ph2, own2, orho2, tiles))
    by_side(side, lambda k: halo_collide(k, hx, fp, red, ph2, s2, rho2, tiles))
    own_finish(third, s2_next, 0, rho2_next, fl, ph2, fp2, red2, tiles)
    two_planes(
        side, lambda x, k: own_finish(x, own2, k, orho2, fl, ph2, fp2, red2, tiles)
    )
    by_side(side, lambda k: halo_second(k, hx, s2, rho2, ph2, fp2, red2, tiles))


def move_last(x, starts, fp2, red2, pops_out, phase_out):
    for n, r in enumerate(starts):
        row = ROW0 + 4 + r
        rows = pl.ds(8 * n, 8)
        total = None
        for d in DIRS:
            v = arrived(d, fp2, x + 1, row)
            pops_out[REF_OF[POS[d]], x, rows, :] = v
            total = v if total is None else total + v
        phase_out[x, rows, :] = 2.0 * red_arrived(red2, x + 1, row) / total - 1.0


def far_kernel(s, rho, fl, ph_in, fp_in, red_in, fp2_in, red2_in, ph2_in, s2_next, rho2_next,
               xb, pops_mid, phase_mid, fp, red, fp2, red2, ph, ph2, hx,
               s2, rho2, own2, orho2):
    ph[...] = ph_in[...]
    ph2[...] = ph2_in[...]
    put_far(xb, lax.axis_index("gx") % 2, hx, ph)
    far_half(
        range(NT), s, rho, fl, ph, fp, red, fp2, red2, ph2, s2_next, rho2_next, hx, s2,
        rho2, own2, orho2,
    )
    for x in range(NXL):
        move_last(x, (8, 16), fp2, red2, pops_mid, phase_mid)


def end_kernel(s, rho, fl, s2_next, rho2_next, xc, pops_mid, phase_mid, fp_in, red_in, fp2_in,
               red2_in, ph_in, ph2_in, hx_in, pops_hbm, phase_hbm, fp, red, fp2, red2, ph, ph2,
               hx, s2, rho2, own2, orho2, pops_out, phase_out, sems):
    middle = pl.ds(8, 16)

    def middle_copies(x):
        return (
            pltpu.make_async_copy(
                pops_mid.at[:, x], pops_hbm.at[:, x, middle], sems.at[6 * x]
            ),
            pltpu.make_async_copy(
                phase_mid.at[x], phase_hbm.at[x, middle], sems.at[6 * x + 1]
            ),
        )

    def edge_copies(x):
        out = []
        for n, r in enumerate((0, NYL - 8)):
            part, rows = pl.ds(8 * n, 8), pl.ds(r, 8)
            out += [
                pltpu.make_async_copy(
                    pops_out.at[:, x, part], pops_hbm.at[:, x, rows], sems.at[6 * x + 2 + n]
                ),
                pltpu.make_async_copy(
                    phase_out.at[x, part], phase_hbm.at[x, rows], sems.at[6 * x + 4 + n]
                ),
            ]
        return out

    for x in range(NXL):
        for copy in middle_copies(x):
            copy.start()
    put_message(xc, 0, lax.axis_index("gx") % 2, True, hx, ph)
    far_half(
        (0, NT - 1), s, rho, fl, ph, fp, red, fp2, red2, ph2, s2_next, rho2_next, hx, s2,
        rho2, own2, orho2,
    )
    for x in range(NXL):
        move_last(x, (0, NYL - 8), fp2, red2, pops_out, phase_out)
        for copy in edge_copies(x):
            copy.start()
    for x in range(NXL):
        for copy in (*middle_copies(x), *edge_copies(x)):
            copy.wait()


F32 = jnp.float32
VM = pl.BlockSpec(memory_space=pltpu.VMEM)
HB = pl.BlockSpec(memory_space=pltpu.HBM)
MIB = 1024 * 1024


def shaped(*dims):
    return jax.ShapeDtypeStruct(dims, F32)


def call(kernel, in_specs, outs, scratch, name, aliases=None, vmem=40, cost=0,
         out_specs=None):
    return pl.pallas_call(
        kernel,
        in_specs=in_specs,
        out_specs=out_specs or [VM] * len(outs),
        out_shape=outs,
        scratch_shapes=scratch,
        input_output_aliases=aliases or {},
        compiler_params=pltpu.CompilerParams(vmem_limit_bytes=vmem * MIB),
        cost_estimate=pl.CostEstimate(flops=cost, bytes_accessed=cost, transcendentals=0),
        name=name,
    )


def pairs(count, first):
    out = []
    for i in range(first, count + first, 2):
        a, b = i % count, (i + 1) % count
        out += [(a, b), (b, a)]
    return out


def swap(value, axis, first):
    return lax.ppermute(value, axis, pairs(lax.axis_size(axis), first))


def on_device(populations, labels, solid_mask):
    state = [
        shaped(19, NXL, EXT, 128), shaped(NXL, EXT, 128), shaped(NXL, EXT, 128),
        shaped(NXL + 4, SROWS, 128), shaped(19, NXL + 2, SROWS, 128),
        shaped(9, NXL + 2, SROWS, 128),
    ]
    inputs = [
        pltpu.with_memory_space_constraint(v, pltpu.HBM)
        for v in (populations, labels, solid_mask)
    ]

    split = [shaped(HALF, EXT, 128), shaped(21 - HALF, EXT, 128)]
    whole = [
        shaped(19, NXL, NYL, 128), jax.ShapeDtypeStruct((NXL, NYL, 128), jnp.int32),
        jax.ShapeDtypeStruct((NXL, NYL, 128), jnp.int32),
    ]
    ya, yb, *held = call(
        pack_kernel, [HB] * 3, [shaped(YROWS, 128)] * 2 + whole,
        [pltpu.SemaphoreType.DMA((6,))], "pack",
    )(*inputs)
    ya = swap(ya, "gy", 0)
    yb = swap(yb, "gy", 1)
    *mid, xa, xd, xb = call(
        start_kernel, [VM] * 3, state + split + [shaped(FAR_ROWS, 128)], [], "start",
    )(*held)
    xb = swap(xb, "gx", 1)
    *mid, xa, xd, xc = call(
        edge_kernel, [VM] * 10, state + split + [shaped(21, 8, 128)],
        [pltpu.VMEM((21, NXL, 8, 128), F32)], "edge", {2 + i: i for i in range(8)},
        cost=10 ** 10,
    )(ya, yb, *mid, xa, xd)
    xc = swap(xc, "gx", 1)
    xa = swap(xa, "gx", 0)
    xd = swap(xd, "gx", 0)
    s, rho, fl, ph, fp, red = mid
    halo = [
        pltpu.VMEM((21, EXT, 128), F32), pltpu.VMEM((19, NXL + 2, EXT, 128), F32),
        pltpu.VMEM((NXL + 2, EXT, 128), F32), pltpu.VMEM((19, 2, EXT, 128), F32),
        pltpu.VMEM((2, EXT, 128), F32),
    ]
    phases = pltpu.VMEM((NXL + 4, SROWS, 128), F32)
    fp, red, fp2, red2, ph2, s2_next, rho2_next = call(
        near_kernel, [VM] * 8,
        [state[4], state[5], state[4], state[5], state[3], shaped(19, 1, EXT, 128),
         shaped(1, EXT, 128)],
        [phases] + halo, "near", {4: 0, 5: 1}, cost=0,
    )(s, rho, fl, ph, fp, red, xa, xd)
    held = [state[4], state[5], state[4], state[5], state[3], state[3], shaped(21, EXT, 128)]
    *mids, fp, red, fp2, red2, ph, ph2, hx = call(
        far_kernel, [VM] * 12, [shaped(19, NXL, 16, 128), shaped(NXL, 16, 128)] + held,
        halo[1:], "far", {4: 2, 5: 3, 6: 4, 7: 5},
    )(s, rho, fl, ph, fp, red, fp2, red2, ph2, s2_next, rho2_next, xb)
    out = call(
        end_kernel, [VM] * 15,
        [shaped(19, NXL, NYL, 128), shaped(NXL, NYL, 128)] + held,
        halo[1:] + [
            pltpu.VMEM((19, NXL, 16, 128), F32), pltpu.VMEM((NXL, 16, 128), F32),
            pltpu.SemaphoreType.DMA((6 * NXL,)),
        ],
        "end", {8 + i: 2 + i for i in range(7)}, out_specs=[HB] * 2 + [VM] * 7,
    )(s, rho, fl, s2_next, rho2_next, xc, *mids, fp, red, fp2, red2, ph, ph2, hx)
    return out[0], out[1]


def solution(mesh):
    in_specs = (P(None, "gx", "gy", None), P("gx", "gy", None), P("gx", "gy", None))
    out_specs = (P(None, "gx", "gy", None), P("gx", "gy", None))

    def run(populations, labels, solid_mask):
        new, phase = on_device(populations, labels, solid_mask)
        return new, phase

    return jax.shard_map(
        run, mesh=mesh, in_specs=in_specs, out_specs=out_specs, check_vma=False
    )
```

```python
import jax
import jax.numpy as jnp
import numpy as np
from jax import lax
from jax.experimental import pallas as pl
from jax.experimental.pallas import tpu as pltpu
from jax.sharding import PartitionSpec as P

VELOCITY_SET = [
    (0, 0, 0), (1, 0, 0), (-1, 0, 0), (0, 1, 0), (0, -1, 0), (0, 0, 1), (0, 0, -1),
    (1, 1, 0), (-1, -1, 0), (1, -1, 0), (-1, 1, 0), (1, 0, 1), (-1, 0, -1), (1, 0, -1),
    (-1, 0, 1), (0, 1, 1), (0, -1, -1), (0, 1, -1), (0, -1, 1),
]
DIRS = [
    (-1, 0, 0), (-1, 1, 0), (-1, -1, 0), (-1, 0, 1), (-1, 0, -1),
    (1, 0, 0), (1, 1, 0), (1, -1, 0), (1, 0, 1), (1, 0, -1),
    (0, 0, 0), (0, 1, 0), (0, -1, 0), (0, 0, 1), (0, 0, -1),
    (0, 1, 1), (0, -1, -1), (0, 1, -1), (0, -1, 1),
]
REF_OF = [VELOCITY_SET.index(d) for d in DIRS]
POS = {d: k for k, d in enumerate(DIRS)}
GROUPS = [(-1, 0), (-1, 1), (-1, -1), (1, 0), (1, 1), (1, -1), (0, 0), (0, 1), (0, -1)]
GPOS = {g: k for k, g in enumerate(GROUPS)}
NXL = 4
NYL = 32
EXT = 40
NT = 5
ROW0 = 8
SROWS = 56
HALF = 11
YROWS = 256
W1 = 1.0 / 18.0
W2 = 1.0 / 36.0


def neg(d):
    return (-d[0], -d[1], -d[2])


def zroll(v, shift):
    if shift == 0:
        return v
    return pltpu.roll(v, shift % 128, 1)


def collide(f, known=None, equilibrium=True):
    def pair(a, b):
        pa, pb = f[a], f[b]
        if pb is None:
            return pa, pa
        if pa is None:
            return pb, -pb
        return pa + pb, pa - pb

    s1, d1 = pair((1, 1, 0), (-1, -1, 0))
    s2, d2 = pair((1, -1, 0), (-1, 1, 0))
    xxyy, xy, xyy, xxy = s1 + s2, s1 - s2, d1 + d2, d1 - d2
    s1, d1 = pair((1, 0, 1), (-1, 0, -1))
    s2, d2 = pair((1, 0, -1), (-1, 0, 1))
    xxzz, xz, xzz, xxz = s1 + s2, s1 - s2, d1 + d2, d1 - d2
    s1, d1 = pair((0, 1, 1), (0, -1, -1))
    s2, d2 = pair((0, 1, -1), (0, -1, 1))
    yyzz, yz, yzz, yyz = s1 + s2, s1 - s2, d1 + d2, d1 - d2
    ax, dx = pair((1, 0, 0), (-1, 0, 0))
    ay, dy = pair((0, 1, 0), (0, -1, 0))
    az, dz = pair((0, 0, 1), (0, 0, -1))
    jx = dx + (xyy + xzz)
    jy = dy + (xxy + yzz)
    jz = dz + (xxz + yyz)
    nxx = ax + (xxyy + xxzz)
    nyy = ay + (xxyy + yyzz)
    nzz = az + (xxzz + yyzz)
    rho = (f[(0, 0, 0)] + (ax + ay)) + (az + (xxyy + (xxzz + yyzz)))
    if known is not None:
        rho, jx, jy, jz = rho + known[0], jx + known[1], jy + known[2], jz + known[3]
    dxy, dxz, dyz = 0.3125 * xy, 0.3125 * xz, 0.3125 * yz
    dxyy, dxzz, dxxy = 0.3 * xyy, 0.3 * xzz, 0.3 * xxy
    dyzz, dxxz, dyyz = 0.3 * yzz, 0.3 * xxz, 0.3 * yyz
    dxxyy, dxxzz, dyyzz = 0.35 * xxyy, 0.35 * xxzz, 0.35 * yyzz
    if equilibrium:
        inv = 1.0 / rho
        ux, uy, uz = jx * inv, jy * inv, jz * inv
        qx, qy, qz = jx * ux, jy * uy, jz * uz
        third = rho * (1.0 / 3.0)
        nxx = nxx - (third + qx)
        nyy = nyy - (third + qy)
        nzz = nzz - (third + qz)
        dxy = 0.3125 * (xy - jx * uy)
        dxz = 0.3125 * (xz - jx * uz)
        dyz = 0.3125 * (yz - jy * uz)
        kx, ky, kz = jx * 0.1, jy * 0.1, jz * 0.1
        dxyy, dxzz = dxyy - kx, dxzz - kx
        dxxy, dyzz = dxxy - ky, dyzz - ky
        dxxz, dyyz = dxxz - kz, dyyz - kz
        base = (0.35 / 9.0) * rho + (0.35 / 3.0) * (qx + qy + qz)
        dxxyy = dxxyy - (base - 0.175 * qz)
        dxxzz = dxxzz - (base - 0.175 * qy)
        dyyzz = dyyzz - (base - 0.175 * qx)
    trace = nxx + nyy + nzz
    iso = trace * (-1.0 / 24.0)
    hxx = 0.625 * nxx + iso
    hyy = 0.625 * nyy + iso
    hzz = 0.625 * nzz + iso
    out = {}

    def less(d, v):
        return -v if f[d] is None else f[d] - v

    def diagonal(quad, cross, la, lb, da, db):
        t1, t2 = quad + cross, quad - cross
        v1, v2 = la + lb, la - lb
        out_dirs = []
        for sa, sb in ((1, 1), (-1, -1), (1, -1), (-1, 1)):
            e = tuple(sa * p + sb * q for p, q in zip(da, db))
            out_dirs.append(e)
        out[out_dirs[0]] = less(out_dirs[0], t1 + v1)
        out[out_dirs[1]] = less(out_dirs[1], t1 - v1)
        out[out_dirs[2]] = less(out_dirs[2], t2 + v2)
        out[out_dirs[3]] = less(out_dirs[3], t2 - v2)

    X, Y, Z = (1, 0, 0), (0, 1, 0), (0, 0, 1)
    diagonal(dxxyy, dxy, dxyy, dxxy, X, Y)
    diagonal(dxxzz, dxz, dxzz, dxxz, X, Z)
    diagonal(dyyzz, dyz, dyzz, dyyz, Y, Z)

    def axis(half, q1, q2, l1, l2, d):
        even = half - 2.0 * (q1 + q2)
        odd = 2.0 * (l1 + l2)
        out[d] = less(d, even - odd)
        out[neg(d)] = less(neg(d), even + odd)

    axis(hxx, dxxyy, dxxzz, dxyy, dxzz, X)
    axis(hyy, dxxyy, dyyzz, dxxy, dyzz, Y)
    axis(hzz, dxxzz, dyyzz, dxxz, dyyz, Z)
    out[(0, 0, 0)] = f[(0, 0, 0)] + trace - 4.0 * (dxxyy + dxxzz + dyyzz)
    return out, rho, (jx, jy, jz)


def gradient(ph, plane, row):
    def at(dx, dy):
        return ph[plane + dx, pl.ds(row + dy, 8), :]

    c = at(0, 0)
    xp, xm, yp, ym = at(1, 0), at(-1, 0), at(0, 1), at(0, -1)
    d1 = at(1, 1) - at(-1, -1)
    d2 = at(1, -1) - at(-1, 1)
    ex = xp - xm
    ey = yp - ym
    h = 2.0 * c + ((xp + xm) + (yp + ym))
    k = 1.0 / 12.0
    gx = k * ((2.0 * ex + (d1 + d2)) + (zroll(ex, 1) + zroll(ex, -1)))
    gy = k * ((2.0 * ey + (d1 - d2)) + (zroll(ey, 1) + zroll(ey, -1)))
    gz = k * (zroll(h, -1) - zroll(h, 1))
    return c, gx, gy, gz


def finish(dirs, s_of, ph, rho, fluid, plane, row, fp, red):
    p, gx, gy, gz = gradient(ph, plane + 1, row)
    g2 = gx * gx + gy * gy + gz * gz
    inv = lax.rsqrt(jnp.maximum(g2, 0.01)) * fluid
    h1 = (0.1 * W1) * inv
    h2 = (0.1 * W2) * inv
    cc = (0.175 * rho) * ((1.0 - p * p) * inv)
    c1 = W1 * cc
    c2 = W2 * cc
    frac = 0.5 + 0.5 * p
    comp = (gx, gy, gz)
    sums = {}
    cache = {}
    for d in dirs:
        moving = [k for k in range(3) if d[k] != 0]
        if not moving:
            q, c = h1 * (6.0 * g2), None
        else:
            sign = d[moving[0]]
            key = d if sign > 0 else neg(d)
            if key not in cache:
                if len(moving) == 1:
                    a = comp[moving[0]]
                    cache[key] = (h1 * (a * a - g2), c1 * a)
                else:
                    u, v = moving
                    a = comp[u] + comp[v] if key[v] > 0 else comp[u] - comp[v]
                    cache[key] = (h2 * (a * a - g2), c2 * a)
            q, c = cache[key]
        known = s_of(d)
        val = q if known is None else known + q
        fp[POS[d], plane, pl.ds(row, 8), :] = zroll(val, d[2])
        r = frac * val
        if c is not None:
            r = r + c if sign > 0 else r - c
        r = zroll(r, d[2])
        g = d[:2]
        sums[g] = r if g not in sums else sums[g] + r
    for g, r in sums.items():
        red[GPOS[g], plane, pl.ds(row, 8), :] = r


def arrived(d, fp, plane, row):
    return fp[POS[d], plane - d[0], pl.ds(row - d[1], 8), :]


def red_arrived(red, plane, row):
    total = None
    for g in GROUPS:
        v = red[GPOS[g], plane - g[0], pl.ds(row - g[1], 8), :]
        total = v if total is None else total + v
    return total


def tile_rows(t):
    return lax.broadcasted_iota(jnp.int32, (8, 128), 0) + (8 * t - 4)


def face(high):
    a = jnp.where(high, NXL - 1, 0)
    b = jnp.where(high, NXL - 2, 1)
    c = jnp.where(high, NXL - 3, 2)
    out = jnp.where(high, 5, 0)
    back = jnp.where(high, 0, 5)
    return a, b, c, out, back


def message_tile(high, row, s, rho, fl, ph, fp, red):
    a, b, c, out, back = face(high)
    gout = jnp.where(high, 3, 0)
    gback = jnp.where(high, 0, 3)
    rows = pl.ds(row - ROW0, 8)
    own = pl.ds(row, 8)

    def plain():
        v = [s[out + j, a, rows, :] for j in range(5)]
        return v, [rho[a, rows, :], ph[a + 2, own, :], ph[b + 2, own, :], fl[a, rows, :]]

    def moved():
        f = {}
        total = None
        for j in range(5):
            d = DIRS[5 + j]
            shifted = pl.ds(row - d[1], 8)
            f[d] = fp[out + j, b + 1, shifted, :]
            f[(-1, d[1], d[2])] = None
            v = fp[out + j, c + 1, shifted, :] + fp[back + j, a + 1, shifted, :]
            total = v if total is None else total + v
        for j in range(10, 19):
            shifted = pl.ds(row - DIRS[j][1], 8)
            f[DIRS[j]] = fp[j, a + 1, shifted, :]
            total = total + fp[j, b + 1, shifted, :]
        linear, dens, mom = collide(f, equilibrium=False)
        at_a, at_b = None, None
        for j in range(3):
            shifted = pl.ds(row - GROUPS[j][1], 8)
            v = red[gout + j, b + 1, shifted, :] + red[6 + j, a + 1, shifted, :]
            at_a = v if at_a is None else at_a + v
            v = (red[gout + j, c + 1, shifted, :] + red[gback + j, a + 1, shifted, :]) + red[
                6 + j, b + 1, shifted, :
            ]
            at_b = v if at_b is None else at_b + v
        return [linear[DIRS[5 + j]] for j in range(5)] + [dens, *mom], [at_a, total, at_b]

    return plain, moved


PLAIN = [0, 1, 2, 3, 4, 14, 15, 16, 17]
MOVED = [5, 6, 7, 8, 9, 10, 11, 12, 13, 18, 19, 20]


def plane_of(msg, j):
    if not isinstance(msg, tuple):
        return msg.at[j]
    return msg[0].at[j] if j < HALF else msg[1].at[j - HALF]


def main_message(msg, high, state):
    for n in range(NYL // 8):
        plain, moved = message_tile(high, ROW0 + 4 + 8 * n, *state)
        for kinds, part in ((PLAIN, plain()), (MOVED, moved())):
            for j, v in zip(kinds, part[0] + part[1]):
                plane_of(msg, j)[pl.ds(8 * n, 8), :] = v


def far_spans():
    out = []
    for i, j in enumerate(PLAIN):
        out += [(j, NYL * i + r, r) for r in range(0, NYL, 8)]
    base = NYL * len(PLAIN)
    for i, j in enumerate(MOVED):
        out += [(j, base + (NYL - 4) * i + r - 2, r) for r in (2, 10, 18, 22)]
    return out


FAR_ROWS = NYL * len(PLAIN) + (NYL - 4) * len(MOVED)


def far_message(msg, high, state):
    values = {}
    for r in range(0, NYL, 8):
        part = message_tile(high, ROW0 + 4 + r, *state)[0]()
        values.update({(j, r): v for j, v in zip(PLAIN, part[0] + part[1])})
    for r in (2, 10, 18, 22):
        part = message_tile(high, ROW0 + 4 + r, *state)[1]()
        values.update({(j, r): v for j, v in zip(MOVED, part[0] + part[1])})
    for j, row, r in far_spans():
        msg[pl.ds(row, 8), :] = values[j, r]


def corner_message(msg, base, high, state):
    for n, (first, second) in enumerate(((0, 2), (EXT - 8, EXT - 6))):
        plain, _ = message_tile(high, ROW0 + first, *state)
        _, moved = message_tile(high, ROW0 + second, *state)
        for kinds, part, r in ((PLAIN, plain(), 4 * n), (MOVED, moved(), 0)):
            for j, v in zip(kinds, part[0] + part[1]):
                plane_of(msg, j)[pl.ds(base + 4 * n, 4), :] = v[r:r + 4]


def inner_step(tiles, s, rho, fl, ph, fp, red):
    def plane(x, carry):
        for t in tiles:
            rows = pl.ds(8 * t, 8)
            finish(
                DIRS, lambda d: s[POS[d], x, rows, :], ph, rho[x, rows, :],
                fl[x, rows, :], x + 1, ROW0 + 8 * t, fp, red,
            )
        return carry

    lax.fori_loop(1, NXL - 1, plane, 0)
    for x, base in ((0, 5), (NXL - 1, 0)):
        for t in tiles:
            row = ROW0 + 8 * t
            frac = 0.5 + 0.5 * ph[x + 2, pl.ds(row, 8), :]
            sums = {}
            for d in DIRS[base:base + 5] + DIRS[10:]:
                v = s[POS[d], x, pl.ds(8 * t, 8), :]
                fp[POS[d], x + 1, pl.ds(row, 8), :] = zroll(v, d[2])
                r = zroll(frac * v, d[2])
                sums[d[:2]] = r if d[:2] not in sums else sums[d[:2]] + r
            for g, r in sums.items():
                red[GPOS[g], x + 1, pl.ds(row, 8), :] = r


def pack_kernel(pops_hbm, labels_hbm, solid_hbm, ya, yb, pops, labels, solid, sems):
    odd = lax.axis_index("gy") % 2
    copies = [
        pltpu.make_async_copy(labels_hbm, labels, sems.at[0]),
        pltpu.make_async_copy(solid_hbm, solid, sems.at[1]),
    ] + [
        pltpu.make_async_copy(pops_hbm.at[:, x], pops.at[:, x], sems.at[2 + x])
        for x in range(NXL)
    ]
    for c in copies:
        c.start()

    def pack(out, high, x):
        three = pl.ds(NYL - 3 if high else 0, 3)
        four = pl.ds(NYL - 4 if high else 0, 4)
        for i in range(19):
            out[pl.ds(i * 12 + x * 3, 3), :] = pops[i, x, three, :]
        out[pl.ds(228 + x * 4, 4), :] = labels[x, four, :].astype(jnp.float32)
        out[pl.ds(244 + x * 3, 3), :] = solid[x, three, :].astype(jnp.float32)

    copies[0].wait()
    copies[1].wait()
    for x in range(NXL):
        copies[2 + x].wait()

        @pl.when(odd == 0)
        def _():
            pack(ya, True, x)
            pack(yb, False, x)

        @pl.when(odd == 1)
        def _():
            pack(ya, False, x)
            pack(yb, True, x)


def start_kernel(pops, labels, solid, s, rho, fl, ph, fp, red, xb):
    gy = lax.axis_index("gy")
    low_edge = gy == 0
    high_edge = gy == lax.axis_size("gy") - 1

    def plane(x, carry):
        for t in range(NYL // 8):
            own = pl.ds(8 * t, 8)
            rows = pl.ds(8 * t + 4, 8)
            f = {d: pops[REF_OF[k], x, own, :] for k, d in enumerate(DIRS)}
            is_solid = solid[x, own, :] > 0
            y = lax.broadcasted_iota(jnp.int32, (8, 128), 0) + 8 * t
            if t == 0:
                is_solid = is_solid | ((y == 0) & low_edge)
            if t == NYL // 8 - 1:
                is_solid = is_solid | ((y == NYL - 1) & high_edge)
            relaxed, total, _ = collide(f)
            for d in DIRS:
                s[POS[d], x, rows, :] = jnp.where(is_solid, f[neg(d)], relaxed[d])
            rho[x, rows, :] = total
            fl[x, rows, :] = jnp.where(is_solid, 0.0, 1.0)
            ph[x + 2, pl.ds(ROW0 + 4 + 8 * t, 8), :] = jnp.where(labels[x, own, :] > 0, 1.0, -1.0)
        return carry

    lax.fori_loop(0, NXL, plane, 0)
    inner_step(range(NT), s, rho, fl, ph, fp, red)
    low_a = lax.axis_index("gx") % 2 == 1
    far_message(xb, low_a, (s, rho, fl, ph, fp, red))


def edge_kernel(ya, yb, s_in, rho_in, fl_in, ph_in, fp_in, red_in,
                s, rho, fl, ph, fp, red, xa, xd, xc, raw):
    gy = lax.axis_index("gy")
    odd = gy % 2
    low_edge = gy == 0
    high_edge = gy == lax.axis_size("gy") - 1

    def unpack(src, top):
        r = 1 if top else 4
        for x in range(NXL):
            for i in range(19):
                raw[i, x, pl.ds(r, 3), :] = src[pl.ds(i * 12 + x * 3, 3), :]
            raw[19, x, pl.ds(0 if top else 4, 4), :] = src[pl.ds(228 + x * 4, 4), :]
            raw[20, x, pl.ds(r, 3), :] = src[pl.ds(244 + x * 3, 3), :]

    @pl.when(odd == 0)
    def _():
        unpack(ya, False)
        unpack(yb, True)

    @pl.when(odd == 1)
    def _():
        unpack(ya, True)
        unpack(yb, False)

    row = lax.broadcasted_iota(jnp.int32, (8, 128), 0)
    inside = jnp.where(row < 4, jnp.where(low_edge, 0, 1), jnp.where(high_edge, 0, 1)) > 0

    def plane(x, carry):
        def put(ref, base, v):
            ref[pl.ds(base, 4), :] = v[0:4]
            ref[pl.ds(base + NYL + 4, 4), :] = v[4:8]

        f = {d: raw[REF_OF[k], x] for k, d in enumerate(DIRS)}
        is_solid = raw[20, x] > 0.5
        relaxed, total, _ = collide(f)
        for d in DIRS:
            v = jnp.where(is_solid, f[neg(d)], relaxed[d])
            put(s.at[POS[d], x], 0, jnp.where(inside, v, 0.0))
        put(rho.at[x], 0, total)
        put(fl.at[x], 0, jnp.where(inside & jnp.logical_not(is_solid), 1.0, 0.0))
        p = jnp.where(raw[19, x] > 0.5, 1.0, -1.0)
        put(ph.at[x + 2], ROW0, jnp.where(inside, p, 0.0))
        return carry

    lax.fori_loop(0, NXL, plane, 0)
    inner_step((0, NT - 1), s, rho, fl, ph, fp, red)
    low_a = lax.axis_index("gx") % 2 == 1
    corner_message(xc, 0, low_a, (s, rho, fl, ph, fp, red))
    main_message((xa, xd), jnp.logical_not(low_a), (s, rho, fl, ph, fp, red))
    corner_message((xa, xd), NYL, jnp.logical_not(low_a), (s, rho, fl, ph, fp, red))


def edges():
    gy = lax.axis_index("gy")
    low_edge = gy == 0
    high_edge = gy == lax.axis_size("gy") - 1

    def mask(t):
        y = tile_rows(t)
        if t == 0:
            return (y >= 0) | jnp.logical_not(low_edge)
        if t == NT - 1:
            return (y < NYL) | jnp.logical_not(high_edge)
        return None

    return mask


def put_message(src, base, side, corner, hx, ph):
    near = jnp.where(side == 1, NXL + 2, 1)
    far = jnp.where(side == 1, NXL + 3, 0)
    for j in range(21):
        moved = 2 if corner and j in MOVED else 0
        if corner:
            spans = ((moved, 0, 4), (EXT - 4 - moved, 4, 4))
        else:
            spans = [(4 + 8 * n, 8 * n, 8) for n in range(NYL // 8)]
        for to, part, n in spans:
            v = plane_of(src, j)[pl.ds(base + part, n), :]
            if j in (15, 16):
                ph[near if j == 15 else far, pl.ds(ROW0 + to, n), :] = v
            else:
                hx[j, pl.ds(to, n), :] = v


def put_far(src, side, hx, ph):
    near = jnp.where(side == 1, NXL + 2, 1)
    far = jnp.where(side == 1, NXL + 3, 0)
    for j, row, r in far_spans():
        v = src[pl.ds(row, 8), :]
        if j in (15, 16):
            ph[near if j == 15 else far, pl.ds(ROW0 + 4 + r, 8), :] = v
        else:
            hx[j, pl.ds(4 + r, 8), :] = v


def by_side(side, step):
    for k in (0, 1):
        pl.when(side == k)(lambda: step(k))


def side_dirs(side):
    if side == 0:
        return 0, DIRS[5:10], DIRS[0:5]
    return NXL + 1, DIRS[0:5], DIRS[5:10]


def halo_first(side, hx, ph, fp, red, tiles=range(NT)):
    index, towards, _ = side_dirs(side)
    for t in tiles:
        rows = pl.ds(8 * t, 8)
        finish(
            DIRS, lambda d: hx[towards.index(d), rows, :] if d in towards else None, ph,
            hx[14, rows, :], hx[17, rows, :], index, ROW0 + 8 * t, fp, red,
        )


def halo_collide(side, hx, fp, red, ph, s2, rho2, tiles=range(NT)):
    mask = edges()
    index, towards, back = side_dirs(side)
    near, far = (NXL + 2, NXL + 3) if side == 1 else (1, 0)
    outwards = 1.0 if side == 0 else -1.0
    for t in tiles:
        row = ROW0 + 8 * t
        rows = pl.ds(8 * t, 8)
        f = {d: None if d in towards else arrived(d, fp, index, row) for d in DIRS}
        known = (
            hx[10, rows, :], outwards * hx[11, rows, :], hx[12, rows, :], hx[13, rows, :],
        )
        relaxed, total, _ = collide(f, known)
        rsum = hx[18, rows, :]
        rfar = hx[20, rows, :]
        for g in GROUPS:
            shifted = pl.ds(row - g[1], 8)
            if g[0] != towards[0][0]:
                rsum = rsum + red[GPOS[g], index - g[0], shifted, :]
            if g[0] == back[0][0]:
                rfar = rfar + red[GPOS[g], index, shifted, :]
        ffar = hx[19, rows, :]
        for d in back:
            ffar = ffar + fp[POS[d], index, pl.ds(row - d[1], 8), :]
        p = 2.0 * rsum / total - 1.0
        pfar = 2.0 * rfar / ffar - 1.0
        inside = mask(t)
        if inside is not None:
            p = jnp.where(inside, p, 0.0)
            pfar = jnp.where(inside, pfar, 0.0)
        is_fluid = hx[17, rows, :] > 0.5
        for j, d in enumerate(towards):
            v = jnp.where(is_fluid, relaxed[d] + hx[5 + j, rows, :], f[neg(d)])
            if inside is not None:
                v = jnp.where(inside, v, 0.0)
            s2[POS[d], index, rows, :] = v
        rho2[index, rows, :] = total
        ph[near, pl.ds(row, 8), :] = p
        ph[far, pl.ds(row, 8), :] = pfar


def halo_second(side, hx, s2, rho2, ph, fp, red, tiles=range(NT)):
    index, towards, _ = side_dirs(side)
    for t in tiles:
        rows = pl.ds(8 * t, 8)
        finish(
            towards, lambda d: s2[POS[d], index, rows, :], ph, rho2[index, rows, :],
            hx[17, rows, :], index, ROW0 + 8 * t, fp, red,
        )


def own_finish(x, s, k, rho, fl, ph, fp, red, tiles=range(NT)):
    for t in tiles:
        rows = pl.ds(8 * t, 8)
        finish(
            DIRS, lambda d: s[POS[d], k, rows, :], ph, rho[k, rows, :], fl[x, rows, :],
            x + 1, ROW0 + 8 * t, fp, red,
        )


def own_collide(x, k, fl, fp, red, ph, s2, rho2, tiles=range(NT)):
    mask = edges()
    for t in tiles:
        row = ROW0 + 8 * t
        rows = pl.ds(8 * t, 8)
        f = {d: arrived(d, fp, x + 1, row) for d in DIRS}
        relaxed, total, _ = collide(f)
        p = 2.0 * red_arrived(red, x + 1, row) / total - 1.0
        inside = mask(t)
        if inside is not None:
            p = jnp.where(inside, p, 0.0)
        is_fluid = fl[x, rows, :] > 0.5
        for d in DIRS:
            v = jnp.where(is_fluid, relaxed[d], f[neg(d)])
            if inside is not None:
                v = jnp.where(inside, v, 0.0)
            s2[POS[d], k, rows, :] = v
        rho2[k, rows, :] = total
        ph[x + 2, pl.ds(row, 8), :] = p


def two_planes(side, step):
    def body(k, carry):
        step(jnp.where(side == 1, NXL - 1 - k, k), k)
        return carry

    lax.fori_loop(0, 2, body, 0)


def near_kernel(s, rho, fl, ph_in, fp_in, red_in, xa, xd,
                fp, red, fp2, red2, ph2, s2_next, rho2_next, ph, hx, s2, rho2, own2, orho2):
    side = 1 - lax.axis_index("gx") % 2
    ph[...] = ph_in[...]
    put_message((xa, xd), 0, side, False, hx, ph)
    put_message((xa, xd), NYL, side, True, hx, ph)
    first = jnp.where(side == 1, NXL - 1, 0)
    own_finish(first, s, first, rho, fl, ph, fp, red)
    by_side(side, lambda k: halo_first(k, hx, ph, fp, red))
    two_planes(side, lambda x, k: own_collide(x, k, fl, fp, red, ph2, own2, orho2))
    by_side(side, lambda k: halo_collide(k, hx, fp, red, ph2, s2, rho2))
    own_finish(first, own2, 0, orho2, fl, ph2, fp2, red2)
    by_side(side, lambda k: halo_second(k, hx, s2, rho2, ph2, fp2, red2))
    s2_next[:, 0] = own2[:, 1]
    rho2_next[0] = orho2[1]


def far_half(tiles, s, rho, fl, ph, fp, red, fp2, red2, ph2, s2_next, rho2_next, hx, s2,
             rho2, own2, orho2):
    side = lax.axis_index("gx") % 2
    first = jnp.where(side == 1, NXL - 1, 0)
    third = jnp.where(side == 1, NXL - 3, 2)
    own_finish(first, s, first, rho, fl, ph, fp, red, tiles)
    by_side(side, lambda k: halo_first(k, hx, ph, fp, red, tiles))
    two_planes(side, lambda x, k: own_collide(x, k, fl, fp, red, ph2, own2, orho2, tiles))
    by_side(side, lambda k: halo_collide(k, hx, fp, red, ph2, s2, rho2, tiles))
    own_finish(third, s2_next, 0, rho2_next, fl, ph2, fp2, red2, tiles)
    two_planes(
        side, lambda x, k: own_finish(x, own2, k, orho2, fl, ph2, fp2, red2, tiles)
    )
    by_side(side, lambda k: halo_second(k, hx, s2, rho2, ph2, fp2, red2, tiles))


def move_last(x, starts, fp2, red2, pops_out, phase_out):
    for n, r in enumerate(starts):
        row = ROW0 + 4 + r
        rows = pl.ds(8 * n, 8)
        total = None
        for d in DIRS:
            v = arrived(d, fp2, x + 1, row)
            pops_out[REF_OF[POS[d]], x, rows, :] = v
            total = v if total is None else total + v
        phase_out[x, rows, :] = 2.0 * red_arrived(red2, x + 1, row) / total - 1.0


def far_kernel(s, rho, fl, ph_in, fp_in, red_in, fp2_in, red2_in, ph2_in, s2_next, rho2_next,
               xb, pops_mid, phase_mid, fp, red, fp2, red2, ph, ph2, hx,
               s2, rho2, own2, orho2):
    ph[...] = ph_in[...]
    ph2[...] = ph2_in[...]
    put_far(xb, lax.axis_index("gx") % 2, hx, ph)
    far_half(
        range(NT), s, rho, fl, ph, fp, red, fp2, red2, ph2, s2_next, rho2_next, hx, s2,
        rho2, own2, orho2,
    )
    for x in range(NXL):
        move_last(x, (8, 16), fp2, red2, pops_mid, phase_mid)


def end_kernel(s, rho, fl, s2_next, rho2_next, xc, pops_mid, phase_mid, fp_in, red_in, fp2_in,
               red2_in, ph_in, ph2_in, hx_in, pops_hbm, phase_hbm, fp, red, fp2, red2, ph, ph2,
               hx, s2, rho2, own2, orho2, pops_out, phase_out, sems):
    middle = pl.ds(8, 16)

    def middle_copies(x):
        return (
            pltpu.make_async_copy(
                pops_mid.at[:, x], pops_hbm.at[:, x, middle], sems.at[6 * x]
            ),
            pltpu.make_async_copy(
                phase_mid.at[x], phase_hbm.at[x, middle], sems.at[6 * x + 1]
            ),
        )

    def edge_copies(x):
        out = []
        for n, r in enumerate((0, NYL - 8)):
            part, rows = pl.ds(8 * n, 8), pl.ds(r, 8)
            out += [
                pltpu.make_async_copy(
                    pops_out.at[:, x, part], pops_hbm.at[:, x, rows], sems.at[6 * x + 2 + n]
                ),
                pltpu.make_async_copy(
                    phase_out.at[x, part], phase_hbm.at[x, rows], sems.at[6 * x + 4 + n]
                ),
            ]
        return out

    for x in range(NXL):
        for copy in middle_copies(x):
            copy.start()
    put_message(xc, 0, lax.axis_index("gx") % 2, True, hx, ph)
    far_half(
        (0, NT - 1), s, rho, fl, ph, fp, red, fp2, red2, ph2, s2_next, rho2_next, hx, s2,
        rho2, own2, orho2,
    )
    for x in range(NXL):
        move_last(x, (0, NYL - 8), fp2, red2, pops_out, phase_out)
        for copy in edge_copies(x):
            copy.start()
    for x in range(NXL):
        for copy in (*middle_copies(x), *edge_copies(x)):
            copy.wait()


F32 = jnp.float32
VM = pl.BlockSpec(memory_space=pltpu.VMEM)
HB = pl.BlockSpec(memory_space=pltpu.HBM)
MIB = 1024 * 1024


def shaped(*dims):
    return jax.ShapeDtypeStruct(dims, F32)


def call(kernel, in_specs, outs, scratch, name, aliases=None, vmem=40, cost=0,
         out_specs=None):
    return pl.pallas_call(
        kernel,
        in_specs=in_specs,
        out_specs=out_specs or [VM] * len(outs),
        out_shape=outs,
        scratch_shapes=scratch,
        input_output_aliases=aliases or {},
        compiler_params=pltpu.CompilerParams(vmem_limit_bytes=vmem * MIB),
        cost_estimate=pl.CostEstimate(flops=cost, bytes_accessed=cost, transcendentals=0),
        name=name,
    )


def pairs(count, first):
    out = []
    for i in range(first, count + first, 2):
        a, b = i % count, (i + 1) % count
        out += [(a, b), (b, a)]
    return out


def swap(value, axis, first):
    return lax.ppermute(value, axis, pairs(lax.axis_size(axis), first))


def on_device(populations, labels, solid_mask):
    state = [
        shaped(19, NXL, EXT, 128), shaped(NXL, EXT, 128), shaped(NXL, EXT, 128),
        shaped(NXL + 4, SROWS, 128), shaped(19, NXL + 2, SROWS, 128),
        shaped(9, NXL + 2, SROWS, 128),
    ]
    inputs = [
        pltpu.with_memory_space_constraint(v, pltpu.HBM)
        for v in (populations, labels, solid_mask)
    ]

    split = [shaped(HALF, EXT, 128), shaped(21 - HALF, EXT, 128)]
    whole = [
        shaped(19, NXL, NYL, 128), jax.ShapeDtypeStruct((NXL, NYL, 128), jnp.int32),
        jax.ShapeDtypeStruct((NXL, NYL, 128), jnp.int32),
    ]
    ya, yb, *held = call(
        pack_kernel, [HB] * 3, [shaped(YROWS, 128)] * 2 + whole,
        [pltpu.SemaphoreType.DMA((6,))], "pack",
    )(*inputs)
    ya = swap(ya, "gy", 0)
    yb = swap(yb, "gy", 1)
    *mid, xb = call(
        start_kernel, [VM] * 3, state + [shaped(FAR_ROWS, 128)], [], "start",
    )(*held)
    xb = swap(xb, "gx", 1)
    *mid, xa, xd, xc = call(
        edge_kernel, [VM] * 8, state + split + [shaped(21, 8, 128)],
        [pltpu.VMEM((21, NXL, 8, 128), F32)], "edge", {2 + i: i for i in range(6)},
        cost=10 ** 10,
    )(ya, yb, *mid)
    xc = swap(xc, "gx", 1)
    xa = swap(xa, "gx", 0)
    xd = swap(xd, "gx", 0)
    s, rho, fl, ph, fp, red = mid
    halo = [
        pltpu.VMEM((21, EXT, 128), F32), pltpu.VMEM((19, NXL + 2, EXT, 128), F32),
        pltpu.VMEM((NXL + 2, EXT, 128), F32), pltpu.VMEM((19, 2, EXT, 128), F32),
        pltpu.VMEM((2, EXT, 128), F32),
    ]
    phases = pltpu.VMEM((NXL + 4, SROWS, 128), F32)
    fp, red, fp2, red2, ph2, s2_next, rho2_next = call(
        near_kernel, [VM] * 8,
        [state[4], state[5], state[4], state[5], state[3], shaped(19, 1, EXT, 128),
         shaped(1, EXT, 128)],
        [phases] + halo, "near", {4: 0, 5: 1}, cost=0,
    )(s, rho, fl, ph, fp, red, xa, xd)
    held = [state[4], state[5], state[4], state[5], state[3], state[3], shaped(21, EXT, 128)]
    *mids, fp, red, fp2, red2, ph, ph2, hx = call(
        far_kernel, [VM] * 12, [shaped(19, NXL, 16, 128), shaped(NXL, 16, 128)] + held,
        halo[1:], "far", {4: 2, 5: 3, 6: 4, 7: 5},
    )(s, rho, fl, ph, fp, red, fp2, red2, ph2, s2_next, rho2_next, xb)
    out = call(
        end_kernel, [VM] * 15,
        [shaped(19, NXL, NYL, 128), shaped(NXL, NYL, 128)] + held,
        halo[1:] + [
            pltpu.VMEM((19, NXL, 16, 128), F32), pltpu.VMEM((NXL, 16, 128), F32),
            pltpu.SemaphoreType.DMA((6 * NXL,)),
        ],
        "end", {8 + i: 2 + i for i in range(7)}, out_specs=[HB] * 2 + [VM] * 7,
    )(s, rho, fl, s2_next, rho2_next, xc, *mids, fp, red, fp2, red2, ph, ph2, hx)
    return out[0], out[1]


def solution(mesh):
    in_specs = (P(None, "gx", "gy", None), P("gx", "gy", None), P("gx", "gy", None))
    out_specs = (P(None, "gx", "gy", None), P("gx", "gy", None))

    def run(populations, labels, solid_mask):
        new, phase = on_device(populations, labels, solid_mask)
        return new, phase

    return jax.shard_map(
        run, mesh=mesh, in_specs=in_specs, out_specs=out_specs, check_vma=False
    )
```

```python
import jax
import jax.numpy as jnp
import numpy as np
from jax import lax
from jax.experimental import pallas as pl
from jax.experimental.pallas import tpu as pltpu
from jax.sharding import PartitionSpec as P

VELOCITY_SET = [
    (0, 0, 0), (1, 0, 0), (-1, 0, 0), (0, 1, 0), (0, -1, 0), (0, 0, 1), (0, 0, -1),
    (1, 1, 0), (-1, -1, 0), (1, -1, 0), (-1, 1, 0), (1, 0, 1), (-1, 0, -1), (1, 0, -1),
    (-1, 0, 1), (0, 1, 1), (0, -1, -1), (0, 1, -1), (0, -1, 1),
]
DIRS = [
    (-1, 0, 0), (-1, 1, 0), (-1, -1, 0), (-1, 0, 1), (-1, 0, -1),
    (1, 0, 0), (1, 1, 0), (1, -1, 0), (1, 0, 1), (1, 0, -1),
    (0, 0, 0), (0, 1, 0), (0, -1, 0), (0, 0, 1), (0, 0, -1),
    (0, 1, 1), (0, -1, -1), (0, 1, -1), (0, -1, 1),
]
REF_OF = [VELOCITY_SET.index(d) for d in DIRS]
POS = {d: k for k, d in enumerate(DIRS)}
GROUPS = [(-1, 0), (-1, 1), (-1, -1), (1, 0), (1, 1), (1, -1), (0, 0), (0, 1), (0, -1)]
GPOS = {g: k for k, g in enumerate(GROUPS)}
NXL = 4
NYL = 32
EXT = 40
NT = 5
ROW0 = 8
SROWS = 56
HALF = 11
YROWS = 256
W1 = 1.0 / 18.0
W2 = 1.0 / 36.0


def neg(d):
    return (-d[0], -d[1], -d[2])


def zroll(v, shift):
    if shift == 0:
        return v
    return pltpu.roll(v, shift % 128, 1)


def collide(f, known=None, equilibrium=True):
    def pair(a, b):
        pa, pb = f[a], f[b]
        if pb is None:
            return pa, pa
        if pa is None:
            return pb, -pb
        return pa + pb, pa - pb

    s1, d1 = pair((1, 1, 0), (-1, -1, 0))
    s2, d2 = pair((1, -1, 0), (-1, 1, 0))
    xxyy, xy, xyy, xxy = s1 + s2, s1 - s2, d1 + d2, d1 - d2
    s1, d1 = pair((1, 0, 1), (-1, 0, -1))
    s2, d2 = pair((1, 0, -1), (-1, 0, 1))
    xxzz, xz, xzz, xxz = s1 + s2, s1 - s2, d1 + d2, d1 - d2
    s1, d1 = pair((0, 1, 1), (0, -1, -1))
    s2, d2 = pair((0, 1, -1), (0, -1, 1))
    yyzz, yz, yzz, yyz = s1 + s2, s1 - s2, d1 + d2, d1 - d2
    ax, dx = pair((1, 0, 0), (-1, 0, 0))
    ay, dy = pair((0, 1, 0), (0, -1, 0))
    az, dz = pair((0, 0, 1), (0, 0, -1))
    jx = dx + (xyy + xzz)
    jy = dy + (xxy + yzz)
    jz = dz + (xxz + yyz)
    nxx = ax + (xxyy + xxzz)
    nyy = ay + (xxyy + yyzz)
    nzz = az + (xxzz + yyzz)
    rho = (f[(0, 0, 0)] + (ax + ay)) + (az + (xxyy + (xxzz + yyzz)))
    if known is not None:
        rho, jx, jy, jz = rho + known[0], jx + known[1], jy + known[2], jz + known[3]
    dxy, dxz, dyz = 0.3125 * xy, 0.3125 * xz, 0.3125 * yz
    dxyy, dxzz, dxxy = 0.3 * xyy, 0.3 * xzz, 0.3 * xxy
    dyzz, dxxz, dyyz = 0.3 * yzz, 0.3 * xxz, 0.3 * yyz
    dxxyy, dxxzz, dyyzz = 0.35 * xxyy, 0.35 * xxzz, 0.35 * yyzz
    if equilibrium:
        inv = 1.0 / rho
        ux, uy, uz = jx * inv, jy * inv, jz * inv
        qx, qy, qz = jx * ux, jy * uy, jz * uz
        third = rho * (1.0 / 3.0)
        nxx = nxx - (third + qx)
        nyy = nyy - (third + qy)
        nzz = nzz - (third + qz)
        dxy = 0.3125 * (xy - jx * uy)
        dxz = 0.3125 * (xz - jx * uz)
        dyz = 0.3125 * (yz - jy * uz)
        kx, ky, kz = jx * 0.1, jy * 0.1, jz * 0.1
        dxyy, dxzz = dxyy - kx, dxzz - kx
        dxxy, dyzz = dxxy - ky, dyzz - ky
        dxxz, dyyz = dxxz - kz, dyyz - kz
        base = (0.35 / 9.0) * rho + (0.35 / 3.0) * (qx + qy + qz)
        dxxyy = dxxyy - (base - 0.175 * qz)
        dxxzz = dxxzz - (base - 0.175 * qy)
        dyyzz = dyyzz - (base - 0.175 * qx)
    trace = nxx + nyy + nzz
    iso = trace * (-1.0 / 24.0)
    hxx = 0.625 * nxx + iso
    hyy = 0.625 * nyy + iso
    hzz = 0.625 * nzz + iso
    out = {}

    def less(d, v):
        return -v if f[d] is None else f[d] - v

    def diagonal(quad, cross, la, lb, da, db):
        t1, t2 = quad + cross, quad - cross
        v1, v2 = la + lb, la - lb
        out_dirs = []
        for sa, sb in ((1, 1), (-1, -1), (1, -1), (-1, 1)):
            e = tuple(sa * p + sb * q for p, q in zip(da, db))
            out_dirs.append(e)
        out[out_dirs[0]] = less(out_dirs[0], t1 + v1)
        out[out_dirs[1]] = less(out_dirs[1], t1 - v1)
        out[out_dirs[2]] = less(out_dirs[2], t2 + v2)
        out[out_dirs[3]] = less(out_dirs[3], t2 - v2)

    X, Y, Z = (1, 0, 0), (0, 1, 0), (0, 0, 1)
    diagonal(dxxyy, dxy, dxyy, dxxy, X, Y)
    diagonal(dxxzz, dxz, dxzz, dxxz, X, Z)
    diagonal(dyyzz, dyz, dyzz, dyyz, Y, Z)

    def axis(half, q1, q2, l1, l2, d):
        even = half - 2.0 * (q1 + q2)
        odd = 2.0 * (l1 + l2)
        out[d] = less(d, even - odd)
        out[neg(d)] = less(neg(d), even + odd)

    axis(hxx, dxxyy, dxxzz, dxyy, dxzz, X)
    axis(hyy, dxxyy, dyyzz, dxxy, dyzz, Y)
    axis(hzz, dxxzz, dyyzz, dxxz, dyyz, Z)
    out[(0, 0, 0)] = f[(0, 0, 0)] + trace - 4.0 * (dxxyy + dxxzz + dyyzz)
    return out, rho, (jx, jy, jz)


def gradient(ph, plane, row):
    def at(dx, dy):
        return ph[plane + dx, pl.ds(row + dy, 8), :]

    c = at(0, 0)
    xp, xm, yp, ym = at(1, 0), at(-1, 0), at(0, 1), at(0, -1)
    d1 = at(1, 1) - at(-1, -1)
    d2 = at(1, -1) - at(-1, 1)
    ex = xp - xm
    ey = yp - ym
    h = 2.0 * c + ((xp + xm) + (yp + ym))
    k = 1.0 / 12.0
    gx = k * ((2.0 * ex + (d1 + d2)) + (zroll(ex, 1) + zroll(ex, -1)))
    gy = k * ((2.0 * ey + (d1 - d2)) + (zroll(ey, 1) + zroll(ey, -1)))
    gz = k * (zroll(h, -1) - zroll(h, 1))
    return c, gx, gy, gz


def finish(dirs, s_of, ph, rho, fluid, plane, row, fp, red):
    p, gx, gy, gz = gradient(ph, plane + 1, row)
    g2 = gx * gx + gy * gy + gz * gz
    inv = lax.rsqrt(jnp.maximum(g2, 0.01)) * fluid
    h1 = (0.1 * W1) * inv
    h2 = (0.1 * W2) * inv
    cc = (0.175 * rho) * ((1.0 - p * p) * inv)
    c1 = W1 * cc
    c2 = W2 * cc
    frac = 0.5 + 0.5 * p
    comp = (gx, gy, gz)
    sums = {}
    cache = {}
    for d in dirs:
        moving = [k for k in range(3) if d[k] != 0]
        if not moving:
            q, c = h1 * (6.0 * g2), None
        else:
            sign = d[moving[0]]
            key = d if sign > 0 else neg(d)
            if key not in cache:
                if len(moving) == 1:
                    a = comp[moving[0]]
                    cache[key] = (h1 * (a * a - g2), c1 * a)
                else:
                    u, v = moving
                    a = comp[u] + comp[v] if key[v] > 0 else comp[u] - comp[v]
                    cache[key] = (h2 * (a * a - g2), c2 * a)
            q, c = cache[key]
        known = s_of(d)
        val = q if known is None else known + q
        fp[POS[d], plane, pl.ds(row, 8), :] = zroll(val, d[2])
        r = frac * val
        if c is not None:
            r = r + c if sign > 0 else r - c
        r = zroll(r, d[2])
        g = d[:2]
        sums[g] = r if g not in sums else sums[g] + r
    for g, r in sums.items():
        red[GPOS[g], plane, pl.ds(row, 8), :] = r


def arrived(d, fp, plane, row):
    return fp[POS[d], plane - d[0], pl.ds(row - d[1], 8), :]


def red_arrived(red, plane, row):
    total = None
    for g in GROUPS:
        v = red[GPOS[g], plane - g[0], pl.ds(row - g[1], 8), :]
        total = v if total is None else total + v
    return total


def tile_rows(t):
    return lax.broadcasted_iota(jnp.int32, (8, 128), 0) + (8 * t - 4)


def face(high):
    a = jnp.where(high, NXL - 1, 0)
    b = jnp.where(high, NXL - 2, 1)
    c = jnp.where(high, NXL - 3, 2)
    out = jnp.where(high, 5, 0)
    back = jnp.where(high, 0, 5)
    return a, b, c, out, back


def message_tile(high, row, s, rho, fl, ph, fp, red):
    a, b, c, out, back = face(high)
    gout = jnp.where(high, 3, 0)
    gback = jnp.where(high, 0, 3)
    rows = pl.ds(row - ROW0, 8)
    own = pl.ds(row, 8)

    def plain():
        v = [s[out + j, a, rows, :] for j in range(5)]
        return v, [rho[a, rows, :], ph[a + 2, own, :], ph[b + 2, own, :], fl[a, rows, :]]

    def moved():
        f = {}
        total = None
        for j in range(5):
            d = DIRS[5 + j]
            shifted = pl.ds(row - d[1], 8)
            f[d] = fp[out + j, b + 1, shifted, :]
            f[(-1, d[1], d[2])] = None
            v = fp[out + j, c + 1, shifted, :] + fp[back + j, a + 1, shifted, :]
            total = v if total is None else total + v
        for j in range(10, 19):
            shifted = pl.ds(row - DIRS[j][1], 8)
            f[DIRS[j]] = fp[j, a + 1, shifted, :]
            total = total + fp[j, b + 1, shifted, :]
        linear, dens, mom = collide(f, equilibrium=False)
        at_a, at_b = None, None
        for j in range(3):
            shifted = pl.ds(row - GROUPS[j][1], 8)
            v = red[gout + j, b + 1, shifted, :] + red[6 + j, a + 1, shifted, :]
            at_a = v if at_a is None else at_a + v
            v = (red[gout + j, c + 1, shifted, :] + red[gback + j, a + 1, shifted, :]) + red[
                6 + j, b + 1, shifted, :
            ]
            at_b = v if at_b is None else at_b + v
        return [linear[DIRS[5 + j]] for j in range(5)] + [dens, *mom], [at_a, total, at_b]

    return plain, moved


PLAIN = [0, 1, 2, 3, 4, 14, 15, 16, 17]
MOVED = [5, 6, 7, 8, 9, 10, 11, 12, 13, 18, 19, 20]


def plane_of(msg, j):
    if not isinstance(msg, tuple):
        return msg.at[j]
    return msg[0].at[j] if j < HALF else msg[1].at[j - HALF]


def main_message(msg, high, state):
    for n in range(NYL // 8):
        plain, moved = message_tile(high, ROW0 + 4 + 8 * n, *state)
        for kinds, part in ((PLAIN, plain()), (MOVED, moved())):
            for j, v in zip(kinds, part[0] + part[1]):
                plane_of(msg, j)[pl.ds(8 * n, 8), :] = v


def corner_spans():
    out, at = [], 0
    for j in range(21):
        if j in (15, 16):
            rows = ((0, 4), (EXT - 4, 4))
        elif j in PLAIN:
            rows = ((1, 3), (EXT - 4, 3))
        elif j in (10, 18, 19, 20):
            rows = ((2, 4), (EXT - 6, 4))
        else:
            rows = ((3, 3), (EXT - 6, 3))
        for end, (row, n) in enumerate(rows):
            out.append((j, end, at, row, n))
            at += n
    return out, at


CORNER_ROWS = corner_spans()[1]


def far_corner(msg, high, state):
    values = {}
    for end, (first, second) in enumerate(((0, 2), (EXT - 8, EXT - 6))):
        part = message_tile(high, ROW0 + first, *state)[0]()
        values.update({(j, end): (v, first) for j, v in zip(PLAIN, part[0] + part[1])})
        part = message_tile(high, ROW0 + second, *state)[1]()
        values.update({(j, end): (v, second) for j, v in zip(MOVED, part[0] + part[1])})
    for j, end, at, row, n in corner_spans()[0]:
        v, first = values[j, end]
        msg[pl.ds(at, n), :] = v[row - first:row - first + n]


def put_corner(src, side, hx, ph):
    near = jnp.where(side == 1, NXL + 2, 1)
    far = jnp.where(side == 1, NXL + 3, 0)
    for j, _, at, row, n in corner_spans()[0]:
        v = src[pl.ds(at, n), :]
        if j in (15, 16):
            ph[near if j == 15 else far, pl.ds(ROW0 + row, n), :] = v
        else:
            hx[j, pl.ds(row, n), :] = v


def far_spans():
    out = []
    for i, j in enumerate(PLAIN):
        out += [(j, NYL * i + r, r) for r in range(0, NYL, 8)]
    base = NYL * len(PLAIN)
    for i, j in enumerate(MOVED):
        out += [(j, base + (NYL - 4) * i + r - 2, r) for r in (2, 10, 18, 22)]
    return out


FAR_ROWS = NYL * len(PLAIN) + (NYL - 4) * len(MOVED)


def far_message(msg, high, state):
    values = {}
    for r in range(0, NYL, 8):
        part = message_tile(high, ROW0 + 4 + r, *state)[0]()
        values.update({(j, r): v for j, v in zip(PLAIN, part[0] + part[1])})
    for r in (2, 10, 18, 22):
        part = message_tile(high, ROW0 + 4 + r, *state)[1]()
        values.update({(j, r): v for j, v in zip(MOVED, part[0] + part[1])})
    for j, row, r in far_spans():
        msg[pl.ds(row, 8), :] = values[j, r]


def corner_message(msg, base, high, state):
    for n, (first, second) in enumerate(((0, 2), (EXT - 8, EXT - 6))):
        plain, _ = message_tile(high, ROW0 + first, *state)
        _, moved = message_tile(high, ROW0 + second, *state)
        for kinds, part, r in ((PLAIN, plain(), 4 * n), (MOVED, moved(), 0)):
            for j, v in zip(kinds, part[0] + part[1]):
                plane_of(msg, j)[pl.ds(base + 4 * n, 4), :] = v[r:r + 4]


def inner_step(tiles, s, rho, fl, ph, fp, red):
    def plane(x, carry):
        for t in tiles:
            rows = pl.ds(8 * t, 8)
            finish(
                DIRS, lambda d: s[POS[d], x, rows, :], ph, rho[x, rows, :],
                fl[x, rows, :], x + 1, ROW0 + 8 * t, fp, red,
            )
        return carry

    lax.fori_loop(1, NXL - 1, plane, 0)
    for x, base in ((0, 5), (NXL - 1, 0)):
        for t in tiles:
            row = ROW0 + 8 * t
            frac = 0.5 + 0.5 * ph[x + 2, pl.ds(row, 8), :]
            sums = {}
            for d in DIRS[base:base + 5] + DIRS[10:]:
                v = s[POS[d], x, pl.ds(8 * t, 8), :]
                fp[POS[d], x + 1, pl.ds(row, 8), :] = zroll(v, d[2])
                r = zroll(frac * v, d[2])
                sums[d[:2]] = r if d[:2] not in sums else sums[d[:2]] + r
            for g, r in sums.items():
                red[GPOS[g], x + 1, pl.ds(row, 8), :] = r


def pack_kernel(pops_hbm, labels_hbm, solid_hbm, ya, yb, pops, labels, solid, sems):
    odd = lax.axis_index("gy") % 2
    copies = [
        pltpu.make_async_copy(labels_hbm, labels, sems.at[0]),
        pltpu.make_async_copy(solid_hbm, solid, sems.at[1]),
    ] + [
        pltpu.make_async_copy(pops_hbm.at[:, x], pops.at[:, x], sems.at[2 + x])
        for x in range(NXL)
    ]
    for c in copies:
        c.start()

    def pack(out, high, x):
        three = pl.ds(NYL - 3 if high else 0, 3)
        four = pl.ds(NYL - 4 if high else 0, 4)
        for i in range(19):
            out[pl.ds(i * 12 + x * 3, 3), :] = pops[i, x, three, :]
        out[pl.ds(228 + x * 4, 4), :] = labels[x, four, :].astype(jnp.float32)
        out[pl.ds(244 + x * 3, 3), :] = solid[x, three, :].astype(jnp.float32)

    copies[0].wait()
    copies[1].wait()
    for x in range(NXL):
        copies[2 + x].wait()

        @pl.when(odd == 0)
        def _():
            pack(ya, True, x)
            pack(yb, False, x)

        @pl.when(odd == 1)
        def _():
            pack(ya, False, x)
            pack(yb, True, x)


def start_kernel(pops, labels, solid, s, rho, fl, ph, fp, red, xb):
    gy = lax.axis_index("gy")
    low_edge = gy == 0
    high_edge = gy == lax.axis_size("gy") - 1

    def plane(x, carry):
        for t in range(NYL // 8):
            own = pl.ds(8 * t, 8)
            rows = pl.ds(8 * t + 4, 8)
            f = {d: pops[REF_OF[k], x, own, :] for k, d in enumerate(DIRS)}
            is_solid = solid[x, own, :] > 0
            y = lax.broadcasted_iota(jnp.int32, (8, 128), 0) + 8 * t
            if t == 0:
                is_solid = is_solid | ((y == 0) & low_edge)
            if t == NYL // 8 - 1:
                is_solid = is_solid | ((y == NYL - 1) & high_edge)
            relaxed, total, _ = collide(f)
            for d in DIRS:
                s[POS[d], x, rows, :] = jnp.where(is_solid, f[neg(d)], relaxed[d])
            rho[x, rows, :] = total
            fl[x, rows, :] = jnp.where(is_solid, 0.0, 1.0)
            ph[x + 2, pl.ds(ROW0 + 4 + 8 * t, 8), :] = jnp.where(labels[x, own, :] > 0, 1.0, -1.0)
        return carry

    lax.fori_loop(0, NXL, plane, 0)
    inner_step(range(NT), s, rho, fl, ph, fp, red)
    low_a = lax.axis_index("gx") % 2 == 1
    far_message(xb, low_a, (s, rho, fl, ph, fp, red))


def edge_kernel(ya, yb, s_in, rho_in, fl_in, ph_in, fp_in, red_in,
                s, rho, fl, ph, fp, red, xa, xd, xc, raw):
    gy = lax.axis_index("gy")
    odd = gy % 2
    low_edge = gy == 0
    high_edge = gy == lax.axis_size("gy") - 1

    def unpack(src, top):
        r = 1 if top else 4
        for x in range(NXL):
            for i in range(19):
                raw[i, x, pl.ds(r, 3), :] = src[pl.ds(i * 12 + x * 3, 3), :]
            raw[19, x, pl.ds(0 if top else 4, 4), :] = src[pl.ds(228 + x * 4, 4), :]
            raw[20, x, pl.ds(r, 3), :] = src[pl.ds(244 + x * 3, 3), :]

    @pl.when(odd == 0)
    def _():
        unpack(ya, False)
        unpack(yb, True)

    @pl.when(odd == 1)
    def _():
        unpack(ya, True)
        unpack(yb, False)

    row = lax.broadcasted_iota(jnp.int32, (8, 128), 0)
    inside = jnp.where(row < 4, jnp.where(low_edge, 0, 1), jnp.where(high_edge, 0, 1)) > 0

    def plane(x, carry):
        def put(ref, base, v):
            ref[pl.ds(base, 4), :] = v[0:4]
            ref[pl.ds(base + NYL + 4, 4), :] = v[4:8]

        f = {d: raw[REF_OF[k], x] for k, d in enumerate(DIRS)}
        is_solid = raw[20, x] > 0.5
        relaxed, total, _ = collide(f)
        for d in DIRS:
            v = jnp.where(is_solid, f[neg(d)], relaxed[d])
            put(s.at[POS[d], x], 0, jnp.where(inside, v, 0.0))
        put(rho.at[x], 0, total)
        put(fl.at[x], 0, jnp.where(inside & jnp.logical_not(is_solid), 1.0, 0.0))
        p = jnp.where(raw[19, x] > 0.5, 1.0, -1.0)
        put(ph.at[x + 2], ROW0, jnp.where(inside, p, 0.0))
        return carry

    lax.fori_loop(0, NXL, plane, 0)
    inner_step((0, NT - 1), s, rho, fl, ph, fp, red)
    low_a = lax.axis_index("gx") % 2 == 1
    far_corner(xc, low_a, (s, rho, fl, ph, fp, red))
    main_message((xa, xd), jnp.logical_not(low_a), (s, rho, fl, ph, fp, red))
    corner_message((xa, xd), NYL, jnp.logical_not(low_a), (s, rho, fl, ph, fp, red))


def edges():
    gy = lax.axis_index("gy")
    low_edge = gy == 0
    high_edge = gy == lax.axis_size("gy") - 1

    def mask(t):
        y = tile_rows(t)
        if t == 0:
            return (y >= 0) | jnp.logical_not(low_edge)
        if t == NT - 1:
            return (y < NYL) | jnp.logical_not(high_edge)
        return None

    return mask


def put_message(src, base, side, corner, hx, ph):
    near = jnp.where(side == 1, NXL + 2, 1)
    far = jnp.where(side == 1, NXL + 3, 0)
    for j in range(21):
        moved = 2 if corner and j in MOVED else 0
        if corner:
            spans = ((moved, 0, 4), (EXT - 4 - moved, 4, 4))
        else:
            spans = [(4 + 8 * n, 8 * n, 8) for n in range(NYL // 8)]
        for to, part, n in spans:
            v = plane_of(src, j)[pl.ds(base + part, n), :]
            if j in (15, 16):
                ph[near if j == 15 else far, pl.ds(ROW0 + to, n), :] = v
            else:
                hx[j, pl.ds(to, n), :] = v


def put_far(src, side, hx, ph):
    near = jnp.where(side == 1, NXL + 2, 1)
    far = jnp.where(side == 1, NXL + 3, 0)
    for j, row, r in far_spans():
        v = src[pl.ds(row, 8), :]
        if j in (15, 16):
            ph[near if j == 15 else far, pl.ds(ROW0 + 4 + r, 8), :] = v
        else:
            hx[j, pl.ds(4 + r, 8), :] = v


def by_side(side, step):
    for k in (0, 1):
        pl.when(side == k)(lambda: step(k))


def side_dirs(side):
    if side == 0:
        return 0, DIRS[5:10], DIRS[0:5]
    return NXL + 1, DIRS[0:5], DIRS[5:10]


def halo_first(side, hx, ph, fp, red, tiles=range(NT)):
    index, towards, _ = side_dirs(side)
    for t in tiles:
        rows = pl.ds(8 * t, 8)
        finish(
            DIRS, lambda d: hx[towards.index(d), rows, :] if d in towards else None, ph,
            hx[14, rows, :], hx[17, rows, :], index, ROW0 + 8 * t, fp, red,
        )


def halo_collide(side, hx, fp, red, ph, s2, rho2, tiles=range(NT)):
    mask = edges()
    index, towards, back = side_dirs(side)
    near, far = (NXL + 2, NXL + 3) if side == 1 else (1, 0)
    outwards = 1.0 if side == 0 else -1.0
    for t in tiles:
        row = ROW0 + 8 * t
        rows = pl.ds(8 * t, 8)
        f = {d: None if d in towards else arrived(d, fp, index, row) for d in DIRS}
        known = (
            hx[10, rows, :], outwards * hx[11, rows, :], hx[12, rows, :], hx[13, rows, :],
        )
        relaxed, total, _ = collide(f, known)
        rsum = hx[18, rows, :]
        rfar = hx[20, rows, :]
        for g in GROUPS:
            shifted = pl.ds(row - g[1], 8)
            if g[0] != towards[0][0]:
                rsum = rsum + red[GPOS[g], index - g[0], shifted, :]
            if g[0] == back[0][0]:
                rfar = rfar + red[GPOS[g], index, shifted, :]
        ffar = hx[19, rows, :]
        for d in back:
            ffar = ffar + fp[POS[d], index, pl.ds(row - d[1], 8), :]
        p = 2.0 * rsum / total - 1.0
        pfar = 2.0 * rfar / ffar - 1.0
        inside = mask(t)
        if inside is not None:
            p = jnp.where(inside, p, 0.0)
            pfar = jnp.where(inside, pfar, 0.0)
        is_fluid = hx[17, rows, :] > 0.5
        for j, d in enumerate(towards):
            v = jnp.where(is_fluid, relaxed[d] + hx[5 + j, rows, :], f[neg(d)])
            if inside is not None:
                v = jnp.where(inside, v, 0.0)
            s2[POS[d], index, rows, :] = v
        rho2[index, rows, :] = total
        ph[near, pl.ds(row, 8), :] = p
        ph[far, pl.ds(row, 8), :] = pfar


def halo_second(side, hx, s2, rho2, ph, fp, red, tiles=range(NT)):
    index, towards, _ = side_dirs(side)
    for t in tiles:
        rows = pl.ds(8 * t, 8)
        finish(
            towards, lambda d: s2[POS[d], index, rows, :], ph, rho2[index, rows, :],
            hx[17, rows, :], index, ROW0 + 8 * t, fp, red,
        )


def own_finish(x, s, k, rho, fl, ph, fp, red, tiles=range(NT)):
    for t in tiles:
        rows = pl.ds(8 * t, 8)
        finish(
            DIRS, lambda d: s[POS[d], k, rows, :], ph, rho[k, rows, :], fl[x, rows, :],
            x + 1, ROW0 + 8 * t, fp, red,
        )


def own_collide(x, k, fl, fp, red, ph, s2, rho2, tiles=range(NT)):
    mask = edges()
    for t in tiles:
        row = ROW0 + 8 * t
        rows = pl.ds(8 * t, 8)
        f = {d: arrived(d, fp, x + 1, row) for d in DIRS}
        relaxed, total, _ = collide(f)
        p = 2.0 * red_arrived(red, x + 1, row) / total - 1.0
        inside = mask(t)
        if inside is not None:
            p = jnp.where(inside, p, 0.0)
        is_fluid = fl[x, rows, :] > 0.5
        for d in DIRS:
            v = jnp.where(is_fluid, relaxed[d], f[neg(d)])
            if inside is not None:
                v = jnp.where(inside, v, 0.0)
            s2[POS[d], k, rows, :] = v
        rho2[k, rows, :] = total
        ph[x + 2, pl.ds(row, 8), :] = p


def two_planes(side, step):
    def body(k, carry):
        step(jnp.where(side == 1, NXL - 1 - k, k), k)
        return carry

    lax.fori_loop(0, 2, body, 0)


def near_kernel(s, rho, fl, ph_in, fp_in, red_in, xa, xd,
                fp, red, fp2, red2, ph2, s2_next, rho2_next, ph, hx, s2, rho2, own2, orho2):
    side = 1 - lax.axis_index("gx") % 2
    ph[...] = ph_in[...]
    put_message((xa, xd), 0, side, False, hx, ph)
    put_message((xa, xd), NYL, side, True, hx, ph)
    first = jnp.where(side == 1, NXL - 1, 0)
    own_finish(first, s, first, rho, fl, ph, fp, red)
    by_side(side, lambda k: halo_first(k, hx, ph, fp, red))
    two_planes(side, lambda x, k: own_collide(x, k, fl, fp, red, ph2, own2, orho2))
    by_side(side, lambda k: halo_collide(k, hx, fp, red, ph2, s2, rho2))
    own_finish(first, own2, 0, orho2, fl, ph2, fp2, red2)
    by_side(side, lambda k: halo_second(k, hx, s2, rho2, ph2, fp2, red2))
    s2_next[:, 0] = own2[:, 1]
    rho2_next[0] = orho2[1]


def far_half(tiles, s, rho, fl, ph, fp, red, fp2, red2, ph2, s2_next, rho2_next, hx, s2,
             rho2, own2, orho2):
    side = lax.axis_index("gx") % 2
    first = jnp.where(side == 1, NXL - 1, 0)
    third = jnp.where(side == 1, NXL - 3, 2)
    own_finish(first, s, first, rho, fl, ph, fp, red, tiles)
    by_side(side, lambda k: halo_first(k, hx, ph, fp, red, tiles))
    two_planes(side, lambda x, k: own_collide(x, k, fl, fp, red, ph2, own2, orho2, tiles))
    by_side(side, lambda k: halo_collide(k, hx, fp, red, ph2, s2, rho2, tiles))
    own_finish(third, s2_next, 0, rho2_next, fl, ph2, fp2, red2, tiles)
    two_planes(
        side, lambda x, k: own_finish(x, own2, k, orho2, fl, ph2, fp2, red2, tiles)
    )
    by_side(side, lambda k: halo_second(k, hx, s2, rho2, ph2, fp2, red2, tiles))


def move_last(x, starts, fp2, red2, pops_out, phase_out):
    for n, r in enumerate(starts):
        row = ROW0 + 4 + r
        rows = pl.ds(8 * n, 8)
        total = None
        for d in DIRS:
            v = arrived(d, fp2, x + 1, row)
            pops_out[REF_OF[POS[d]], x, rows, :] = v
            total = v if total is None else total + v
        phase_out[x, rows, :] = 2.0 * red_arrived(red2, x + 1, row) / total - 1.0


def far_kernel(s, rho, fl, ph_in, fp_in, red_in, fp2_in, red2_in, ph2_in, s2_next, rho2_next,
               xb, pops_mid, phase_mid, fp, red, fp2, red2, ph, ph2, hx,
               s2, rho2, own2, orho2):
    ph[...] = ph_in[...]
    ph2[...] = ph2_in[...]
    put_far(xb, lax.axis_index("gx") % 2, hx, ph)
    far_half(
        range(NT), s, rho, fl, ph, fp, red, fp2, red2, ph2, s2_next, rho2_next, hx, s2,
        rho2, own2, orho2,
    )
    for x in range(NXL):
        move_last(x, (8, 16), fp2, red2, pops_mid, phase_mid)


def end_kernel(s, rho, fl, s2_next, rho2_next, xc, pops_mid, phase_mid, fp_in, red_in, fp2_in,
               red2_in, ph_in, ph2_in, hx_in, pops_hbm, phase_hbm, fp, red, fp2, red2, ph, ph2,
               hx, s2, rho2, own2, orho2, pops_out, phase_out, sems):
    middle = pl.ds(8, 16)

    def middle_copies(x):
        return (
            pltpu.make_async_copy(
                pops_mid.at[:, x], pops_hbm.at[:, x, middle], sems.at[6 * x]
            ),
            pltpu.make_async_copy(
                phase_mid.at[x], phase_hbm.at[x, middle], sems.at[6 * x + 1]
            ),
        )

    def edge_copies(x):
        out = []
        for n, r in enumerate((0, NYL - 8)):
            part, rows = pl.ds(8 * n, 8), pl.ds(r, 8)
            out += [
                pltpu.make_async_copy(
                    pops_out.at[:, x, part], pops_hbm.at[:, x, rows], sems.at[6 * x + 2 + n]
                ),
                pltpu.make_async_copy(
                    phase_out.at[x, part], phase_hbm.at[x, rows], sems.at[6 * x + 4 + n]
                ),
            ]
        return out

    for x in range(NXL):
        for copy in middle_copies(x):
            copy.start()
    put_corner(xc, lax.axis_index("gx") % 2, hx, ph)
    far_half(
        (0, NT - 1), s, rho, fl, ph, fp, red, fp2, red2, ph2, s2_next, rho2_next, hx, s2,
        rho2, own2, orho2,
    )
    for x in range(NXL):
        move_last(x, (0, NYL - 8), fp2, red2, pops_out, phase_out)
        for copy in edge_copies(x):
            copy.start()
    for x in range(NXL):
        for copy in (*middle_copies(x), *edge_copies(x)):
            copy.wait()


F32 = jnp.float32
VM = pl.BlockSpec(memory_space=pltpu.VMEM)
HB = pl.BlockSpec(memory_space=pltpu.HBM)
MIB = 1024 * 1024


def shaped(*dims):
    return jax.ShapeDtypeStruct(dims, F32)


def call(kernel, in_specs, outs, scratch, name, aliases=None, vmem=40, cost=0,
         out_specs=None):
    return pl.pallas_call(
        kernel,
        in_specs=in_specs,
        out_specs=out_specs or [VM] * len(outs),
        out_shape=outs,
        scratch_shapes=scratch,
        input_output_aliases=aliases or {},
        compiler_params=pltpu.CompilerParams(vmem_limit_bytes=vmem * MIB),
        cost_estimate=pl.CostEstimate(flops=cost, bytes_accessed=cost, transcendentals=0),
        name=name,
    )


def pairs(count, first):
    out = []
    for i in range(first, count + first, 2):
        a, b = i % count, (i + 1) % count
        out += [(a, b), (b, a)]
    return out


def swap(value, axis, first):
    return lax.ppermute(value, axis, pairs(lax.axis_size(axis), first))


def on_device(populations, labels, solid_mask):
    state = [
        shaped(19, NXL, EXT, 128), shaped(NXL, EXT, 128), shaped(NXL, EXT, 128),
        shaped(NXL + 4, SROWS, 128), shaped(19, NXL + 2, SROWS, 128),
        shaped(9, NXL + 2, SROWS, 128),
    ]
    inputs = [
        pltpu.with_memory_space_constraint(v, pltpu.HBM)
        for v in (populations, labels, solid_mask)
    ]

    split = [shaped(HALF, EXT, 128), shaped(21 - HALF, EXT, 128)]
    whole = [
        shaped(19, NXL, NYL, 128), jax.ShapeDtypeStruct((NXL, NYL, 128), jnp.int32),
        jax.ShapeDtypeStruct((NXL, NYL, 128), jnp.int32),
    ]
    ya, yb, *held = call(
        pack_kernel, [HB] * 3, [shaped(YROWS, 128)] * 2 + whole,
        [pltpu.SemaphoreType.DMA((6,))], "pack",
    )(*inputs)
    ya = swap(ya, "gy", 0)
    yb = swap(yb, "gy", 1)
    *mid, xb = call(
        start_kernel, [VM] * 3, state + [shaped(FAR_ROWS, 128)], [], "start",
    )(*held)
    xb = swap(xb, "gx", 1)
    *mid, xa, xd, xc = call(
        edge_kernel, [VM] * 8, state + split + [shaped(CORNER_ROWS, 128)],
        [pltpu.VMEM((21, NXL, 8, 128), F32)], "edge", {2 + i: i for i in range(6)},
        cost=10 ** 10,
    )(ya, yb, *mid)
    xc = swap(xc, "gx", 1)
    xa = swap(xa, "gx", 0)
    xd = swap(xd, "gx", 0)
    s, rho, fl, ph, fp, red = mid
    halo = [
        pltpu.VMEM((21, EXT, 128), F32), pltpu.VMEM((19, NXL + 2, EXT, 128), F32),
        pltpu.VMEM((NXL + 2, EXT, 128), F32), pltpu.VMEM((19, 2, EXT, 128), F32),
        pltpu.VMEM((2, EXT, 128), F32),
    ]
    phases = pltpu.VMEM((NXL + 4, SROWS, 128), F32)
    fp, red, fp2, red2, ph2, s2_next, rho2_next = call(
        near_kernel, [VM] * 8,
        [state[4], state[5], state[4], state[5], state[3], shaped(19, 1, EXT, 128),
         shaped(1, EXT, 128)],
        [phases] + halo, "near", {4: 0, 5: 1}, cost=0,
    )(s, rho, fl, ph, fp, red, xa, xd)
    held = [state[4], state[5], state[4], state[5], state[3], state[3], shaped(21, EXT, 128)]
    *mids, fp, red, fp2, red2, ph, ph2, hx = call(
        far_kernel, [VM] * 12, [shaped(19, NXL, 16, 128), shaped(NXL, 16, 128)] + held,
        halo[1:], "far", {4: 2, 5: 3, 6: 4, 7: 5},
    )(s, rho, fl, ph, fp, red, fp2, red2, ph2, s2_next, rho2_next, xb)
    out = call(
        end_kernel, [VM] * 15,
        [shaped(19, NXL, NYL, 128), shaped(NXL, NYL, 128)] + held,
        halo[1:] + [
            pltpu.VMEM((19, NXL, 16, 128), F32), pltpu.VMEM((NXL, 16, 128), F32),
            pltpu.SemaphoreType.DMA((6 * NXL,)),
        ],
        "end", {8 + i: 2 + i for i in range(7)}, out_specs=[HB] * 2 + [VM] * 7,
    )(s, rho, fl, s2_next, rho2_next, xc, *mids, fp, red, fp2, red2, ph, ph2, hx)
    return out[0], out[1]


def solution(mesh):
    in_specs = (P(None, "gx", "gy", None), P("gx", "gy", None), P("gx", "gy", None))
    out_specs = (P(None, "gx", "gy", None), P("gx", "gy", None))

    def run(populations, labels, solid_mask):
        new, phase = on_device(populations, labels, solid_mask)
        return new, phase

    return jax.shard_map(
        run, mesh=mesh, in_specs=in_specs, out_specs=out_specs, check_vma=False
    )
```

```python
import jax
import jax.numpy as jnp
import numpy as np
from jax import lax
from jax.experimental import pallas as pl
from jax.experimental.pallas import tpu as pltpu
from jax.sharding import PartitionSpec as P

VELOCITY_SET = [
    (0, 0, 0), (1, 0, 0), (-1, 0, 0), (0, 1, 0), (0, -1, 0), (0, 0, 1), (0, 0, -1),
    (1, 1, 0), (-1, -1, 0), (1, -1, 0), (-1, 1, 0), (1, 0, 1), (-1, 0, -1), (1, 0, -1),
    (-1, 0, 1), (0, 1, 1), (0, -1, -1), (0, 1, -1), (0, -1, 1),
]
DIRS = [
    (-1, 0, 0), (-1, 1, 0), (-1, -1, 0), (-1, 0, 1), (-1, 0, -1),
    (1, 0, 0), (1, 1, 0), (1, -1, 0), (1, 0, 1), (1, 0, -1),
    (0, 0, 0), (0, 1, 0), (0, -1, 0), (0, 0, 1), (0, 0, -1),
    (0, 1, 1), (0, -1, -1), (0, 1, -1), (0, -1, 1),
]
REF_OF = [VELOCITY_SET.index(d) for d in DIRS]
POS = {d: k for k, d in enumerate(DIRS)}
GROUPS = [(-1, 0), (-1, 1), (-1, -1), (1, 0), (1, 1), (1, -1), (0, 0), (0, 1), (0, -1)]
GPOS = {g: k for k, g in enumerate(GROUPS)}
NXL = 4
NYL = 32
EXT = 40
NT = 5
ROW0 = 8
SROWS = 56
HALF = 11
YROWS = 256
W1 = 1.0 / 18.0
W2 = 1.0 / 36.0


def neg(d):
    return (-d[0], -d[1], -d[2])


def zroll(v, shift):
    if shift == 0:
        return v
    return pltpu.roll(v, shift % 128, 1)


def collide(f, known=None, equilibrium=True):
    def pair(a, b):
        pa, pb = f[a], f[b]
        if pb is None:
            return pa, pa
        if pa is None:
            return pb, -pb
        return pa + pb, pa - pb

    s1, d1 = pair((1, 1, 0), (-1, -1, 0))
    s2, d2 = pair((1, -1, 0), (-1, 1, 0))
    xxyy, xy, xyy, xxy = s1 + s2, s1 - s2, d1 + d2, d1 - d2
    s1, d1 = pair((1, 0, 1), (-1, 0, -1))
    s2, d2 = pair((1, 0, -1), (-1, 0, 1))
    xxzz, xz, xzz, xxz = s1 + s2, s1 - s2, d1 + d2, d1 - d2
    s1, d1 = pair((0, 1, 1), (0, -1, -1))
    s2, d2 = pair((0, 1, -1), (0, -1, 1))
    yyzz, yz, yzz, yyz = s1 + s2, s1 - s2, d1 + d2, d1 - d2
    ax, dx = pair((1, 0, 0), (-1, 0, 0))
    ay, dy = pair((0, 1, 0), (0, -1, 0))
    az, dz = pair((0, 0, 1), (0, 0, -1))
    jx = dx + (xyy + xzz)
    jy = dy + (xxy + yzz)
    jz = dz + (xxz + yyz)
    nxx = ax + (xxyy + xxzz)
    nyy = ay + (xxyy + yyzz)
    nzz = az + (xxzz + yyzz)
    rho = (f[(0, 0, 0)] + (ax + ay)) + (az + (xxyy + (xxzz + yyzz)))
    if known is not None:
        rho, jx, jy, jz = rho + known[0], jx + known[1], jy + known[2], jz + known[3]
    dxy, dxz, dyz = 0.3125 * xy, 0.3125 * xz, 0.3125 * yz
    dxyy, dxzz, dxxy = 0.3 * xyy, 0.3 * xzz, 0.3 * xxy
    dyzz, dxxz, dyyz = 0.3 * yzz, 0.3 * xxz, 0.3 * yyz
    dxxyy, dxxzz, dyyzz = 0.35 * xxyy, 0.35 * xxzz, 0.35 * yyzz
    if equilibrium:
        inv = 1.0 / rho
        ux, uy, uz = jx * inv, jy * inv, jz * inv
        qx, qy, qz = jx * ux, jy * uy, jz * uz
        third = rho * (1.0 / 3.0)
        nxx = nxx - (third + qx)
        nyy = nyy - (third + qy)
        nzz = nzz - (third + qz)
        dxy = 0.3125 * (xy - jx * uy)
        dxz = 0.3125 * (xz - jx * uz)
        dyz = 0.3125 * (yz - jy * uz)
        kx, ky, kz = jx * 0.1, jy * 0.1, jz * 0.1
        dxyy, dxzz = dxyy - kx, dxzz - kx
        dxxy, dyzz = dxxy - ky, dyzz - ky
        dxxz, dyyz = dxxz - kz, dyyz - kz
        base = (0.35 / 9.0) * rho + (0.35 / 3.0) * (qx + qy + qz)
        dxxyy = dxxyy - (base - 0.175 * qz)
        dxxzz = dxxzz - (base - 0.175 * qy)
        dyyzz = dyyzz - (base - 0.175 * qx)
    trace = nxx + nyy + nzz
    iso = trace * (-1.0 / 24.0)
    hxx = 0.625 * nxx + iso
    hyy = 0.625 * nyy + iso
    hzz = 0.625 * nzz + iso
    out = {}

    def less(d, v):
        return -v if f[d] is None else f[d] - v

    def diagonal(quad, cross, la, lb, da, db):
        t1, t2 = quad + cross, quad - cross
        v1, v2 = la + lb, la - lb
        out_dirs = []
        for sa, sb in ((1, 1), (-1, -1), (1, -1), (-1, 1)):
            e = tuple(sa * p + sb * q for p, q in zip(da, db))
            out_dirs.append(e)
        out[out_dirs[0]] = less(out_dirs[0], t1 + v1)
        out[out_dirs[1]] = less(out_dirs[1], t1 - v1)
        out[out_dirs[2]] = less(out_dirs[2], t2 + v2)
        out[out_dirs[3]] = less(out_dirs[3], t2 - v2)

    X, Y, Z = (1, 0, 0), (0, 1, 0), (0, 0, 1)
    diagonal(dxxyy, dxy, dxyy, dxxy, X, Y)
    diagonal(dxxzz, dxz, dxzz, dxxz, X, Z)
    diagonal(dyyzz, dyz, dyzz, dyyz, Y, Z)

    def axis(half, q1, q2, l1, l2, d):
        even = half - 2.0 * (q1 + q2)
        odd = 2.0 * (l1 + l2)
        out[d] = less(d, even - odd)
        out[neg(d)] = less(neg(d), even + odd)

    axis(hxx, dxxyy, dxxzz, dxyy, dxzz, X)
    axis(hyy, dxxyy, dyyzz, dxxy, dyzz, Y)
    axis(hzz, dxxzz, dyyzz, dxxz, dyyz, Z)
    out[(0, 0, 0)] = f[(0, 0, 0)] + trace - 4.0 * (dxxyy + dxxzz + dyyzz)
    return out, rho, (jx, jy, jz)


def gradient(ph, plane, row):
    def at(dx, dy):
        return ph[plane + dx, pl.ds(row + dy, 8), :]

    c = at(0, 0)
    xp, xm, yp, ym = at(1, 0), at(-1, 0), at(0, 1), at(0, -1)
    d1 = at(1, 1) - at(-1, -1)
    d2 = at(1, -1) - at(-1, 1)
    ex = xp - xm
    ey = yp - ym
    h = 2.0 * c + ((xp + xm) + (yp + ym))
    k = 1.0 / 12.0
    gx = k * ((2.0 * ex + (d1 + d2)) + (zroll(ex, 1) + zroll(ex, -1)))
    gy = k * ((2.0 * ey + (d1 - d2)) + (zroll(ey, 1) + zroll(ey, -1)))
    gz = k * (zroll(h, -1) - zroll(h, 1))
    return c, gx, gy, gz


def finish(dirs, s_of, ph, rho, fluid, plane, row, fp, red):
    p, gx, gy, gz = gradient(ph, plane + 1, row)
    g2 = gx * gx + gy * gy + gz * gz
    inv = lax.rsqrt(jnp.maximum(g2, 0.01)) * fluid
    h1 = (0.1 * W1) * inv
    h2 = (0.1 * W2) * inv
    cc = (0.175 * rho) * ((1.0 - p * p) * inv)
    c1 = W1 * cc
    c2 = W2 * cc
    frac = 0.5 + 0.5 * p
    comp = (gx, gy, gz)
    sums = {}
    cache = {}
    for d in dirs:
        moving = [k for k in range(3) if d[k] != 0]
        if not moving:
            q, c = h1 * (6.0 * g2), None
        else:
            sign = d[moving[0]]
            key = d if sign > 0 else neg(d)
            if key not in cache:
                if len(moving) == 1:
                    a = comp[moving[0]]
                    cache[key] = (h1 * (a * a - g2), c1 * a)
                else:
                    u, v = moving
                    a = comp[u] + comp[v] if key[v] > 0 else comp[u] - comp[v]
                    cache[key] = (h2 * (a * a - g2), c2 * a)
            q, c = cache[key]
        known = s_of(d)
        val = q if known is None else known + q
        fp[POS[d], plane, pl.ds(row, 8), :] = zroll(val, d[2])
        r = frac * val
        if c is not None:
            r = r + c if sign > 0 else r - c
        r = zroll(r, d[2])
        g = d[:2]
        sums[g] = r if g not in sums else sums[g] + r
    for g, r in sums.items():
        red[GPOS[g], plane, pl.ds(row, 8), :] = r


def arrived(d, fp, plane, row):
    return fp[POS[d], plane - d[0], pl.ds(row - d[1], 8), :]


def red_arrived(red, plane, row):
    total = None
    for g in GROUPS:
        v = red[GPOS[g], plane - g[0], pl.ds(row - g[1], 8), :]
        total = v if total is None else total + v
    return total


def tile_rows(t):
    return lax.broadcasted_iota(jnp.int32, (8, 128), 0) + (8 * t - 4)


def face(high):
    a = jnp.where(high, NXL - 1, 0)
    b = jnp.where(high, NXL - 2, 1)
    c = jnp.where(high, NXL - 3, 2)
    out = jnp.where(high, 5, 0)
    back = jnp.where(high, 0, 5)
    return a, b, c, out, back


def message_tile(high, row, s, rho, fl, ph, fp, red):
    a, b, c, out, back = face(high)
    gout = jnp.where(high, 3, 0)
    gback = jnp.where(high, 0, 3)
    rows = pl.ds(row - ROW0, 8)
    own = pl.ds(row, 8)

    def plain():
        v = [s[out + j, a, rows, :] for j in range(5)]
        return v, [rho[a, rows, :], ph[a + 2, own, :], ph[b + 2, own, :], fl[a, rows, :]]

    def moved():
        f = {}
        total = None
        for j in range(5):
            d = DIRS[5 + j]
            shifted = pl.ds(row - d[1], 8)
            f[d] = fp[out + j, b + 1, shifted, :]
            f[(-1, d[1], d[2])] = None
            v = fp[out + j, c + 1, shifted, :] + fp[back + j, a + 1, shifted, :]
            total = v if total is None else total + v
        for j in range(10, 19):
            shifted = pl.ds(row - DIRS[j][1], 8)
            f[DIRS[j]] = fp[j, a + 1, shifted, :]
            total = total + fp[j, b + 1, shifted, :]
        linear, dens, mom = collide(f, equilibrium=False)
        at_a, at_b = None, None
        for j in range(3):
            shifted = pl.ds(row - GROUPS[j][1], 8)
            v = red[gout + j, b + 1, shifted, :] + red[6 + j, a + 1, shifted, :]
            at_a = v if at_a is None else at_a + v
            v = (red[gout + j, c + 1, shifted, :] + red[gback + j, a + 1, shifted, :]) + red[
                6 + j, b + 1, shifted, :
            ]
            at_b = v if at_b is None else at_b + v
        return [linear[DIRS[5 + j]] for j in range(5)] + [dens, *mom], [at_a, total, at_b]

    return plain, moved


PLAIN = [0, 1, 2, 3, 4, 14, 15, 16, 17]
MOVED = [5, 6, 7, 8, 9, 10, 11, 12, 13, 18, 19, 20]


def plane_of(msg, j):
    if not isinstance(msg, tuple):
        return msg.at[j]
    return msg[0].at[j] if j < HALF else msg[1].at[j - HALF]


def main_message(msg, high, state):
    for n in range(NYL // 8):
        plain, moved = message_tile(high, ROW0 + 4 + 8 * n, *state)
        for kinds, part in ((PLAIN, plain()), (MOVED, moved())):
            for j, v in zip(kinds, part[0] + part[1]):
                plane_of(msg, j)[pl.ds(8 * n, 8), :] = v


def corner_spans():
    out, at = [], 0
    for j in range(21):
        if j in (15, 16):
            rows = ((0, 4), (EXT - 4, 4))
        elif j in PLAIN:
            rows = ((1, 3), (EXT - 4, 3))
        elif j in (10, 18, 19, 20):
            rows = ((2, 4), (EXT - 6, 4))
        else:
            rows = ((3, 3), (EXT - 6, 3))
        for end, (row, n) in enumerate(rows):
            out.append((j, end, at, row, n))
            at += n
    return out, at


CORNER_ROWS = corner_spans()[1]


def far_corner(msg, high, state):
    values = {}
    for end, (first, second) in enumerate(((0, 2), (EXT - 8, EXT - 6))):
        part = message_tile(high, ROW0 + first, *state)[0]()
        values.update({(j, end): (v, first) for j, v in zip(PLAIN, part[0] + part[1])})
        part = message_tile(high, ROW0 + second, *state)[1]()
        values.update({(j, end): (v, second) for j, v in zip(MOVED, part[0] + part[1])})
    for j, end, at, row, n in corner_spans()[0]:
        v, first = values[j, end]
        msg[pl.ds(at, n), :] = v[row - first:row - first + n]


def put_corner(src, side, hx, ph):
    near = jnp.where(side == 1, NXL + 2, 1)
    far = jnp.where(side == 1, NXL + 3, 0)
    for j, _, at, row, n in corner_spans()[0]:
        v = src[pl.ds(at, n), :]
        if j in (15, 16):
            ph[near if j == 15 else far, pl.ds(ROW0 + row, n), :] = v
        else:
            hx[j, pl.ds(row, n), :] = v


def far_spans():
    out = []
    for i, j in enumerate(PLAIN):
        out += [(j, NYL * i + r, r) for r in range(0, NYL, 8)]
    base = NYL * len(PLAIN)
    for i, j in enumerate(MOVED):
        out += [(j, base + (NYL - 4) * i + r - 2, r) for r in (2, 10, 18, 22)]
    return out


FAR_ROWS = NYL * len(PLAIN) + (NYL - 4) * len(MOVED)


def far_message(msg, high, state):
    values = {}
    for r in range(0, NYL, 8):
        part = message_tile(high, ROW0 + 4 + r, *state)[0]()
        values.update({(j, r): v for j, v in zip(PLAIN, part[0] + part[1])})
    for r in (2, 10, 18, 22):
        part = message_tile(high, ROW0 + 4 + r, *state)[1]()
        values.update({(j, r): v for j, v in zip(MOVED, part[0] + part[1])})
    for j, row, r in far_spans():
        msg[pl.ds(row, 8), :] = values[j, r]


def corner_message(msg, base, high, state):
    for n, (first, second) in enumerate(((0, 2), (EXT - 8, EXT - 6))):
        plain, _ = message_tile(high, ROW0 + first, *state)
        _, moved = message_tile(high, ROW0 + second, *state)
        for kinds, part, r in ((PLAIN, plain(), 4 * n), (MOVED, moved(), 0)):
            for j, v in zip(kinds, part[0] + part[1]):
                plane_of(msg, j)[pl.ds(base + 4 * n, 4), :] = v[r:r + 4]


def inner_step(tiles, s, rho, fl, ph, fp, red):
    def plane(x, carry):
        for t in tiles:
            rows = pl.ds(8 * t, 8)
            finish(
                DIRS, lambda d: s[POS[d], x, rows, :], ph, rho[x, rows, :],
                fl[x, rows, :], x + 1, ROW0 + 8 * t, fp, red,
            )
        return carry

    lax.fori_loop(1, NXL - 1, plane, 0)
    for x, base in ((0, 5), (NXL - 1, 0)):
        for t in tiles:
            row = ROW0 + 8 * t
            frac = 0.5 + 0.5 * ph[x + 2, pl.ds(row, 8), :]
            sums = {}
            for d in DIRS[base:base + 5] + DIRS[10:]:
                v = s[POS[d], x, pl.ds(8 * t, 8), :]
                fp[POS[d], x + 1, pl.ds(row, 8), :] = zroll(v, d[2])
                r = zroll(frac * v, d[2])
                sums[d[:2]] = r if d[:2] not in sums else sums[d[:2]] + r
            for g, r in sums.items():
                red[GPOS[g], x + 1, pl.ds(row, 8), :] = r


def pack_kernel(pops_hbm, labels_hbm, solid_hbm, ya, yb, pops, labels, solid, sems):
    odd = lax.axis_index("gy") % 2
    copies = [
        pltpu.make_async_copy(labels_hbm, labels, sems.at[0]),
        pltpu.make_async_copy(solid_hbm, solid, sems.at[1]),
    ] + [
        pltpu.make_async_copy(pops_hbm.at[:, x], pops.at[:, x], sems.at[2 + x])
        for x in range(NXL)
    ]
    for c in copies:
        c.start()

    def pack(out, high, x):
        three = pl.ds(NYL - 3 if high else 0, 3)
        four = pl.ds(NYL - 4 if high else 0, 4)
        for i in range(19):
            out[pl.ds(i * 12 + x * 3, 3), :] = pops[i, x, three, :]
        out[pl.ds(228 + x * 4, 4), :] = labels[x, four, :].astype(jnp.float32)
        out[pl.ds(244 + x * 3, 3), :] = solid[x, three, :].astype(jnp.float32)

    copies[0].wait()
    copies[1].wait()
    for x in range(NXL):
        copies[2 + x].wait()

        @pl.when(odd == 0)
        def _():
            pack(ya, True, x)
            pack(yb, False, x)

        @pl.when(odd == 1)
        def _():
            pack(ya, False, x)
            pack(yb, True, x)


def start_kernel(pops, labels, solid, s, rho, fl, ph, fp, red, xb):
    gy = lax.axis_index("gy")
    low_edge = gy == 0
    high_edge = gy == lax.axis_size("gy") - 1

    def plane(x, carry):
        for t in range(NYL // 8):
            own = pl.ds(8 * t, 8)
            rows = pl.ds(8 * t + 4, 8)
            f = {d: pops[REF_OF[k], x, own, :] for k, d in enumerate(DIRS)}
            is_solid = solid[x, own, :] > 0
            y = lax.broadcasted_iota(jnp.int32, (8, 128), 0) + 8 * t
            if t == 0:
                is_solid = is_solid | ((y == 0) & low_edge)
            if t == NYL // 8 - 1:
                is_solid = is_solid | ((y == NYL - 1) & high_edge)
            relaxed, total, _ = collide(f)
            for d in DIRS:
                s[POS[d], x, rows, :] = jnp.where(is_solid, f[neg(d)], relaxed[d])
            rho[x, rows, :] = total
            fl[x, rows, :] = jnp.where(is_solid, 0.0, 1.0)
            ph[x + 2, pl.ds(ROW0 + 4 + 8 * t, 8), :] = jnp.where(labels[x, own, :] > 0, 1.0, -1.0)
        return carry

    lax.fori_loop(0, NXL, plane, 0)
    inner_step(range(NT), s, rho, fl, ph, fp, red)
    low_a = lax.axis_index("gx") % 2 == 1
    far_message(xb, low_a, (s, rho, fl, ph, fp, red))


def edge_kernel(yb, ya, s_in, rho_in, fl_in, ph_in, fp_in, red_in,
                s, rho, fl, ph, fp, red, xa, xd, xc, raw):
    gy = lax.axis_index("gy")
    odd = gy % 2
    low_edge = gy == 0
    high_edge = gy == lax.axis_size("gy") - 1

    def unpack(src, top):
        r = 1 if top else 4
        for x in range(NXL):
            for i in range(19):
                raw[i, x, pl.ds(r, 3), :] = src[pl.ds(i * 12 + x * 3, 3), :]
            raw[19, x, pl.ds(0 if top else 4, 4), :] = src[pl.ds(228 + x * 4, 4), :]
            raw[20, x, pl.ds(r, 3), :] = src[pl.ds(244 + x * 3, 3), :]

    @pl.when(odd == 0)
    def _():
        unpack(ya, False)
        unpack(yb, True)

    @pl.when(odd == 1)
    def _():
        unpack(ya, True)
        unpack(yb, False)

    row = lax.broadcasted_iota(jnp.int32, (8, 128), 0)
    inside = jnp.where(row < 4, jnp.where(low_edge, 0, 1), jnp.where(high_edge, 0, 1)) > 0

    def plane(x, carry):
        def put(ref, base, v):
            ref[pl.ds(base, 4), :] = v[0:4]
            ref[pl.ds(base + NYL + 4, 4), :] = v[4:8]

        f = {d: raw[REF_OF[k], x] for k, d in enumerate(DIRS)}
        is_solid = raw[20, x] > 0.5
        relaxed, total, _ = collide(f)
        for d in DIRS:
            v = jnp.where(is_solid, f[neg(d)], relaxed[d])
            put(s.at[POS[d], x], 0, jnp.where(inside, v, 0.0))
        put(rho.at[x], 0, total)
        put(fl.at[x], 0, jnp.where(inside & jnp.logical_not(is_solid), 1.0, 0.0))
        p = jnp.where(raw[19, x] > 0.5, 1.0, -1.0)
        put(ph.at[x + 2], ROW0, jnp.where(inside, p, 0.0))
        return carry

    lax.fori_loop(0, NXL, plane, 0)
    inner_step((0, NT - 1), s, rho, fl, ph, fp, red)
    low_a = lax.axis_index("gx") % 2 == 1
    far_corner(xc, low_a, (s, rho, fl, ph, fp, red))
    main_message((xa, xd), jnp.logical_not(low_a), (s, rho, fl, ph, fp, red))
    corner_message((xa, xd), NYL, jnp.logical_not(low_a), (s, rho, fl, ph, fp, red))


def edges():
    gy = lax.axis_index("gy")
    low_edge = gy == 0
    high_edge = gy == lax.axis_size("gy") - 1

    def mask(t):
        y = tile_rows(t)
        if t == 0:
            return (y >= 0) | jnp.logical_not(low_edge)
        if t == NT - 1:
            return (y < NYL) | jnp.logical_not(high_edge)
        return None

    return mask


def put_message(src, base, side, corner, hx, ph):
    near = jnp.where(side == 1, NXL + 2, 1)
    far = jnp.where(side == 1, NXL + 3, 0)
    for j in range(21):
        moved = 2 if corner and j in MOVED else 0
        if corner:
            spans = ((moved, 0, 4), (EXT - 4 - moved, 4, 4))
        else:
            spans = [(4 + 8 * n, 8 * n, 8) for n in range(NYL // 8)]
        for to, part, n in spans:
            v = plane_of(src, j)[pl.ds(base + part, n), :]
            if j in (15, 16):
                ph[near if j == 15 else far, pl.ds(ROW0 + to, n), :] = v
            else:
                hx[j, pl.ds(to, n), :] = v


def put_far(src, side, hx, ph):
    near = jnp.where(side == 1, NXL + 2, 1)
    far = jnp.where(side == 1, NXL + 3, 0)
    for j, row, r in far_spans():
        v = src[pl.ds(row, 8), :]
        if j in (15, 16):
            ph[near if j == 15 else far, pl.ds(ROW0 + 4 + r, 8), :] = v
        else:
            hx[j, pl.ds(4 + r, 8), :] = v


def by_side(side, step):
    for k in (0, 1):
        pl.when(side == k)(lambda: step(k))


def side_dirs(side):
    if side == 0:
        return 0, DIRS[5:10], DIRS[0:5]
    return NXL + 1, DIRS[0:5], DIRS[5:10]


def halo_first(side, hx, ph, fp, red, tiles=range(NT)):
    index, towards, _ = side_dirs(side)
    for t in tiles:
        rows = pl.ds(8 * t, 8)
        finish(
            DIRS, lambda d: hx[towards.index(d), rows, :] if d in towards else None, ph,
            hx[14, rows, :], hx[17, rows, :], index, ROW0 + 8 * t, fp, red,
        )


def halo_collide(side, hx, fp, red, ph, s2, rho2, tiles=range(NT)):
    mask = edges()
    index, towards, back = side_dirs(side)
    near, far = (NXL + 2, NXL + 3) if side == 1 else (1, 0)
    outwards = 1.0 if side == 0 else -1.0
    for t in tiles:
        row = ROW0 + 8 * t
        rows = pl.ds(8 * t, 8)
        f = {d: None if d in towards else arrived(d, fp, index, row) for d in DIRS}
        known = (
            hx[10, rows, :], outwards * hx[11, rows, :], hx[12, rows, :], hx[13, rows, :],
        )
        relaxed, total, _ = collide(f, known)
        rsum = hx[18, rows, :]
        rfar = hx[20, rows, :]
        for g in GROUPS:
            shifted = pl.ds(row - g[1], 8)
            if g[0] != towards[0][0]:
                rsum = rsum + red[GPOS[g], index - g[0], shifted, :]
            if g[0] == back[0][0]:
                rfar = rfar + red[GPOS[g], index, shifted, :]
        ffar = hx[19, rows, :]
        for d in back:
            ffar = ffar + fp[POS[d], index, pl.ds(row - d[1], 8), :]
        p = 2.0 * rsum / total - 1.0
        pfar = 2.0 * rfar / ffar - 1.0
        inside = mask(t)
        if inside is not None:
            p = jnp.where(inside, p, 0.0)
            pfar = jnp.where(inside, pfar, 0.0)
        is_fluid = hx[17, rows, :] > 0.5
        for j, d in enumerate(towards):
            v = jnp.where(is_fluid, relaxed[d] + hx[5 + j, rows, :], f[neg(d)])
            if inside is not None:
                v = jnp.where(inside, v, 0.0)
            s2[POS[d], index, rows, :] = v
        rho2[index, rows, :] = total
        ph[near, pl.ds(row, 8), :] = p
        ph[far, pl.ds(row, 8), :] = pfar


def halo_second(side, hx, s2, rho2, ph, fp, red, tiles=range(NT)):
    index, towards, _ = side_dirs(side)
    for t in tiles:
        rows = pl.ds(8 * t, 8)
        finish(
            towards, lambda d: s2[POS[d], index, rows, :], ph, rho2[index, rows, :],
            hx[17, rows, :], index, ROW0 + 8 * t, fp, red,
        )


def own_finish(x, s, k, rho, fl, ph, fp, red, tiles=range(NT)):
    for t in tiles:
        rows = pl.ds(8 * t, 8)
        finish(
            DIRS, lambda d: s[POS[d], k, rows, :], ph, rho[k, rows, :], fl[x, rows, :],
            x + 1, ROW0 + 8 * t, fp, red,
        )


def own_collide(x, k, fl, fp, red, ph, s2, rho2, tiles=range(NT)):
    mask = edges()
    for t in tiles:
        row = ROW0 + 8 * t
        rows = pl.ds(8 * t, 8)
        f = {d: arrived(d, fp, x + 1, row) for d in DIRS}
        relaxed, total, _ = collide(f)
        p = 2.0 * red_arrived(red, x + 1, row) / total - 1.0
        inside = mask(t)
        if inside is not None:
            p = jnp.where(inside, p, 0.0)
        is_fluid = fl[x, rows, :] > 0.5
        for d in DIRS:
            v = jnp.where(is_fluid, relaxed[d], f[neg(d)])
            if inside is not None:
                v = jnp.where(inside, v, 0.0)
            s2[POS[d], k, rows, :] = v
        rho2[k, rows, :] = total
        ph[x + 2, pl.ds(row, 8), :] = p


def two_planes(side, step):
    def body(k, carry):
        step(jnp.where(side == 1, NXL - 1 - k, k), k)
        return carry

    lax.fori_loop(0, 2, body, 0)


def near_kernel(s, rho, fl, ph_in, fp_in, red_in, xa, xd,
                fp, red, fp2, red2, ph2, s2_next, rho2_next, ph, hx, s2, rho2, own2, orho2):
    side = 1 - lax.axis_index("gx") % 2
    ph[...] = ph_in[...]
    put_message((xa, xd), 0, side, False, hx, ph)
    put_message((xa, xd), NYL, side, True, hx, ph)
    first = jnp.where(side == 1, NXL - 1, 0)
    own_finish(first, s, first, rho, fl, ph, fp, red)
    by_side(side, lambda k: halo_first(k, hx, ph, fp, red))
    two_planes(side, lambda x, k: own_collide(x, k, fl, fp, red, ph2, own2, orho2))
    by_side(side, lambda k: halo_collide(k, hx, fp, red, ph2, s2, rho2))
    own_finish(first, own2, 0, orho2, fl, ph2, fp2, red2)
    by_side(side, lambda k: halo_second(k, hx, s2, rho2, ph2, fp2, red2))
    s2_next[:, 0] = own2[:, 1]
    rho2_next[0] = orho2[1]


def far_half(tiles, s, rho, fl, ph, fp, red, fp2, red2, ph2, s2_next, rho2_next, hx, s2,
             rho2, own2, orho2):
    side = lax.axis_index("gx") % 2
    first = jnp.where(side == 1, NXL - 1, 0)
    third = jnp.where(side == 1, NXL - 3, 2)
    own_finish(first, s, first, rho, fl, ph, fp, red, tiles)
    by_side(side, lambda k: halo_first(k, hx, ph, fp, red, tiles))
    two_planes(side, lambda x, k: own_collide(x, k, fl, fp, red, ph2, own2, orho2, tiles))
    by_side(side, lambda k: halo_collide(k, hx, fp, red, ph2, s2, rho2, tiles))
    own_finish(third, s2_next, 0, rho2_next, fl, ph2, fp2, red2, tiles)
    two_planes(
        side, lambda x, k: own_finish(x, own2, k, orho2, fl, ph2, fp2, red2, tiles)
    )
    by_side(side, lambda k: halo_second(k, hx, s2, rho2, ph2, fp2, red2, tiles))


def move_last(x, starts, fp2, red2, pops_out, phase_out):
    for n, r in enumerate(starts):
        row = ROW0 + 4 + r
        rows = pl.ds(8 * n, 8)
        total = None
        for d in DIRS:
            v = arrived(d, fp2, x + 1, row)
            pops_out[REF_OF[POS[d]], x, rows, :] = v
            total = v if total is None else total + v
        phase_out[x, rows, :] = 2.0 * red_arrived(red2, x + 1, row) / total - 1.0


def far_kernel(s, rho, fl, ph_in, fp_in, red_in, fp2_in, red2_in, ph2_in, s2_next, rho2_next,
               xb, pops_mid, phase_mid, fp, red, fp2, red2, ph, ph2, hx,
               s2, rho2, own2, orho2):
    ph[...] = ph_in[...]
    ph2[...] = ph2_in[...]
    put_far(xb, lax.axis_index("gx") % 2, hx, ph)
    far_half(
        range(NT), s, rho, fl, ph, fp, red, fp2, red2, ph2, s2_next, rho2_next, hx, s2,
        rho2, own2, orho2,
    )
    for x in range(NXL):
        move_last(x, (8, 16), fp2, red2, pops_mid, phase_mid)


def end_kernel(s, rho, fl, s2_next, rho2_next, xc, pops_mid, phase_mid, fp_in, red_in, fp2_in,
               red2_in, ph_in, ph2_in, hx_in, pops_hbm, phase_hbm, fp, red, fp2, red2, ph, ph2,
               hx, s2, rho2, own2, orho2, pops_out, phase_out, sems):
    middle = pl.ds(8, 16)

    def middle_copies(x):
        return (
            pltpu.make_async_copy(
                pops_mid.at[:, x], pops_hbm.at[:, x, middle], sems.at[6 * x]
            ),
            pltpu.make_async_copy(
                phase_mid.at[x], phase_hbm.at[x, middle], sems.at[6 * x + 1]
            ),
        )

    def edge_copies(x):
        out = []
        for n, r in enumerate((0, NYL - 8)):
            part, rows = pl.ds(8 * n, 8), pl.ds(r, 8)
            out += [
                pltpu.make_async_copy(
                    pops_out.at[:, x, part], pops_hbm.at[:, x, rows], sems.at[6 * x + 2 + n]
                ),
                pltpu.make_async_copy(
                    phase_out.at[x, part], phase_hbm.at[x, rows], sems.at[6 * x + 4 + n]
                ),
            ]
        return out

    for x in range(NXL):
        for copy in middle_copies(x):
            copy.start()
    put_corner(xc, lax.axis_index("gx") % 2, hx, ph)
    far_half(
        (0, NT - 1), s, rho, fl, ph, fp, red, fp2, red2, ph2, s2_next, rho2_next, hx, s2,
        rho2, own2, orho2,
    )
    for x in range(NXL):
        move_last(x, (0, NYL - 8), fp2, red2, pops_out, phase_out)
        for copy in edge_copies(x):
            copy.start()
    for x in range(NXL):
        for copy in (*middle_copies(x), *edge_copies(x)):
            copy.wait()


F32 = jnp.float32
VM = pl.BlockSpec(memory_space=pltpu.VMEM)
HB = pl.BlockSpec(memory_space=pltpu.HBM)
MIB = 1024 * 1024


def shaped(*dims):
    return jax.ShapeDtypeStruct(dims, F32)


def call(kernel, in_specs, outs, scratch, name, aliases=None, vmem=40, cost=0,
         out_specs=None):
    return pl.pallas_call(
        kernel,
        in_specs=in_specs,
        out_specs=out_specs or [VM] * len(outs),
        out_shape=outs,
        scratch_shapes=scratch,
        input_output_aliases=aliases or {},
        compiler_params=pltpu.CompilerParams(vmem_limit_bytes=vmem * MIB),
        cost_estimate=pl.CostEstimate(flops=cost, bytes_accessed=cost, transcendentals=0),
        name=name,
    )


def pairs(count, first):
    out = []
    for i in range(first, count + first, 2):
        a, b = i % count, (i + 1) % count
        out += [(a, b), (b, a)]
    return out


def swap(value, axis, first):
    return lax.ppermute(value, axis, pairs(lax.axis_size(axis), first))


def on_device(populations, labels, solid_mask):
    state = [
        shaped(19, NXL, EXT, 128), shaped(NXL, EXT, 128), shaped(NXL, EXT, 128),
        shaped(NXL + 4, SROWS, 128), shaped(19, NXL + 2, SROWS, 128),
        shaped(9, NXL + 2, SROWS, 128),
    ]
    inputs = [
        pltpu.with_memory_space_constraint(v, pltpu.HBM)
        for v in (populations, labels, solid_mask)
    ]

    split = [shaped(HALF, EXT, 128), shaped(21 - HALF, EXT, 128)]
    whole = [
        shaped(19, NXL, NYL, 128), jax.ShapeDtypeStruct((NXL, NYL, 128), jnp.int32),
        jax.ShapeDtypeStruct((NXL, NYL, 128), jnp.int32),
    ]
    ya, yb, *held = call(
        pack_kernel, [HB] * 3, [shaped(YROWS, 128)] * 2 + whole,
        [pltpu.SemaphoreType.DMA((6,))], "pack",
    )(*inputs)
    ya = swap(ya, "gy", 0)
    yb = swap(yb, "gy", 1)
    *mid, xb = call(
        start_kernel, [VM] * 3, state + [shaped(FAR_ROWS, 128)], [], "start",
    )(*held)
    xb = swap(xb, "gx", 1)
    *mid, xa, xd, xc = call(
        edge_kernel, [VM] * 8, state + split + [shaped(CORNER_ROWS, 128)],
        [pltpu.VMEM((21, NXL, 8, 128), F32)], "edge", {2 + i: i for i in range(6)},
        cost=10 ** 10,
    )(yb, ya, *mid)
    xc = swap(xc, "gx", 1)
    xa = swap(xa, "gx", 0)
    xd = swap(xd, "gx", 0)
    s, rho, fl, ph, fp, red = mid
    halo = [
        pltpu.VMEM((21, EXT, 128), F32), pltpu.VMEM((19, NXL + 2, EXT, 128), F32),
        pltpu.VMEM((NXL + 2, EXT, 128), F32), pltpu.VMEM((19, 2, EXT, 128), F32),
        pltpu.VMEM((2, EXT, 128), F32),
    ]
    phases = pltpu.VMEM((NXL + 4, SROWS, 128), F32)
    fp, red, fp2, red2, ph2, s2_next, rho2_next = call(
        near_kernel, [VM] * 8,
        [state[4], state[5], state[4], state[5], state[3], shaped(19, 1, EXT, 128),
         shaped(1, EXT, 128)],
        [phases] + halo, "near", {4: 0, 5: 1}, cost=0,
    )(s, rho, fl, ph, fp, red, xa, xd)
    held = [state[4], state[5], state[4], state[5], state[3], state[3], shaped(21, EXT, 128)]
    *mids, fp, red, fp2, red2, ph, ph2, hx = call(
        far_kernel, [VM] * 12, [shaped(19, NXL, 16, 128), shaped(NXL, 16, 128)] + held,
        halo[1:], "far", {4: 2, 5: 3, 6: 4, 7: 5},
    )(s, rho, fl, ph, fp, red, fp2, red2, ph2, s2_next, rho2_next, xb)
    out = call(
        end_kernel, [VM] * 15,
        [shaped(19, NXL, NYL, 128), shaped(NXL, NYL, 128)] + held,
        halo[1:] + [
            pltpu.VMEM((19, NXL, 16, 128), F32), pltpu.VMEM((NXL, 16, 128), F32),
            pltpu.SemaphoreType.DMA((6 * NXL,)),
        ],
        "end", {8 + i: 2 + i for i in range(7)}, out_specs=[HB] * 2 + [VM] * 7,
    )(s, rho, fl, s2_next, rho2_next, xc, *mids, fp, red, fp2, red2, ph, ph2, hx)
    return out[0], out[1]


def solution(mesh):
    in_specs = (P(None, "gx", "gy", None), P("gx", "gy", None), P("gx", "gy", None))
    out_specs = (P(None, "gx", "gy", None), P("gx", "gy", None))

    def run(populations, labels, solid_mask):
        new, phase = on_device(populations, labels, solid_mask)
        return new, phase

    return jax.shard_map(
        run, mesh=mesh, in_specs=in_specs, out_specs=out_specs, check_vma=False
    )
```
